128 devices in a mesh: orient: 8 (over z, y_lo), frame: 16 (over x, y_hi, core).
Axes of the slice: x: 4, y: 4 (y_hi: 2, y_lo: 2; y = y_hi * 2 + y_lo), z: 4, core: 2. Of those that a mesh axis runs over, the one named last changes fastest.
Arguments:
- slices: float32 [512, 2048], P('orient', 'frame'), may hold values from 0.2 to 5
- counts: float32 [8192, 2048], P('frame'), may hold values from 0 to 600, as said below
- fluence: float32 [8192], P('frame'), may hold values from 0.5 to 2
- tile_brick: int32 [16, 512, 1], P('frame', 'orient'), may hold values from 0 to 127; in each aligned block of 64 rows (0 to 63, 64 to 127, ..., all dimensions but the last counted through in order) at most 4 rows name the same one
- tile_base: int32 [16, 512], P('frame', 'orient'), may hold values from 0 to 896
Outputs:
- new_slices: float32 [512, 2048], P('orient', 'frame')
- intensity: float32 [128, 1024], P(('orient', 'frame'))
The draws below stay inside these ranges and needn't reach their ends.
Inputs may be any that keep to these rules, and one draw needn't show every extreme that they name: `tile_brick`: in each aligned block of 64 rows (one tile of each of one index of orient's orientations) no brick is named more than 4 times. `counts`: whole numbers.
All inputs are finite; a program needn't handle non-finite values.
Results may differ from the reference program's by a relative error of at most 0.0003.
Values sent between devices are 32-bit elements; how exact they have to be, the bound alone decides.
A program may use at most 64 MiB of HBM per device.

```python
import math
import jax
import jax.numpy as jnp
import numpy as np
from jax import lax

P_SIZE = 2048
TILE = 128
R_DEV = 64
FRAMES_DEV = 512
VOX_DEV = 1024
ITERS = 2
ORIENTS = 512
FRAMES = 8192
BRICKS = 128
CAP = 4


def draw_counts(key, part):
    first, second, third = jax.random.split(jax.random.fold_in(key, 17), 3)
    rate = jnp.exp(jax.random.uniform(first, (1, P_SIZE), jnp.float32, jnp.log(0.3), jnp.log(3.0)))
    scale = jax.random.uniform(second, (FRAMES, 1), jnp.float32, 0.5, 2.0)
    unit = jax.random.uniform(third, (FRAMES, P_SIZE), jnp.float32, 1e-07, 1.0)
    return jnp.floor(-jnp.log(unit) * rate * scale).astype(jnp.float32)


def place_ends(drawn, stream_key, least, high):
    longest = drawn.shape.index(max(drawn.shape))
    spots = []
    for shift in (0, 1):
        where = [jax.random.randint(jax.random.fold_in(stream_key, axis), (), 0, length) for axis, length in enumerate(drawn.shape)]
        where[longest] = (where[longest] + shift) % drawn.shape[longest]
        spots.append(tuple(where))
    return drawn.at[spots[0]].set(least).at[spots[1]].set(high)


def shard_levels(own_key, dims, shards, least, largest):
    gain = 1.0
    for axis_at, parts in shards:
        heights = jax.random.uniform(jax.random.fold_in(jax.random.fold_in(own_key, 6), axis_at), (parts,), jnp.float32, least / len(shards), largest / len(shards))
        gain = gain * jnp.repeat(jnp.exp(heights), dims[axis_at] // parts).reshape((-1,) + (1,) * (len(dims) - 1 - axis_at))
    return gain


def deal_out(stream_key, own, number, rows, number_of, top, reach, lean):
    order = jax.random.permutation(stream_key, number_of)
    packed, ordinary = portions_of(number_of, rows * top, reach, lean, True), portions_of(number_of, rows * top, reach, lean, False)
    places = jnp.arange(number_of)

    def named(tallies, offset_by):
        used = int((tallies > 0).sum())
        fixed = max(1, used // 4)
        moved = fixed + (places - fixed + offset_by * (used - fixed)) % max(1, number_of - fixed)
        return jnp.zeros((number_of,), jnp.int32).at[order[jnp.where(places < fixed, places, moved)]].set(jnp.asarray(tallies, jnp.int32))

    tallies = jnp.where(number % 4 == 0, named(packed, number // 4), named(ordinary, number - number // 4 - 1))
    mixed = jax.random.permutation(jax.random.fold_in(own, 3), number_of)
    giver, sink = mixed[0:number_of // 2 * 2:2], mixed[1:number_of // 2 * 2:2]
    margin = jnp.minimum(tallies[giver] - 1, reach - tallies[sink]) // 2
    margin = jnp.where((giver == order[0]) | (sink == order[0]) | (tallies[sink] == 0), 0, jnp.maximum(margin, 0))
    moved = jax.random.randint(jax.random.fold_in(own, 4), (number_of // 2,), 0, 1 << 20) % (margin + 1)
    tallies = tallies.at[giver].add(-moved).at[sink].add(moved)
    labels = jnp.searchsorted(jnp.cumsum(tallies), jnp.arange(rows * top), side="right").astype(jnp.int32)
    table = labels.reshape(top, rows).T
    table = table[jax.random.permutation(jax.random.fold_in(own, 1), rows)]
    offset_by = jax.random.randint(jax.random.fold_in(own, 2), (rows, 1), 0, top)
    return jnp.take_along_axis(table, (jnp.arange(top)[None, :] + offset_by) % top, axis=1)


def portions_of(number_of, total, bound, lean, full):
    loads = [(1 << 20) // math.isqrt(grade ** lean) + 1 for grade in range(1, number_of + 1)]
    largest = bound if full else min(bound, max(-(-total // number_of), total * loads[0] // sum(loads)))
    least = 1 if total - largest >= number_of - 1 else 0
    given, rest = [largest] + [least] * (number_of - 1), total - largest - least * (number_of - 1)
    while rest > 0:
        candidates = [i for i in range(1, number_of) if given[i] < largest] or [i for i in range(1, number_of) if given[i] < bound]
        mass, left = sum([loads[i] for i in candidates]), rest
        for i in candidates:
            addition = min(bound - given[i], max(1, left * loads[i] // mass), rest)
            given[i] = given[i] + addition
            rest = rest - addition
    return np.array(given)


def setup_inputs(seed: int = 0) -> dict:
    key_list = jax.random.split(jax.random.key(seed), 6)
    slices = jnp.clip(jnp.exp(math.log(5.0) - 3.218876 * jax.random.uniform(key_list[0], (ORIENTS, P_SIZE), jnp.float32) ** shard_levels(key_list[0], (ORIENTS, P_SIZE), ((0, 8), (1, 16)), -0.2, 0.2)), 0.2, 5.0)
    counts = draw_counts(jax.random.fold_in(key_list[5], 71), 0)
    fluence = jnp.clip(jnp.exp(math.log(2.0) - 1.3862944 * jax.random.uniform(key_list[2], (FRAMES,), jnp.float32) ** shard_levels(key_list[2], (FRAMES,), ((0, 16),), -0.2, 0.2)), 0.5, 2.0)
    tile_brick_keys = jax.random.split(jax.random.fold_in(key_list[3], 1), (P_SIZE // TILE) * ORIENTS // R_DEV)
    tile_brick_turns = jax.random.permutation(jax.random.fold_in(key_list[3], 3), (P_SIZE // TILE) * ORIENTS // R_DEV)
    tile_brick = jax.vmap(lambda own, number: deal_out(jax.random.fold_in(key_list[3], 2), own, number, R_DEV, BRICKS, 1, CAP, 2))(tile_brick_keys, tile_brick_turns).reshape((P_SIZE // TILE, ORIENTS, 1))
    tile_base = place_ends(jax.random.randint(key_list[4], (P_SIZE // TILE, ORIENTS), 0, VOX_DEV - TILE + 1), jax.random.fold_in(key_list[4], 1), 0, VOX_DEV - TILE).astype(jnp.int32)
    return {"slices": slices, "counts": counts, "fluence": fluence, "tile_brick": tile_brick, "tile_base": tile_base}


BACKGROUND = 0.1
SHARPNESS = 0.02


def voxel_index(tile_brick, tile_base):
    offsets = jnp.arange(TILE, dtype=jnp.int32)
    start = (tile_brick[:, :, 0] * VOX_DEV + tile_base).astype(jnp.int32)
    return (start[:, :, None] + offsets[None, None, :]).reshape(-1)


def compress_expand(updated, flat):
    columns = P_SIZE // TILE
    tiles = updated.reshape(ORIENTS, columns, TILE).transpose(1, 0, 2).reshape(-1)
    sums = jnp.zeros((BRICKS * VOX_DEV,), updated.dtype).at[flat].add(tiles)
    hits = jnp.zeros((BRICKS * VOX_DEV,), updated.dtype).at[flat].add(jnp.ones_like(tiles))
    volume = sums / jnp.maximum(hits, 1.0)
    expanded = volume[flat].reshape(columns, ORIENTS, TILE).transpose(1, 0, 2).reshape(ORIENTS, P_SIZE)
    return expanded, volume.reshape(BRICKS, VOX_DEV)


def iterate(current, counts, fluence):
    logs = jnp.log(current + BACKGROUND)
    total = jnp.sum(current, axis=1)
    blocks = counts.reshape(FRAMES // FRAMES_DEV, FRAMES_DEV, P_SIZE)
    weights = fluence.reshape(FRAMES // FRAMES_DEV, FRAMES_DEV)

    def step(carry, item):
        numer, denom = carry
        block, flu = item
        like = lax.dot_general(logs, block, (((1,), (1,)), ((), ())), precision=lax.Precision.HIGHEST, preferred_element_type=current.dtype)
        score = SHARPNESS * (like - total[:, None] * flu[None, :])
        peak = jnp.max(score, axis=0)
        expo = jnp.exp(score - peak[None, :])
        prob = expo / jnp.sum(expo, axis=0)[None, :]
        numer = numer + jnp.dot(prob, block, precision=lax.Precision.HIGHEST)
        denom = denom + jnp.dot(prob, flu, precision=lax.Precision.HIGHEST)
        return (numer, denom), None

    init = (jnp.zeros((ORIENTS, P_SIZE), current.dtype), jnp.zeros((ORIENTS,), current.dtype))
    (numer, denom), _ = lax.scan(step, init, (blocks, weights))
    return (numer + current) / (denom + 1.0)[:, None]


def reference(slices, counts, fluence, tile_brick, tile_base):
    flat = voxel_index(tile_brick, tile_base)
    current = slices
    volume = None
    for turn in range(ITERS):
        updated = iterate(current, counts, fluence)
        current, volume = compress_expand(updated, flat)
    return current, volume
```

```python
import functools

import jax
import jax.numpy as jnp
from jax import lax
from jax.experimental import pallas as pl
from jax.experimental.pallas import tpu as pltpu
from jax.sharding import PartitionSpec as P

VOX = 1024
TILE = 128
SUB = VOX // TILE
ITERS = 2
BACKGROUND = 0.1
SHARPNESS = 0.02
MESH = pl.DeviceIdType.MESH
F32 = jnp.float32
BF16 = jnp.bfloat16
LOAD = 4


def split2(x):
    high = x.astype(BF16)
    return high, (x - high.astype(F32)).astype(BF16)


def split3(x):
    high = x.astype(BF16)
    rest = x - high.astype(F32)
    mid = rest.astype(BF16)
    return high, mid, (rest - mid.astype(F32)).astype(BF16)


def iota(shape, axis):
    return lax.broadcasted_iota(jnp.int32, shape, axis)


def kernel(
    n_o,
    n_f,
    slices_ref,
    codes_ref,
    fluence_ref,
    counts_ref,
    new_ref,
    out_ref,
    raw,
    count_high,
    count_low,
    held,
    codes,
    stats,
    dens,
    gather_to,
    gather_from,
    shifts,
    tiles,
    marks,
    logs,
    part_out,
    part_in,
    brick_out,
    brick_in,
    volume,
    spread,
    hits_out,
    hits_in,
    load_sem,
    frame_send,
    frame_recv,
    orient_send,
    orient_recv,
):
    o = lax.axis_index("orient")
    f = lax.axis_index("frame")
    rows = slices_ref.shape[0]
    frames = counts_ref.shape[0]
    pair = 2 * rows
    block = n_f * SUB
    chunks = frames // TILE

    barrier = pltpu.get_barrier_semaphore()

    def greet_frame(j, c):
        pl.semaphore_signal(
            barrier, inc=1, device_id=(o, lax.rem(f + j, n_f)), device_id_type=MESH
        )
        return c

    def greet_orient(j, c):
        pl.semaphore_signal(
            barrier, inc=1, device_id=(lax.rem(o + j, n_o), f), device_id_type=MESH
        )
        return c

    lax.fori_loop(1, n_f, greet_frame, 0)
    lax.fori_loop(1, n_o, greet_orient, 0)
    step = frames // LOAD
    for i in range(LOAD):
        pltpu.make_async_copy(
            counts_ref.at[pl.ds(i * step, step)], raw.at[pl.ds(i * step, step)], load_sem.at[i]
        ).start()
    pl.semaphore_wait(barrier, n_f + n_o - 2)

    def to_frame(which, src, dst, peer):
        return pltpu.make_async_remote_copy(
            src_ref=src,
            dst_ref=dst,
            send_sem=frame_send.at[which, peer],
            recv_sem=frame_recv.at[which, f],
            device_id=(o, peer),
            device_id_type=MESH,
        )

    def to_orient(which, src, dst, peer):
        return pltpu.make_async_remote_copy(
            src_ref=src,
            dst_ref=dst,
            send_sem=orient_send.at[which, peer],
            recv_sem=orient_recv.at[which, o],
            device_id=(peer, f),
            device_id_type=MESH,
        )

    def send_frame(which, src, dst):
        def body(j, c):
            peer = lax.rem(f + j, n_f)
            to_frame(which, src(peer), dst, peer).start()
            return c

        lax.fori_loop(1, n_f, body, 0)

    def send_orient(which, src, dst):
        def body(j, c):
            peer = lax.rem(o + j, n_o)
            to_orient(which, src(peer), dst, peer).start()
            return c

        lax.fori_loop(1, n_o, body, 0)

    def from_frame(which, dst, peer):
        pltpu.make_async_remote_copy(
            src_ref=dst,
            dst_ref=dst,
            send_sem=frame_send.at[which, peer],
            recv_sem=frame_recv.at[which, peer],
            device_id=(o, peer),
            device_id_type=MESH,
        ).wait_recv()

    def from_orient(which, dst, peer):
        pltpu.make_async_remote_copy(
            src_ref=dst,
            dst_ref=dst,
            send_sem=orient_send.at[which, peer],
            recv_sem=orient_recv.at[which, peer],
            device_id=(peer, f),
            device_id_type=MESH,
        ).wait_recv()

    def wait_frame(which, dst):
        def body(j, c):
            peer = lax.rem(f + n_f - j, n_f)
            from_frame(which, dst(peer), peer)
            return c

        lax.fori_loop(1, n_f, body, 0)

    def wait_orient(which, dst):
        def body(j, c):
            peer = lax.rem(o + n_o - j, n_o)
            from_orient(which, dst(peer), peer)
            return c

        lax.fori_loop(1, n_o, body, 0)

    def sent_frame(which, src):
        def body(j, c):
            peer = lax.rem(f + j, n_f)
            to_frame(which, src(peer), src(peer), peer).wait_send()
            return c

        lax.fori_loop(1, n_f, body, 0)

    def sent_orient(which, src):
        def body(j, c):
            peer = lax.rem(o + j, n_o)
            to_orient(which, src(peer), src(peer), peer).wait_send()
            return c

        lax.fori_loop(1, n_o, body, 0)

    send_frame(0, lambda peer: codes_ref, codes.at[f])
    send_frame(1, lambda peer: slices_ref, held.at[0, f])
    codes[f] = codes_ref[...]
    held[0, f] = slices_ref[...]

    for i in range(LOAD):
        pltpu.make_async_copy(
            counts_ref.at[pl.ds(i * step, step)], raw.at[pl.ds(i * step, step)], load_sem.at[i]
        ).wait()

        def convert(j, c):
            at = pl.ds(pl.multiple_of(i * step + j * 16, 16), 16)
            high, low = split2(raw[at, :])
            count_high[at, :] = high
            count_low[at, :] = low
            return c

        lax.fori_loop(0, step // 16, convert, 0)

    wait_frame(0, lambda peer: codes.at[peer])
    lane = iota((rows, TILE), 1)
    eye = iota((pair, pair), 0) == iota((pair, pair), 1)
    places = n_o * block

    def prepare(t, c):
        row = codes[t, 0:1, :]
        at = pl.ds(pl.multiple_of(t * pair, pair), pair)

        def fill(i, c):
            here = pl.ds(pl.multiple_of(i * block, block), block)
            place = (iota((block, pair), 0) + i * block).astype(F32)
            gather_to[here, at] = jnp.where(place == row, 1.0, 0.0).astype(BF16)
            return c

        lax.fori_loop(0, n_o, fill, 0)
        column = jnp.sum(jnp.where(eye, row, 0.0), axis=1, keepdims=True)
        place = iota((pair, places), 1).astype(F32)
        gather_from[at, :] = jnp.where(place == column, 1.0, 0.0).astype(BF16)
        shift = jnp.sum(jnp.where(eye, codes[t, 1:2, :], 0.0), axis=1, keepdims=True)
        shift = jnp.broadcast_to(shift[0:rows], (rows, TILE)).astype(jnp.int32)
        shifts[t] = shift
        mark = jnp.where(lane >= shift, 1.0, 0.0)
        marks[at, :] = jnp.concatenate([mark, 1.0 - mark], axis=0).astype(BF16)
        return c

    lax.fori_loop(0, n_f, prepare, 0)

    def count_hits(i, c):
        here = pl.ds(pl.multiple_of((i * n_f + f) * SUB, SUB), SUB)
        place = (iota((SUB, pair), 0) + (i * n_f + f) * SUB).astype(F32)

        def add(t, total):
            at = pl.ds(pl.multiple_of(t * pair, pair), pair)
            chosen = jnp.where(place == codes[t, 0:1, :], 1.0, 0.0).astype(BF16)
            return total + jnp.dot(chosen, marks[at, :], preferred_element_type=F32)

        hits_out[i] = lax.fori_loop(0, n_f, add, jnp.zeros((SUB, TILE), F32))
        return c

    lax.fori_loop(0, n_o, count_hits, 0)
    send_orient(0, lambda peer: hits_out.at[peer], hits_in.at[o])
    hits_in[o] = hits_out[o]

    wait_frame(1, lambda peer: held.at[0, peer])

    def expand(t):
        at = pl.ds(pl.multiple_of(t * pair, pair), pair)
        found = jnp.dot(gather_from[at, :], spread[...], preferred_element_type=F32)
        found = found[:, :TILE] + found[:, TILE:]
        shift = shifts[t]
        value = jnp.where(lane >= shift, found[:rows], found[rows:])
        for k in range(7):
            value = jnp.where(
                (shift & (1 << k)) != 0, pltpu.roll(value, TILE - (1 << k), 1), value
            )
        return value

    def iteration(turn, c):
        def take_logs(t, total):
            value = held[turn, t]
            at = pl.ds(pl.multiple_of(t * TILE, TILE), TILE)
            high, mid, low = split3(jnp.log(value + BACKGROUND))
            logs[0:rows, at] = high
            logs[rows : 2 * rows, at] = mid
            logs[2 * rows : 3 * rows, at] = low
            return total + value

        total = lax.fori_loop(0, n_f, take_logs, jnp.zeros((rows, TILE), F32))
        total = jnp.sum(total, axis=1, keepdims=True)
        across = (((1,), (1,)), ((), ()))
        like = lax.dot_general(
            logs[...], count_high[...], across, preferred_element_type=F32
        ) + lax.dot_general(logs[...], count_low[...], across, preferred_element_type=F32)
        like = like[:rows] + like[rows : 2 * rows] + like[2 * rows :]
        score = SHARPNESS * (like - total * fluence_ref[...])
        top = jnp.max(score, axis=0, keepdims=True)
        expo = jnp.exp(score - top)
        norm = jnp.sum(expo, axis=0, keepdims=True)
        own = stats.at[turn, o]
        for k in range(chunks):
            own[k : k + 1, :] = top[:, k * TILE : (k + 1) * TILE]
            own[chunks + k : chunks + k + 1, :] = norm[:, k * TILE : (k + 1) * TILE]
        send_orient(1 + turn, lambda peer: stats.at[turn, o], stats.at[turn, o])
        wait_orient(1 + turn, lambda peer: stats.at[turn, peer])
        peak = stats[turn, 0, 0:chunks, :]
        for i in range(1, n_o):
            peak = jnp.maximum(peak, stats[turn, i, 0:chunks, :])
        whole = jnp.zeros((chunks, TILE), F32)
        for i in range(n_o):
            whole = whole + stats[turn, i, chunks : 2 * chunks, :] * jnp.exp(
                stats[turn, i, 0:chunks, :] - peak
            )
        factor = jnp.exp(stats[turn, o, 0:chunks, :] - peak) / whole
        factor = jnp.concatenate([factor[k : k + 1, :] for k in range(chunks)], axis=1)
        prob = expo * factor
        den = jnp.sum(prob * fluence_ref[...], axis=1, keepdims=True)
        den = jnp.sum(
            jnp.where(iota((rows, TILE), 0) == lane, den, 0.0), axis=0, keepdims=True
        )
        dens[turn, f] = jnp.broadcast_to(den, (SUB, TILE))
        send_frame(2 + turn, lambda peer: dens.at[turn, f], dens.at[turn, f])
        probs = jnp.concatenate(split2(prob), axis=0)
        num = jnp.dot(probs, count_high[...], preferred_element_type=F32) + jnp.dot(
            probs, count_low[...], preferred_element_type=F32
        )
        num = num[:rows] + num[rows:]
        wait_frame(2 + turn, lambda peer: dens.at[turn, peer])
        weight = dens[turn, 0]
        for i in range(1, n_f):
            weight = weight + dens[turn, i]
        weight = jnp.sum(
            jnp.where(iota((rows, TILE), 0) == lane, weight[0:1, :], 0.0),
            axis=1,
            keepdims=True,
        )
        inverse = 1.0 / (weight + 1.0)

        for t in range(n_f):
            value = num[:, t * TILE : (t + 1) * TILE]
            value = (value + jnp.where(f == t, held[turn, t], 0.0)) * inverse
            shift = shifts[t]
            for k in range(7):
                value = jnp.where((shift & (1 << k)) != 0, pltpu.roll(value, 1 << k, 1), value)
            high, low = split2(value)
            first = lane >= shift
            none = jnp.zeros((rows, TILE), BF16)
            at = t * pair
            tiles[at : at + rows, :TILE] = jnp.where(first, high, none)
            tiles[at : at + rows, TILE:] = jnp.where(first, low, none)
            tiles[at + rows : at + pair, :TILE] = jnp.where(first, none, high)
            tiles[at + rows : at + pair, TILE:] = jnp.where(first, none, low)

        def collect(i):
            here = pl.ds(pl.multiple_of(i * block, block), block)
            part = jnp.dot(gather_to[here, :], tiles[...], preferred_element_type=F32)
            return part[:, :TILE] + part[:, TILE:]

        def scatter(j, c):
            peer = lax.rem(o + j, n_o)
            part_out[turn, peer] = collect(peer)
            to_orient(3 + turn, part_out.at[turn, peer], part_in.at[turn, o], peer).start()
            return c

        lax.fori_loop(1, n_o, scatter, 0)
        part_in[turn, o] = collect(o)
        wait_orient(3 + turn, lambda peer: part_in.at[turn, peer])
        part = part_in[turn, 0]
        for i in range(1, n_o):
            part = part + part_in[turn, i]
        for i in range(n_f):
            brick_out[turn, i] = part[i * SUB : (i + 1) * SUB]
        send_frame(4 + turn, lambda peer: brick_out.at[turn, peer], brick_in.at[turn, f])
        brick_in[turn, f] = brick_out[turn, f]

        @pl.when(turn == 0)
        def _():
            wait_orient(0, lambda peer: hits_in.at[peer])

        hits = hits_in[0]
        for i in range(1, n_o):
            hits = hits + hits_in[i]
        wait_frame(4 + turn, lambda peer: brick_in.at[turn, peer])
        brick = brick_in[turn, 0]
        for i in range(1, n_f):
            brick = brick + brick_in[turn, i]
        brick = brick / jnp.maximum(hits, 1.0)
        out_ref[...] = brick
        volume[turn, o, f] = brick
        send_frame(6 + turn, lambda peer: volume.at[turn, o, f], volume.at[turn, o, f])
        wait_frame(6 + turn, lambda peer: volume.at[turn, o, peer])
        send_orient(5 + turn, lambda peer: volume.at[turn, o], volume.at[turn, o])
        wait_orient(5 + turn, lambda peer: volume.at[turn, peer])
        for i in range(n_o):
            high, low = split2(volume[turn, i].reshape(block, TILE))
            spread[i * block : (i + 1) * block, :TILE] = high
            spread[i * block : (i + 1) * block, TILE:] = low

        @pl.when(turn < ITERS - 1)
        def _():
            def fill(t, c):
                held[turn + 1, t] = expand(t)
                return c

            lax.fori_loop(0, n_f, fill, 0)

        return c

    lax.fori_loop(0, ITERS, iteration, 0)
    new_ref[...] = expand(f)

    sent_frame(0, lambda peer: codes_ref)
    sent_frame(1, lambda peer: slices_ref)
    sent_orient(0, lambda peer: hits_out.at[peer])

    def finish(turn, c):
        sent_frame(2 + turn, lambda peer: dens.at[turn, f])
        sent_frame(4 + turn, lambda peer: brick_out.at[turn, peer])
        sent_frame(6 + turn, lambda peer: volume.at[turn, o, f])
        sent_orient(1 + turn, lambda peer: stats.at[turn, o])
        sent_orient(3 + turn, lambda peer: part_out.at[turn, peer])
        sent_orient(5 + turn, lambda peer: volume.at[turn, o])
        return c

    lax.fori_loop(0, ITERS, finish, 0)


def on_device(n_o, n_f, slices, counts, fluence, tile_brick, tile_base):
    rows = slices.shape[0]
    frames, pixels = counts.shape
    pair = 2 * rows
    block = n_f * SUB
    places = n_o * block
    code = tile_brick[:, :, 0] * VOX + tile_base
    place = code // TILE
    shift = code % TILE
    codes = jnp.concatenate(
        [
            jnp.concatenate([place, place + 1], axis=1),
            jnp.concatenate([shift, shift], axis=1),
            jnp.zeros((SUB - 2, pair), jnp.int32),
        ],
        axis=0,
    ).astype(F32)
    vmem = pl.BlockSpec(memory_space=pltpu.VMEM)
    new, brick = pl.pallas_call(
        functools.partial(kernel, n_o, n_f),
        out_shape=(
            jax.ShapeDtypeStruct((rows, TILE), F32),
            jax.ShapeDtypeStruct((SUB, TILE), F32),
        ),
        in_specs=[vmem, vmem, vmem, pl.BlockSpec(memory_space=pl.ANY)],
        out_specs=(vmem, vmem),
        scratch_shapes=[
            pltpu.VMEM((frames, pixels), F32),
            pltpu.VMEM((frames, pixels), BF16),
            pltpu.VMEM((frames, pixels), BF16),
            pltpu.VMEM((ITERS, n_f, rows, TILE), F32),
            pltpu.VMEM((n_f, SUB, pair), F32),
            pltpu.VMEM((ITERS, n_o, 2 * (frames // TILE), TILE), F32),
            pltpu.VMEM((ITERS, n_f, SUB, TILE), F32),
            pltpu.VMEM((places, n_f * pair), BF16),
            pltpu.VMEM((n_f * pair, places), BF16),
            pltpu.VMEM((n_f, rows, TILE), jnp.int32),
            pltpu.VMEM((n_f * pair, 2 * TILE), BF16),
            pltpu.VMEM((n_f * pair, TILE), BF16),
            pltpu.VMEM((3 * rows, pixels), BF16),
            pltpu.VMEM((ITERS, n_o, block, TILE), F32),
            pltpu.VMEM((ITERS, n_o, block, TILE), F32),
            pltpu.VMEM((ITERS, n_f, SUB, TILE), F32),
            pltpu.VMEM((ITERS, n_f, SUB, TILE), F32),
            pltpu.VMEM((ITERS, n_o, n_f, SUB, TILE), F32),
            pltpu.VMEM((places, 2 * TILE), BF16),
            pltpu.VMEM((n_o, SUB, TILE), F32),
            pltpu.VMEM((n_o, SUB, TILE), F32),
            pltpu.SemaphoreType.DMA((LOAD,)),
            pltpu.SemaphoreType.DMA((2 + 3 * ITERS, n_f)),
            pltpu.SemaphoreType.DMA((2 + 3 * ITERS, n_f)),
            pltpu.SemaphoreType.DMA((1 + 3 * ITERS, n_o)),
            pltpu.SemaphoreType.DMA((1 + 3 * ITERS, n_o)),
        ],
        compiler_params=pltpu.CompilerParams(
            collective_id=0, has_side_effects=True, vmem_limit_bytes=60 << 20
        ),
    )(slices, codes, fluence[None, :], counts)
    return new, brick.reshape(1, SUB * TILE)


def solution(mesh):
    n_o, n_f = mesh.shape["orient"], mesh.shape["frame"]
    in_specs = (
        P("orient", "frame"),
        P("frame", None),
        P("frame"),
        P("frame", "orient", None),
        P("frame", "orient"),
    )
    out_specs = (P("orient", "frame"), P(("orient", "frame"), None))
    return jax.shard_map(
        functools.partial(on_device, n_o, n_f),
        mesh=mesh,
        in_specs=in_specs,
        out_specs=out_specs,
        check_vma=False,
    )
```

```python
import functools

import jax
import jax.numpy as jnp
from jax import lax
from jax.experimental import pallas as pl
from jax.experimental.pallas import tpu as pltpu
from jax.sharding import PartitionSpec as P

VOX = 1024
TILE = 128
SUB = VOX // TILE
ITERS = 2
BACKGROUND = 0.1
SHARPNESS = 0.02
MESH = pl.DeviceIdType.MESH
F32 = jnp.float32
BF16 = jnp.bfloat16
LOAD = 4


def split2(x):
    high = x.astype(BF16)
    return high, (x - high.astype(F32)).astype(BF16)


def split3(x):
    high = x.astype(BF16)
    rest = x - high.astype(F32)
    mid = rest.astype(BF16)
    return high, mid, (rest - mid.astype(F32)).astype(BF16)


def iota(shape, axis):
    return lax.broadcasted_iota(jnp.int32, shape, axis)


def kernel(
    n_o,
    n_f,
    slices_ref,
    codes_ref,
    fluence_ref,
    counts_ref,
    new_ref,
    out_ref,
    raw,
    count_high,
    count_low,
    held,
    codes,
    stats,
    dens,
    gather_to,
    gather_from,
    shifts,
    moved,
    tiles,
    marks,
    logs,
    part_out,
    part_in,
    volume,
    spread,
    hits_out,
    hits_in,
    load_sem,
    send_sem,
    recv_sem,
):
    o = lax.axis_index("orient")
    f = lax.axis_index("frame")
    n = n_o * n_f
    me = o * n_f + f
    rows = slices_ref.shape[0]
    frames = counts_ref.shape[0]
    pair = 2 * rows
    block = n_f * SUB
    places = n_o * block
    chunks = frames // TILE

    barrier = pltpu.get_barrier_semaphore()

    def greet(j, c):
        peer = lax.rem(me + j, n)
        pl.semaphore_signal(
            barrier,
            inc=1,
            device_id=(lax.div(peer, n_f), lax.rem(peer, n_f)),
            device_id_type=MESH,
        )
        return c

    lax.fori_loop(1, n, greet, 0)
    step = frames // LOAD
    for i in range(LOAD):
        pltpu.make_async_copy(
            counts_ref.at[pl.ds(i * step, step)], raw.at[pl.ds(i * step, step)], load_sem.at[i]
        ).start()
    pl.semaphore_wait(barrier, n - 1)

    def copy(which, src, dst, to):
        return pltpu.make_async_remote_copy(
            src_ref=src,
            dst_ref=dst,
            send_sem=send_sem.at[which],
            recv_sem=recv_sem.at[which],
            device_id=to,
            device_id_type=MESH,
        )

    def send_frame(which, src, dst):
        def body(j, c):
            peer = lax.rem(f + j, n_f)
            copy(which, src(peer), dst, (o, peer)).start()
            return c

        lax.fori_loop(1, n_f, body, 0)

    def send_orient(which, src, dst):
        def body(j, c):
            peer = lax.rem(o + j, n_o)
            copy(which, src(peer), dst, (peer, f)).start()
            return c

        lax.fori_loop(1, n_o, body, 0)

    def received(which, whole):
        copy(which, whole, whole, (lax.rem(o + 1, n_o), f)).wait_recv()

    def sent(which, whole):
        copy(which, whole, whole, (lax.rem(o + 1, n_o), f)).wait_send()

    send_frame(0, lambda peer: codes_ref, codes.at[f])
    send_frame(1, lambda peer: slices_ref, held.at[0, f])
    codes[f] = codes_ref[...]
    held[0, f] = slices_ref[...]

    for i in range(LOAD):
        pltpu.make_async_copy(
            counts_ref.at[pl.ds(i * step, step)], raw.at[pl.ds(i * step, step)], load_sem.at[i]
        ).wait()

        def convert(j, c):
            at = pl.ds(pl.multiple_of(i * step + j * 16, 16), 16)
            high, low = split2(raw[at, :])
            count_high[at, :] = high
            count_low[at, :] = low
            return c

        lax.fori_loop(0, step // 16, convert, 0)

    received(0, codes.at[pl.ds(0, n_f - 1)])
    lane = iota((rows, TILE), 1)
    diagonal = iota((rows, TILE), 0) == lane
    eye = iota((pair, pair), 0) == iota((pair, pair), 1)

    def prepare(t, c):
        row = codes[t, 0:1, :]
        at = pl.ds(pl.multiple_of(t * pair, pair), pair)

        def fill(i, c):
            here = pl.ds(pl.multiple_of(i * block, block), block)
            place = (iota((block, pair), 0) + i * block).astype(F32)
            gather_to[here, at] = jnp.where(place == row, 1.0, 0.0).astype(BF16)
            return c

        lax.fori_loop(0, n_o, fill, 0)
        column = jnp.sum(jnp.where(eye, row, 0.0), axis=1, keepdims=True)
        place = iota((pair, places), 1).astype(F32)
        gather_from[at, :] = jnp.where(place == column, 1.0, 0.0).astype(BF16)
        shift = jnp.sum(jnp.where(eye, codes[t, 1:2, :], 0.0), axis=1, keepdims=True)
        shift = jnp.broadcast_to(shift[0:rows], (rows, TILE)).astype(jnp.int32)
        shifts[t] = shift
        mark = jnp.where(lane >= shift, 1.0, 0.0)
        marks[at, :] = jnp.concatenate([mark, 1.0 - mark], axis=0).astype(BF16)
        return c

    lax.fori_loop(0, n_f, prepare, 0)
    received(1, held.at[0, pl.ds(0, n_f - 1)])

    def count_hits():
        index = iota((n_o * SUB, pair), 0)
        place = (lax.div(index, SUB) * block + f * SUB + lax.rem(index, SUB)).astype(F32)
        chosen = jnp.concatenate(
            [jnp.where(place == codes[t, 0:1, :], 1.0, 0.0).astype(BF16) for t in range(n_f)],
            axis=1,
        )
        hits = jnp.dot(chosen, marks[...], preferred_element_type=F32)
        for i in range(n_o):
            hits_out[i] = hits[i * SUB : (i + 1) * SUB]
        send_orient(2, lambda peer: hits_out.at[peer], hits_in.at[o])
        hits_in[o] = hits_out[o]

    def expand(t):
        at = pl.ds(pl.multiple_of(t * pair, pair), pair)
        found = jnp.dot(gather_from[at, :], spread[...], preferred_element_type=F32)
        found = found[:, :TILE] + found[:, TILE:]
        shift = shifts[t]
        value = jnp.where(lane >= shift, found[:rows], found[rows:])
        for k in range(7):
            value = jnp.where(
                (shift & (1 << k)) != 0, pltpu.roll(value, TILE - (1 << k), 1), value
            )
        return value

    def iteration(turn, c):
        def take_logs(t, total):
            value = held[turn, t]
            at = pl.ds(pl.multiple_of(t * TILE, TILE), TILE)
            high, mid, low = split3(jnp.log(value + BACKGROUND))
            logs[0:rows, at] = high
            logs[rows : 2 * rows, at] = mid
            logs[2 * rows : 3 * rows, at] = low
            return total + value

        total = lax.fori_loop(0, n_f, take_logs, jnp.zeros((rows, TILE), F32))
        total = jnp.sum(total, axis=1, keepdims=True)
        across = (((1,), (1,)), ((), ()))
        like = lax.dot_general(
            logs[...], count_high[...], across, preferred_element_type=F32
        ) + lax.dot_general(logs[...], count_low[...], across, preferred_element_type=F32)
        like = like[:rows] + like[rows : 2 * rows] + like[2 * rows :]
        score = SHARPNESS * (like - total * fluence_ref[...])
        top = jnp.max(score, axis=0, keepdims=True)
        expo = jnp.exp(score - top)
        norm = jnp.sum(expo, axis=0, keepdims=True)
        own = stats.at[turn, o]
        for k in range(chunks):
            own[k : k + 1, :] = top[:, k * TILE : (k + 1) * TILE]
            own[chunks + k : chunks + k + 1, :] = norm[:, k * TILE : (k + 1) * TILE]
        send_orient(3 + turn, lambda peer: stats.at[turn, o], stats.at[turn, o])

        @pl.when(turn == 0)
        def _():
            count_hits()

        received(3 + turn, stats.at[turn, pl.ds(0, n_o - 1)])
        peak = stats[turn, 0, 0:chunks, :]
        for i in range(1, n_o):
            peak = jnp.maximum(peak, stats[turn, i, 0:chunks, :])
        whole = jnp.zeros((chunks, TILE), F32)
        for i in range(n_o):
            whole = whole + stats[turn, i, chunks : 2 * chunks, :] * jnp.exp(
                stats[turn, i, 0:chunks, :] - peak
            )
        factor = jnp.exp(stats[turn, o, 0:chunks, :] - peak) / whole
        factor = jnp.concatenate([factor[k : k + 1, :] for k in range(chunks)], axis=1)
        prob = expo * factor
        den = jnp.sum(prob * fluence_ref[...], axis=1, keepdims=True)
        dens[turn, f] = jnp.sum(jnp.where(diagonal, den, 0.0), axis=0, keepdims=True)
        send_frame(5 + turn, lambda peer: dens.at[turn, f], dens.at[turn, f])

        probs = jnp.concatenate(split2(prob), axis=0)
        num = jnp.dot(probs, count_high[...], preferred_element_type=F32) + jnp.dot(
            probs, count_low[...], preferred_element_type=F32
        )
        num = num[:rows] + num[rows:]
        for t in range(n_f):
            value = num[:, t * TILE : (t + 1) * TILE] + jnp.where(f == t, held[turn, t], 0.0)
            shift = shifts[t]
            for k in range(7):
                value = jnp.where((shift & (1 << k)) != 0, pltpu.roll(value, 1 << k, 1), value)
            moved[t] = value
        received(5 + turn, dens.at[turn, pl.ds(0, n_f - 1)])
        weight = dens[turn, 0]
        for i in range(1, n_f):
            weight = weight + dens[turn, i]
        weight = jnp.sum(jnp.where(diagonal, weight, 0.0), axis=1, keepdims=True)
        inverse = 1.0 / (weight + 1.0)
        for t in range(n_f):
            high, low = split2(moved[t] * inverse)
            first = lane >= shifts[t]
            none = jnp.zeros((rows, TILE), BF16)
            at = t * pair
            tiles[at : at + rows, :TILE] = jnp.where(first, high, none)
            tiles[at : at + rows, TILE:] = jnp.where(first, low, none)
            tiles[at + rows : at + pair, :TILE] = jnp.where(first, none, high)
            tiles[at + rows : at + pair, TILE:] = jnp.where(first, none, low)

        def collect(i):
            here = pl.ds(pl.multiple_of(i * block, block), block)
            part = jnp.dot(gather_to[here, :], tiles[...], preferred_element_type=F32)
            part = part[:, :TILE] + part[:, TILE:]
            for k in range(n_f):
                part_out[turn, i * n_f + k] = part[k * SUB : (k + 1) * SUB]

        def give(peer_o, peer_f):
            copy(
                7 + turn,
                part_out.at[turn, peer_o * n_f + peer_f],
                part_in.at[turn, me],
                (peer_o, peer_f),
            ).start()

        def scatter(j, c):
            peer = lax.rem(o + j, n_o)
            collect(peer)

            def each(k, c):
                give(peer, lax.rem(f + k, n_f))
                return c

            lax.fori_loop(0, n_f, each, 0)
            return c

        lax.fori_loop(1, n_o, scatter, 0)
        collect(o)

        def each(k, c):
            give(o, lax.rem(f + k, n_f))
            return c

        lax.fori_loop(1, n_f, each, 0)
        part_in[turn, me] = part_out[turn, me]

        @pl.when(turn == 0)
        def _():
            received(2, hits_in.at[pl.ds(0, n_o - 1)])

        hits = jnp.sum(hits_in[...], axis=0)
        received(7 + turn, part_in.at[turn, pl.ds(0, n - 1)])
        brick = jnp.sum(part_in[turn], axis=0) / jnp.maximum(hits, 1.0)
        out_ref[...] = brick
        volume[turn, me] = brick

        def spread_out(j, c):
            peer = lax.rem(me + j, n)
            copy(
                9 + turn,
                volume.at[turn, me],
                volume.at[turn, me],
                (lax.div(peer, n_f), lax.rem(peer, n_f)),
            ).start()
            return c

        lax.fori_loop(1, n, spread_out, 0)
        received(9 + turn, volume.at[turn, pl.ds(0, n - 1)])
        high, low = split2(volume[turn].reshape(places, TILE))
        spread[:, :TILE] = high
        spread[:, TILE:] = low

        @pl.when(turn < ITERS - 1)
        def _():
            def fill(t, c):
                for k in range(4):
                    held[turn + 1, t * 4 + k] = expand(t * 4 + k)
                return c

            lax.fori_loop(0, n_f // 4, fill, 0)

        return c

    lax.fori_loop(0, ITERS, iteration, 0)
    new_ref[...] = expand(f)

    sent(0, codes.at[pl.ds(0, n_f - 1)])
    sent(1, held.at[0, pl.ds(0, n_f - 1)])
    sent(2, hits_out.at[pl.ds(0, n_o - 1)])
    for turn in range(ITERS):
        sent(3 + turn, stats.at[turn, pl.ds(0, n_o - 1)])
        sent(5 + turn, dens.at[turn, pl.ds(0, n_f - 1)])
        sent(7 + turn, part_out.at[turn, pl.ds(0, n - 1)])
        sent(9 + turn, volume.at[turn, pl.ds(0, n - 1)])


def on_device(n_o, n_f, slices, counts, fluence, tile_brick, tile_base):
    rows = slices.shape[0]
    frames, pixels = counts.shape
    pair = 2 * rows
    block = n_f * SUB
    places = n_o * block
    code = tile_brick[:, :, 0] * VOX + tile_base
    place = code // TILE
    shift = code % TILE
    codes = jnp.concatenate(
        [
            jnp.concatenate([place, place + 1], axis=1),
            jnp.concatenate([shift, shift], axis=1),
            jnp.zeros((SUB - 2, pair), jnp.int32),
        ],
        axis=0,
    ).astype(F32)
    vmem = pl.BlockSpec(memory_space=pltpu.VMEM)
    new, brick = pl.pallas_call(
        functools.partial(kernel, n_o, n_f),
        out_shape=(
            jax.ShapeDtypeStruct((rows, TILE), F32),
            jax.ShapeDtypeStruct((SUB, TILE), F32),
        ),
        in_specs=[vmem, vmem, vmem, pl.BlockSpec(memory_space=pl.ANY)],
        out_specs=(vmem, vmem),
        scratch_shapes=[
            pltpu.VMEM((frames, pixels), F32),
            pltpu.VMEM((frames, pixels), BF16),
            pltpu.VMEM((frames, pixels), BF16),
            pltpu.VMEM((ITERS, n_f, rows, TILE), F32),
            pltpu.VMEM((n_f, SUB, pair), F32),
            pltpu.VMEM((ITERS, n_o, 2 * (frames // TILE), TILE), F32),
            pltpu.VMEM((ITERS, n_f, 1, TILE), F32),
            pltpu.VMEM((places, n_f * pair), BF16),
            pltpu.VMEM((n_f * pair, places), BF16),
            pltpu.VMEM((n_f, rows, TILE), jnp.int32),
            pltpu.VMEM((n_f, rows, TILE), F32),
            pltpu.VMEM((n_f * pair, 2 * TILE), BF16),
            pltpu.VMEM((n_f * pair, TILE), BF16),
            pltpu.VMEM((3 * rows, pixels), BF16),
            pltpu.VMEM((ITERS, n_o * n_f, SUB, TILE), F32),
            pltpu.VMEM((ITERS, n_o * n_f, SUB, TILE), F32),
            pltpu.VMEM((ITERS, n_o * n_f, SUB, TILE), F32),
            pltpu.VMEM((places, 2 * TILE), BF16),
            pltpu.VMEM((n_o, SUB, TILE), F32),
            pltpu.VMEM((n_o, SUB, TILE), F32),
            pltpu.SemaphoreType.DMA((LOAD,)),
            pltpu.SemaphoreType.DMA((3 + 4 * ITERS,)),
            pltpu.SemaphoreType.DMA((3 + 4 * ITERS,)),
        ],
        compiler_params=pltpu.CompilerParams(
            collective_id=0, has_side_effects=True, vmem_limit_bytes=60 << 20
        ),
    )(slices, codes, fluence[None, :], counts)
    return new, brick.reshape(1, SUB * TILE)


def solution(mesh):
    n_o, n_f = mesh.shape["orient"], mesh.shape["frame"]
    in_specs = (
        P("orient", "frame"),
        P("frame", None),
        P("frame"),
        P("frame", "orient", None),
        P("frame", "orient"),
    )
    out_specs = (P("orient", "frame"), P(("orient", "frame"), None))
    return jax.shard_map(
        functools.partial(on_device, n_o, n_f),
        mesh=mesh,
        in_specs=in_specs,
        out_specs=out_specs,
        check_vma=False,
    )
```

```python
import functools

import jax
import jax.numpy as jnp
from jax import lax
from jax.experimental import pallas as pl
from jax.experimental.pallas import tpu as pltpu
from jax.sharding import PartitionSpec as P

VOX = 1024
TILE = 128
SUB = VOX // TILE
ITERS = 2
BACKGROUND = 0.1
SHARPNESS = 0.02
MESH = pl.DeviceIdType.MESH
F32 = jnp.float32
BF16 = jnp.bfloat16
LOAD = 4


def split2(x):
    high = x.astype(BF16)
    return high, (x - high.astype(F32)).astype(BF16)


def split3(x):
    high = x.astype(BF16)
    rest = x - high.astype(F32)
    mid = rest.astype(BF16)
    return high, mid, (rest - mid.astype(F32)).astype(BF16)


def iota(shape, axis):
    return lax.broadcasted_iota(jnp.int32, shape, axis)


def kernel(
    n_o,
    n_f,
    slices_ref,
    brick_ref,
    base_ref,
    fluence_ref,
    counts_ref,
    new_ref,
    out_ref,
    raw,
    count_high,
    count_low,
    held,
    stats,
    dens,
    gather_to,
    gather_from,
    shifts,
    moved,
    tiles,
    marks,
    logs,
    part_out,
    part_in,
    volume,
    spread,
    hits_out,
    hits_in,
    load_sem,
    send_sem,
    recv_sem,
    first_recv,
    first_pass,
    wide_recv,
    wide_pass,
):
    o = lax.axis_index("orient")
    f = lax.axis_index("frame")
    n = n_o * n_f
    me = o * n_f + f
    rows = slices_ref.shape[0]
    frames = counts_ref.shape[0]
    pair = 2 * rows
    block = n_f * SUB
    places = n_o * block
    chunks = frames // TILE
    half = n_f // 2
    ring = n_f // 4
    core = lax.rem(f, 2)
    chip = lax.div(f, 2)
    sibling = f + 1 - 2 * core
    mine = core * half + chip
    lane = iota((rows, TILE), 1)

    barrier = pltpu.get_barrier_semaphore()

    def greet(j, c):
        peer = lax.rem(me + j, n)
        pl.semaphore_signal(
            barrier,
            inc=1,
            device_id=(lax.div(peer, n_f), lax.rem(peer, n_f)),
            device_id_type=MESH,
        )
        return c

    lax.fori_loop(1, n, greet, 0)
    step = frames // LOAD
    for i in range(LOAD):
        pltpu.make_async_copy(
            counts_ref.at[pl.ds(i * step, step)], raw.at[pl.ds(i * step, step)], load_sem.at[i]
        ).start()

    held[0, f, 0:rows] = slices_ref[...]
    named = brick_ref[...]
    inside = lax.rem(named, n_f)
    place = (
        lax.div(named, n_f) * block
        + (lax.rem(inside, 2) * half + lax.div(inside, 2)) * SUB
        + lax.div(base_ref[...], TILE)
    )
    shift = lax.rem(base_ref[...], TILE)
    held[0, f, rows : rows + 1] = jnp.concatenate([place, place + 1], axis=1).astype(F32)
    held[0, f, rows + 1 : rows + 2] = jnp.concatenate([shift, shift], axis=1).astype(F32)
    held[0, f, rows + 2 : rows + SUB] = jnp.zeros((SUB - 2, TILE), F32)

    for i in range(LOAD):
        pltpu.make_async_copy(
            counts_ref.at[pl.ds(i * step, step)], raw.at[pl.ds(i * step, step)], load_sem.at[i]
        ).wait()

        def convert(j, c):
            at = pl.ds(pl.multiple_of(i * step + j * 16, 16), 16)
            high, low = split2(raw[at, :])
            count_high[at, :] = high
            count_low[at, :] = low
            return c

        lax.fori_loop(0, step // 16, convert, 0)

    pl.semaphore_wait(barrier, n - 1)

    def copy(which, src, dst, to):
        return pltpu.make_async_remote_copy(
            src_ref=src,
            dst_ref=dst,
            send_sem=send_sem.at[which],
            recv_sem=recv_sem.at[which],
            device_id=to,
            device_id_type=MESH,
        )

    def send_frame(which, src, dst):
        def body(j, c):
            peer = lax.rem(f + j, n_f)
            copy(which, src(peer), dst, (o, peer)).start()
            return c

        lax.fori_loop(1, n_f, body, 0)

    def send_orient(which, src, dst):
        def body(j, c):
            peer = lax.rem(o + j, n_o)
            copy(which, src(peer), dst, (peer, f)).start()
            return c

        lax.fori_loop(1, n_o, body, 0)

    def received(which, whole):
        copy(which, whole, whole, (lax.rem(o + 1, n_o), f)).wait_recv()

    def sent(which, whole):
        copy(which, whole, whole, (lax.rem(o + 1, n_o), f)).wait_send()

    def chip_at(k):
        x = lax.rem(lax.div(chip, 2) + lax.div(k, 2) + ring // 2, ring)
        return x * 2 + lax.rem(chip + 1 + k, 2)

    def far_first(i):
        return lax.rem(o + n_o // 2 + (1 - 2 * lax.rem(i, 2)) * lax.div(i + 1, 2), n_o)

    def deliver(src, dst, out, into, to):
        return pltpu.make_async_remote_copy(
            src_ref=src,
            dst_ref=dst,
            send_sem=out,
            recv_sem=into,
            device_id=to,
            device_id_type=MESH,
        )

    def pass_first(at):
        packet = held.at[0, at * 2 + core]
        deliver(packet, packet, send_sem.at[1], first_pass.at[at], (o, sibling)).start()

    def send_first(k, c):
        at = chip_at(k)

        @pl.when(at != chip)
        def _():
            packet = held.at[0, f]
            deliver(
                packet, packet, send_sem.at[0], first_recv.at[chip], (o, at * 2 + core)
            ).start()

        return c

    lax.fori_loop(0, half, send_first, 0)
    pass_first(chip)

    def relay_first(k, c):
        at = chip_at(half - 1 - k)

        @pl.when(at != chip)
        def _():
            packet = held.at[0, at * 2 + core]
            deliver(packet, packet, send_sem.at[0], first_recv.at[at], (o, sibling)).wait_recv()
            pass_first(at)

        return c

    lax.fori_loop(0, half, relay_first, 0)

    def land_first(k, c):
        at = chip_at(half - 1 - k)
        packet = held.at[0, at * 2 + 1 - core]
        deliver(packet, packet, send_sem.at[1], first_pass.at[at], (o, sibling)).wait_recv()
        return c

    lax.fori_loop(0, half, land_first, 0)
    diagonal = iota((rows, TILE), 0) == lane
    eye = iota((pair, pair), 0) == iota((pair, pair), 1)

    def prepare(t, c):
        row = held[0, t, rows : rows + 1]
        at = pl.ds(pl.multiple_of(t * pair, pair), pair)

        def fill(i, c):
            here = pl.ds(pl.multiple_of(i * block, block), block)
            place = (iota((block, pair), 0) + i * block).astype(F32)
            gather_to[here, at] = jnp.where(place == row, 1.0, 0.0).astype(BF16)
            return c

        lax.fori_loop(0, n_o, fill, 0)
        column = jnp.sum(jnp.where(eye, row, 0.0), axis=1, keepdims=True)
        place = iota((pair, places), 1).astype(F32)
        gather_from[at, :] = jnp.where(place == column, 1.0, 0.0).astype(BF16)
        shift = jnp.sum(jnp.where(eye, held[0, t, rows + 1 : rows + 2], 0.0), axis=1, keepdims=True)
        shift = jnp.broadcast_to(shift[0:rows], (rows, TILE)).astype(jnp.int32)
        shifts[t] = shift
        mark = jnp.where(lane >= shift, 1.0, 0.0)
        marks[at, :] = jnp.concatenate([mark, 1.0 - mark], axis=0).astype(BF16)
        return c

    lax.fori_loop(0, n_f, prepare, 0)

    def count_hits():
        index = iota((n_o * SUB, pair), 0)
        place = (lax.div(index, SUB) * block + mine * SUB + lax.rem(index, SUB)).astype(F32)
        chosen = jnp.concatenate(
            [jnp.where(place == held[0, t, rows : rows + 1], 1.0, 0.0).astype(BF16) for t in range(n_f)],
            axis=1,
        )
        hits = jnp.dot(chosen, marks[...], preferred_element_type=F32)
        for i in range(n_o):
            hits_out[i] = hits[i * SUB : (i + 1) * SUB]
        send_orient(2, lambda peer: hits_out.at[peer], hits_in.at[o])
        hits_in[o] = hits_out[o]

    def expand(t):
        at = pl.ds(pl.multiple_of(t * pair, pair), pair)
        found = jnp.dot(gather_from[at, :], spread[...], preferred_element_type=F32)
        found = found[:, :TILE] + found[:, TILE:]
        shift = shifts[t]
        value = jnp.where(lane >= shift, found[:rows], found[rows:])
        for k in range(7):
            value = jnp.where(
                (shift & (1 << k)) != 0, pltpu.roll(value, TILE - (1 << k), 1), value
            )
        return value

    def iteration(turn, c):
        def take_logs(t, total):
            value = held[turn, t, 0:rows]
            at = pl.ds(pl.multiple_of(t * TILE, TILE), TILE)
            high, mid, low = split3(jnp.log(value + BACKGROUND))
            logs[0:rows, at] = high
            logs[rows : 2 * rows, at] = mid
            logs[2 * rows : 3 * rows, at] = low
            return total + value

        total = lax.fori_loop(0, n_f, take_logs, jnp.zeros((rows, TILE), F32))
        total = jnp.sum(total, axis=1, keepdims=True)
        across = (((1,), (1,)), ((), ()))
        like = lax.dot_general(
            logs[...], count_high[...], across, preferred_element_type=F32
        ) + lax.dot_general(logs[...], count_low[...], across, preferred_element_type=F32)
        like = like[:rows] + like[rows : 2 * rows] + like[2 * rows :]
        score = SHARPNESS * (like - total * fluence_ref[...])
        top = jnp.max(score, axis=0, keepdims=True)
        expo = jnp.exp(score - top)
        norm = jnp.sum(expo, axis=0, keepdims=True)
        own = stats.at[turn, o]
        for k in range(chunks):
            own[k : k + 1, :] = top[:, k * TILE : (k + 1) * TILE]
            own[chunks + k : chunks + k + 1, :] = norm[:, k * TILE : (k + 1) * TILE]
        send_orient(3 + turn, lambda peer: stats.at[turn, o], stats.at[turn, o])

        @pl.when(turn == 0)
        def _():
            count_hits()

        received(3 + turn, stats.at[turn, pl.ds(0, n_o - 1)])
        peak = stats[turn, 0, 0:chunks, :]
        for i in range(1, n_o):
            peak = jnp.maximum(peak, stats[turn, i, 0:chunks, :])
        whole = jnp.zeros((chunks, TILE), F32)
        for i in range(n_o):
            whole = whole + stats[turn, i, chunks : 2 * chunks, :] * jnp.exp(
                stats[turn, i, 0:chunks, :] - peak
            )
        factor = jnp.exp(stats[turn, o, 0:chunks, :] - peak) / whole
        factor = jnp.concatenate([factor[k : k + 1, :] for k in range(chunks)], axis=1)
        prob = expo * factor
        den = jnp.sum(prob * fluence_ref[...], axis=1, keepdims=True)
        dens[turn, f] = jnp.sum(jnp.where(diagonal, den, 0.0), axis=0, keepdims=True)
        send_frame(5 + turn, lambda peer: dens.at[turn, f], dens.at[turn, f])

        probs = jnp.concatenate(split2(prob), axis=0)
        num = jnp.dot(probs, count_high[...], preferred_element_type=F32) + jnp.dot(
            probs, count_low[...], preferred_element_type=F32
        )
        num = num[:rows] + num[rows:]
        for t in range(n_f):
            value = num[:, t * TILE : (t + 1) * TILE] + jnp.where(f == t, held[turn, t, 0:rows], 0.0)
            shift = shifts[t]
            for k in range(7):
                value = jnp.where((shift & (1 << k)) != 0, pltpu.roll(value, 1 << k, 1), value)
            moved[t] = value
        received(5 + turn, dens.at[turn, pl.ds(0, n_f - 1)])
        weight = dens[turn, 0]
        for i in range(1, n_f):
            weight = weight + dens[turn, i]
        weight = jnp.sum(jnp.where(diagonal, weight, 0.0), axis=1, keepdims=True)
        inverse = 1.0 / (weight + 1.0)
        for t in range(n_f):
            high, low = split2(moved[t] * inverse)
            first = lane >= shifts[t]
            none = jnp.zeros((rows, TILE), BF16)
            at = t * pair
            tiles[at : at + rows, :TILE] = jnp.where(first, high, none)
            tiles[at : at + rows, TILE:] = jnp.where(first, low, none)
            tiles[at + rows : at + pair, :TILE] = jnp.where(first, none, high)
            tiles[at + rows : at + pair, TILE:] = jnp.where(first, none, low)

        def collect(i):
            here = pl.ds(pl.multiple_of(i * block, block), block)
            part = jnp.dot(gather_to[here, :], tiles[...], preferred_element_type=F32)
            part = part[:, :TILE] + part[:, TILE:]
            for k in range(n_f):
                part_out[turn, i * n_f + k] = part[k * SUB : (k + 1) * SUB]

        def scatter(i, c):
            peer = far_first(i)
            collect(peer)

            def give(k, c):
                at = chip_at(lax.div(k, 2))
                side = lax.rem(core + k, 2)

                @pl.when((peer != o) | (at * 2 + side != f))
                def _():
                    deliver(
                        part_out.at[turn, peer * n_f + side * half + at],
                        part_in.at[turn, me],
                        send_sem.at[7 + turn],
                        recv_sem.at[7 + turn],
                        (peer, at * 2 + side),
                    ).start()

                return c

            lax.fori_loop(0, n_f, give, 0)
            return c

        lax.fori_loop(0, n_o, scatter, 0)
        part_in[turn, me] = part_out[turn, o * n_f + mine]

        @pl.when(turn == 0)
        def _():
            received(2, hits_in.at[pl.ds(0, n_o - 1)])

        hits = jnp.sum(hits_in[...], axis=0)
        received(7 + turn, part_in.at[turn, pl.ds(0, n - 1)])
        brick = jnp.sum(part_in[turn], axis=0) / jnp.maximum(hits, 1.0)
        out_ref[...] = brick
        slot = o * n_f + mine
        volume[turn, slot] = brick

        def spread_out(i, c):
            peer = far_first(i)

            def give(k, c):
                at = chip_at(k)

                @pl.when((peer != o) | (at != chip))
                def _():
                    deliver(
                        volume.at[turn, slot],
                        volume.at[turn, slot],
                        send_sem.at[9 + turn],
                        wide_recv.at[turn, o],
                        (peer, at * 2 + core),
                    ).start()

                return c

            return lax.fori_loop(0, half, give, c)

        lax.fori_loop(0, n_o, spread_out, 0)

        def relay(i, c):
            peer = far_first(n_o - 1 - i)

            @pl.when(peer == o)
            def _():
                few = volume.at[turn, pl.ds(0, half - 1)]
                deliver(
                    few, few, send_sem.at[9 + turn], wide_recv.at[turn, peer], (o, sibling)
                ).wait_recv()

            bricks = volume.at[turn, pl.ds(peer * n_f + core * half, half)]

            @pl.when(peer != o)
            def _():
                deliver(
                    bricks, bricks, send_sem.at[9 + turn], wide_recv.at[turn, peer], (o, sibling)
                ).wait_recv()

            deliver(
                bricks, bricks, send_sem.at[11 + turn], wide_pass.at[turn, peer], (o, sibling)
            ).start()
            return c

        lax.fori_loop(0, n_o, relay, 0)

        def land(i, c):
            peer = far_first(n_o - 1 - i)
            bricks = volume.at[turn, pl.ds(peer * n_f + (1 - core) * half, half)]
            deliver(
                bricks, bricks, send_sem.at[11 + turn], wide_pass.at[turn, peer], (o, sibling)
            ).wait_recv()
            here = pl.ds(pl.multiple_of(peer * block, block), block)
            high, low = split2(volume[turn, pl.ds(peer * n_f, n_f)].reshape(block, TILE))
            spread[here, :TILE] = high
            spread[here, TILE:] = low
            return c

        lax.fori_loop(0, n_o, land, 0)

        @pl.when(turn < ITERS - 1)
        def _():
            def fill(t, c):
                for k in range(4):
                    held[turn + 1, t * 4 + k, 0:rows] = expand(t * 4 + k)
                return c

            lax.fori_loop(0, n_f // 4, fill, 0)

        return c

    lax.fori_loop(0, ITERS, iteration, 0)
    new_ref[...] = expand(f)

    sent(0, held.at[0, pl.ds(0, half - 1)])
    sent(1, held.at[0, pl.ds(0, half)])
    sent(2, hits_out.at[pl.ds(0, n_o - 1)])
    for turn in range(ITERS):
        sent(3 + turn, stats.at[turn, pl.ds(0, n_o - 1)])
        sent(5 + turn, dens.at[turn, pl.ds(0, n_f - 1)])
        sent(7 + turn, part_out.at[turn, pl.ds(0, n - 1)])
        sent(9 + turn, volume.at[turn, pl.ds(0, n_o * half - 1)])
        sent(11 + turn, volume.at[turn, pl.ds(0, n_o * half)])


def on_device(n_o, n_f, slices, counts, fluence, tile_brick, tile_base):
    rows = slices.shape[0]
    frames, pixels = counts.shape
    pair = 2 * rows
    block = n_f * SUB
    places = n_o * block
    vmem = pl.BlockSpec(memory_space=pltpu.VMEM)
    new, brick = pl.pallas_call(
        functools.partial(kernel, n_o, n_f),
        out_shape=(
            jax.ShapeDtypeStruct((rows, TILE), F32),
            jax.ShapeDtypeStruct((SUB, TILE), F32),
        ),
        in_specs=[vmem, vmem, vmem, vmem, pl.BlockSpec(memory_space=pl.ANY)],
        out_specs=(vmem, vmem),
        scratch_shapes=[
            pltpu.VMEM((frames, pixels), F32),
            pltpu.VMEM((frames, pixels), BF16),
            pltpu.VMEM((frames, pixels), BF16),
            pltpu.VMEM((ITERS, n_f, rows + SUB, TILE), F32),
            pltpu.VMEM((ITERS, n_o, 2 * (frames // TILE), TILE), F32),
            pltpu.VMEM((ITERS, n_f, 1, TILE), F32),
            pltpu.VMEM((places, n_f * pair), BF16),
            pltpu.VMEM((n_f * pair, places), BF16),
            pltpu.VMEM((n_f, rows, TILE), jnp.int32),
            pltpu.VMEM((n_f, rows, TILE), F32),
            pltpu.VMEM((n_f * pair, 2 * TILE), BF16),
            pltpu.VMEM((n_f * pair, TILE), BF16),
            pltpu.VMEM((3 * rows, pixels), BF16),
            pltpu.VMEM((ITERS, n_o * n_f, SUB, TILE), F32),
            pltpu.VMEM((ITERS, n_o * n_f, SUB, TILE), F32),
            pltpu.VMEM((ITERS, n_o * n_f, SUB, TILE), F32),
            pltpu.VMEM((places, 2 * TILE), BF16),
            pltpu.VMEM((n_o, SUB, TILE), F32),
            pltpu.VMEM((n_o, SUB, TILE), F32),
            pltpu.SemaphoreType.DMA((LOAD,)),
            pltpu.SemaphoreType.DMA((3 + 5 * ITERS,)),
            pltpu.SemaphoreType.DMA((3 + 5 * ITERS,)),
            pltpu.SemaphoreType.DMA((n_f // 2,)),
            pltpu.SemaphoreType.DMA((n_f // 2,)),
            pltpu.SemaphoreType.DMA((ITERS, n_o)),
            pltpu.SemaphoreType.DMA((ITERS, n_o)),
        ],
        compiler_params=pltpu.CompilerParams(
            collective_id=0, has_side_effects=True, vmem_limit_bytes=60 << 20
        ),
    )(slices, tile_brick[:, :, 0], tile_base, fluence[None, :], counts)
    return new, brick.reshape(1, SUB * TILE)


def solution(mesh):
    n_o, n_f = mesh.shape["orient"], mesh.shape["frame"]
    in_specs = (
        P("orient", "frame"),
        P("frame", None),
        P("frame"),
        P("frame", "orient", None),
        P("frame", "orient"),
    )
    out_specs = (P("orient", "frame"), P(("orient", "frame"), None))
    return jax.shard_map(
        functools.partial(on_device, n_o, n_f),
        mesh=mesh,
        in_specs=in_specs,
        out_specs=out_specs,
        check_vma=False,
    )
```

```python
import functools

import jax
import jax.numpy as jnp
from jax import lax
from jax.experimental import pallas as pl
from jax.experimental.pallas import tpu as pltpu
from jax.sharding import PartitionSpec as P

VOX = 1024
TILE = 128
SUB = VOX // TILE
ITERS = 2
BACKGROUND = 0.1
SHARPNESS = 0.02
MESH = pl.DeviceIdType.MESH
F32 = jnp.float32
BF16 = jnp.bfloat16
LOAD = 4


def split2(x):
    high = x.astype(BF16)
    return high, (x - high.astype(F32)).astype(BF16)


def split3(x):
    high = x.astype(BF16)
    rest = x - high.astype(F32)
    mid = rest.astype(BF16)
    return high, mid, (rest - mid.astype(F32)).astype(BF16)


def iota(shape, axis):
    return lax.broadcasted_iota(jnp.int32, shape, axis)


def kernel(
    n_o,
    n_f,
    slices_ref,
    brick_ref,
    base_ref,
    fluence_ref,
    counts_ref,
    new_ref,
    out_ref,
    raw,
    count_high,
    count_low,
    held,
    stats,
    dens,
    gather_to,
    gather_from,
    shifts,
    moved,
    tiles,
    marks,
    logs,
    part_out,
    part_in,
    volume,
    spread,
    hits_out,
    hits_in,
    load_sem,
    send_sem,
    recv_sem,
    first_recv,
    first_pass,
    wide_recv,
    wide_pass,
):
    o = lax.axis_index("orient")
    f = lax.axis_index("frame")
    n = n_o * n_f
    me = o * n_f + f
    rows = slices_ref.shape[0]
    frames = counts_ref.shape[0]
    pair = 2 * rows
    block = n_f * SUB
    places = n_o * block
    chunks = frames // TILE
    half = n_f // 2
    ring = n_f // 4
    core = lax.rem(f, 2)
    chip = lax.div(f, 2)
    sibling = f + 1 - 2 * core
    mine = core * half + chip
    lane = iota((rows, TILE), 1)

    near = lambda d, size: min(d, size - d)
    turns_o = sorted(range(n_o), key=lambda d: -near(d, n_o))
    turns_f = sorted(
        ((x, y, c) for x in range(ring) for y in range(2) for c in range(2)),
        key=lambda d: -(4 * near(d[0], ring) + 4 * d[1] + d[2]),
    )
    peers_o = [lax.rem(o + d, n_o) for d in turns_o]
    chip_x, chip_y = lax.div(chip, 2), lax.rem(chip, 2)
    chips = [
        lax.rem(chip_x + x, ring) * 2 + lax.rem(chip_y + y, 2) for x, y, c in turns_f
    ]
    sides = [lax.rem(core + c, 2) for x, y, c in turns_f]
    peers_f = [at * 2 + side for at, side in zip(chips, sides)]
    slots_f = [side * half + at for at, side in zip(chips, sides)]
    here_f = turns_f.index((0, 0, 0))
    same_core = [k for k in range(n_f) if turns_f[k][2] == 0]

    step = frames // LOAD
    for i in range(LOAD):
        pltpu.make_async_copy(
            counts_ref.at[pl.ds(i * step, step)], raw.at[pl.ds(i * step, step)], load_sem.at[i]
        ).start()
    barrier = pltpu.get_barrier_semaphore()
    for i in range(n_o):
        for k in range(n_f):
            if turns_o[i] != 0 or k != here_f:
                pl.semaphore_signal(
                    barrier, inc=1, device_id=(peers_o[i], peers_f[k]), device_id_type=MESH
                )

    held[0, f, 0:rows] = slices_ref[...]
    named = brick_ref[...]
    inside = lax.rem(named, n_f)
    place = (
        lax.div(named, n_f) * block
        + (lax.rem(inside, 2) * half + lax.div(inside, 2)) * SUB
        + lax.div(base_ref[...], TILE)
    )
    shift = lax.rem(base_ref[...], TILE)
    held[0, f, rows : rows + 1] = jnp.concatenate([place, place + 1], axis=1).astype(F32)
    held[0, f, rows + 1 : rows + 2] = jnp.concatenate([shift, shift], axis=1).astype(F32)
    held[0, f, rows + 2 : rows + SUB] = jnp.zeros((SUB - 2, TILE), F32)

    for i in range(LOAD):
        pltpu.make_async_copy(
            counts_ref.at[pl.ds(i * step, step)], raw.at[pl.ds(i * step, step)], load_sem.at[i]
        ).wait()

        def convert(j, c):
            at = pl.ds(pl.multiple_of(i * step + j * 16, 16), 16)
            high, low = split2(raw[at, :])
            count_high[at, :] = high
            count_low[at, :] = low
            return c

        lax.fori_loop(0, step // 16, convert, 0)

    pl.semaphore_wait(barrier, n - 1)

    def copy(which, src, dst, to):
        return pltpu.make_async_remote_copy(
            src_ref=src,
            dst_ref=dst,
            send_sem=send_sem.at[which],
            recv_sem=recv_sem.at[which],
            device_id=to,
            device_id_type=MESH,
        )

    def send_frame(which, src, dst):
        def body(j, c):
            peer = lax.rem(f + j, n_f)
            copy(which, src(peer), dst, (o, peer)).start()
            return c

        lax.fori_loop(1, n_f, body, 0)

    def send_orient(which, src, dst):
        def body(j, c):
            peer = lax.rem(o + j, n_o)
            copy(which, src(peer), dst, (peer, f)).start()
            return c

        lax.fori_loop(1, n_o, body, 0)

    def received(which, whole):
        copy(which, whole, whole, (lax.rem(o + 1, n_o), f)).wait_recv()

    def sent(which, whole):
        copy(which, whole, whole, (lax.rem(o + 1, n_o), f)).wait_send()

    def deliver(src, dst, out, into, to):
        return pltpu.make_async_remote_copy(
            src_ref=src,
            dst_ref=dst,
            send_sem=out,
            recv_sem=into,
            device_id=to,
            device_id_type=MESH,
        )

    def pass_first(at):
        packet = held.at[0, at * 2 + core]
        deliver(packet, packet, send_sem.at[1], first_pass.at[at], (o, sibling)).start()

    away = [k for k in same_core if k != here_f]
    for k in away:
        packet = held.at[0, f]
        deliver(packet, packet, send_sem.at[0], first_recv.at[chip], (o, peers_f[k])).start()
    pass_first(chip)
    for k in reversed(away):
        packet = held.at[0, peers_f[k]]
        into = first_recv.at[chips[k]]
        deliver(packet, packet, send_sem.at[0], into, (o, sibling)).wait_recv()
        pass_first(chips[k])
    for k in reversed(same_core):
        packet = held.at[0, chips[k] * 2 + 1 - core]
        into = first_pass.at[chips[k]]
        deliver(packet, packet, send_sem.at[1], into, (o, sibling)).wait_recv()
    diagonal = iota((rows, TILE), 0) == lane
    eye = iota((pair, pair), 0) == iota((pair, pair), 1)

    def prepare_to(t):
        row = held[0, t, rows : rows + 1]
        at = pl.ds(pl.multiple_of(t * pair, pair), pair)
        for i in range(n_o):
            place = (iota((block, pair), 0) + i * block).astype(F32)
            gather_to[i * block : (i + 1) * block, at] = jnp.where(
                place == row, 1.0, 0.0
            ).astype(BF16)
        shift = jnp.sum(
            jnp.where(eye, held[0, t, rows + 1 : rows + 2], 0.0), axis=1, keepdims=True
        )
        shift = jnp.broadcast_to(shift[0:rows], (rows, TILE)).astype(jnp.int32)
        shifts[t] = shift
        mark = jnp.where(lane >= shift, 1.0, 0.0)
        marks[at, :] = jnp.concatenate([mark, 1.0 - mark], axis=0).astype(BF16)

    def prepare_from(t):
        row = held[0, t, rows : rows + 1]
        at = pl.ds(pl.multiple_of(t * pair, pair), pair)
        column = jnp.sum(jnp.where(eye, row, 0.0), axis=1, keepdims=True)
        place = iota((pair, places), 1).astype(F32)
        gather_from[at, :] = jnp.where(place == column, 1.0, 0.0).astype(BF16)

    def by_twos(work):
        def body(t, c):
            work(t * 2)
            work(t * 2 + 1)
            return c

        lax.fori_loop(0, n_f // 2, body, 0)

    def count_hits():
        index = iota((n_o * SUB, pair), 0)
        place = (lax.div(index, SUB) * block + mine * SUB + lax.rem(index, SUB)).astype(F32)
        chosen = jnp.concatenate(
            [jnp.where(place == held[0, t, rows : rows + 1], 1.0, 0.0).astype(BF16) for t in range(n_f)],
            axis=1,
        )
        hits = jnp.dot(chosen, marks[...], preferred_element_type=F32)
        for i in range(n_o):
            hits_out[i] = hits[i * SUB : (i + 1) * SUB]
        send_orient(2, lambda peer: hits_out.at[peer], hits_in.at[o])
        hits_in[o] = hits_out[o]

    def expand(t):
        at = pl.ds(pl.multiple_of(t * pair, pair), pair)
        found = jnp.dot(gather_from[at, :], spread[...], preferred_element_type=F32)
        found = found[:, :TILE] + found[:, TILE:]
        shift = shifts[t]
        value = jnp.where(lane >= shift, found[:rows], found[rows:])
        for k in range(7):
            value = jnp.where(
                (shift & (1 << k)) != 0, pltpu.roll(value, TILE - (1 << k), 1), value
            )
        return value

    def iteration(turn, c):
        def take_logs(t, total):
            value = held[turn, t, 0:rows]
            at = pl.ds(pl.multiple_of(t * TILE, TILE), TILE)
            high, mid, low = split3(jnp.log(value + BACKGROUND))
            logs[0:rows, at] = high
            logs[rows : 2 * rows, at] = mid
            logs[2 * rows : 3 * rows, at] = low
            return total + value

        total = lax.fori_loop(0, n_f, take_logs, jnp.zeros((rows, TILE), F32))
        total = jnp.sum(total, axis=1, keepdims=True)
        across = (((1,), (1,)), ((), ()))
        like = lax.dot_general(
            logs[...], count_high[...], across, preferred_element_type=F32
        ) + lax.dot_general(logs[...], count_low[...], across, preferred_element_type=F32)
        like = like[:rows] + like[rows : 2 * rows] + like[2 * rows :]
        score = SHARPNESS * (like - total * fluence_ref[...])
        top = jnp.max(score, axis=0, keepdims=True)
        expo = jnp.exp(score - top)
        norm = jnp.sum(expo, axis=0, keepdims=True)
        own = stats.at[turn, o]
        for k in range(chunks):
            own[k : k + 1, :] = top[:, k * TILE : (k + 1) * TILE]
            own[chunks + k : chunks + k + 1, :] = norm[:, k * TILE : (k + 1) * TILE]
        send_orient(3 + turn, lambda peer: stats.at[turn, o], stats.at[turn, o])

        @pl.when(turn == 0)
        def _():
            by_twos(prepare_to)
            count_hits()

        received(3 + turn, stats.at[turn, pl.ds(0, n_o - 1)])
        peak = stats[turn, 0, 0:chunks, :]
        for i in range(1, n_o):
            peak = jnp.maximum(peak, stats[turn, i, 0:chunks, :])
        whole = jnp.zeros((chunks, TILE), F32)
        for i in range(n_o):
            whole = whole + stats[turn, i, chunks : 2 * chunks, :] * jnp.exp(
                stats[turn, i, 0:chunks, :] - peak
            )
        factor = jnp.exp(stats[turn, o, 0:chunks, :] - peak) / whole
        factor = jnp.concatenate([factor[k : k + 1, :] for k in range(chunks)], axis=1)
        prob = expo * factor
        den = jnp.sum(prob * fluence_ref[...], axis=1, keepdims=True)
        dens[turn, f] = jnp.sum(jnp.where(diagonal, den, 0.0), axis=0, keepdims=True)
        send_frame(5 + turn, lambda peer: dens.at[turn, f], dens.at[turn, f])

        probs = jnp.concatenate(split2(prob), axis=0)
        num = jnp.dot(probs, count_high[...], preferred_element_type=F32) + jnp.dot(
            probs, count_low[...], preferred_element_type=F32
        )
        num = num[:rows] + num[rows:]
        for t in range(n_f):
            value = num[:, t * TILE : (t + 1) * TILE] + jnp.where(f == t, held[turn, t, 0:rows], 0.0)
            shift = shifts[t]
            for k in range(7):
                value = jnp.where((shift & (1 << k)) != 0, pltpu.roll(value, 1 << k, 1), value)
            moved[t] = value

        @pl.when(turn == 0)
        def _():
            by_twos(prepare_from)

        received(5 + turn, dens.at[turn, pl.ds(0, n_f - 1)])
        weight = dens[turn, 0]
        for i in range(1, n_f):
            weight = weight + dens[turn, i]
        weight = jnp.sum(jnp.where(diagonal, weight, 0.0), axis=1, keepdims=True)
        inverse = 1.0 / (weight + 1.0)
        for t in range(n_f):
            high, low = split2(moved[t] * inverse)
            first = lane >= shifts[t]
            none = jnp.zeros((rows, TILE), BF16)
            at = t * pair
            tiles[at : at + rows, :TILE] = jnp.where(first, high, none)
            tiles[at : at + rows, TILE:] = jnp.where(first, low, none)
            tiles[at + rows : at + pair, :TILE] = jnp.where(first, none, high)
            tiles[at + rows : at + pair, TILE:] = jnp.where(first, none, low)

        def collect(i):
            here = pl.ds(pl.multiple_of(i * block, block), block)
            part = jnp.dot(gather_to[here, :], tiles[...], preferred_element_type=F32)
            part = part[:, :TILE] + part[:, TILE:]
            for k in range(n_f):
                part_out[turn, i * n_f + k] = part[k * SUB : (k + 1) * SUB]

        def give(i):
            for k in range(n_f):
                if turns_o[i] != 0 or k != here_f:
                    deliver(
                        part_out.at[turn, peers_o[i] * n_f + slots_f[k]],
                        part_in.at[turn, me],
                        send_sem.at[7 + turn],
                        recv_sem.at[7 + turn],
                        (peers_o[i], peers_f[k]),
                    ).start()

        for i in range(n_o):
            collect(peers_o[i])
            if i > 0:
                give(i - 1)
        give(n_o - 1)
        part_in[turn, me] = part_out[turn, o * n_f + mine]

        @pl.when(turn == 0)
        def _():
            received(2, hits_in.at[pl.ds(0, n_o - 1)])

        hits = jnp.sum(hits_in[...], axis=0)
        received(7 + turn, part_in.at[turn, pl.ds(0, n - 1)])
        brick = jnp.sum(part_in[turn], axis=0) / jnp.maximum(hits, 1.0)
        out_ref[...] = brick
        slot = o * n_f + mine
        volume[turn, slot] = brick

        for i in range(n_o):
            for k in same_core:
                if turns_o[i] != 0 or k != here_f:
                    deliver(
                        volume.at[turn, slot],
                        volume.at[turn, slot],
                        send_sem.at[9 + turn],
                        wide_recv.at[turn, o],
                        (peers_o[i], peers_f[k]),
                    ).start()

        for i in reversed(range(n_o)):
            peer = peers_o[i]
            count = half if turns_o[i] != 0 else half - 1
            some = volume.at[turn, pl.ds(peer * n_f + core * half, count)]
            deliver(
                some, some, send_sem.at[9 + turn], wide_recv.at[turn, peer], (o, sibling)
            ).wait_recv()
            bricks = volume.at[turn, pl.ds(peer * n_f + core * half, half)]
            deliver(
                bricks, bricks, send_sem.at[11 + turn], wide_pass.at[turn, peer], (o, sibling)
            ).start()
        for i in reversed(range(n_o)):
            peer = peers_o[i]
            bricks = volume.at[turn, pl.ds(peer * n_f + (1 - core) * half, half)]
            deliver(
                bricks, bricks, send_sem.at[11 + turn], wide_pass.at[turn, peer], (o, sibling)
            ).wait_recv()
            here = pl.ds(pl.multiple_of(peer * block, block), block)
            high, low = split2(volume[turn, pl.ds(peer * n_f, n_f)].reshape(block, TILE))
            spread[here, :TILE] = high
            spread[here, TILE:] = low

        @pl.when(turn < ITERS - 1)
        def _():
            def fill(t, c):
                for k in range(4):
                    held[turn + 1, t * 4 + k, 0:rows] = expand(t * 4 + k)
                return c

            lax.fori_loop(0, n_f // 4, fill, 0)

        return c

    lax.fori_loop(0, ITERS, iteration, 0)
    new_ref[...] = expand(f)

    sent(0, held.at[0, pl.ds(0, half - 1)])
    sent(1, held.at[0, pl.ds(0, half)])
    sent(2, hits_out.at[pl.ds(0, n_o - 1)])
    for turn in range(ITERS):
        sent(3 + turn, stats.at[turn, pl.ds(0, n_o - 1)])
        sent(5 + turn, dens.at[turn, pl.ds(0, n_f - 1)])
        sent(7 + turn, part_out.at[turn, pl.ds(0, n - 1)])
        sent(9 + turn, volume.at[turn, pl.ds(0, n_o * half - 1)])
        sent(11 + turn, volume.at[turn, pl.ds(0, n_o * half)])


def on_device(n_o, n_f, slices, counts, fluence, tile_brick, tile_base):
    rows = slices.shape[0]
    frames, pixels = counts.shape
    pair = 2 * rows
    block = n_f * SUB
    places = n_o * block
    vmem = pl.BlockSpec(memory_space=pltpu.VMEM)
    new, brick = pl.pallas_call(
        functools.partial(kernel, n_o, n_f),
        out_shape=(
            jax.ShapeDtypeStruct((rows, TILE), F32),
            jax.ShapeDtypeStruct((SUB, TILE), F32),
        ),
        in_specs=[vmem, vmem, vmem, vmem, pl.BlockSpec(memory_space=pl.ANY)],
        out_specs=(vmem, vmem),
        scratch_shapes=[
            pltpu.VMEM((frames, pixels), F32),
            pltpu.VMEM((frames, pixels), BF16),
            pltpu.VMEM((frames, pixels), BF16),
            pltpu.VMEM((ITERS, n_f, rows + SUB, TILE), F32),
            pltpu.VMEM((ITERS, n_o, 2 * (frames // TILE), TILE), F32),
            pltpu.VMEM((ITERS, n_f, 1, TILE), F32),
            pltpu.VMEM((places, n_f * pair), BF16),
            pltpu.VMEM((n_f * pair, places), BF16),
            pltpu.VMEM((n_f, rows, TILE), jnp.int32),
            pltpu.VMEM((n_f, rows, TILE), F32),
            pltpu.VMEM((n_f * pair, 2 * TILE), BF16),
            pltpu.VMEM((n_f * pair, TILE), BF16),
            pltpu.VMEM((3 * rows, pixels), BF16),
            pltpu.VMEM((ITERS, n_o * n_f, SUB, TILE), F32),
            pltpu.VMEM((ITERS, n_o * n_f, SUB, TILE), F32),
            pltpu.VMEM((ITERS, n_o * n_f, SUB, TILE), F32),
            pltpu.VMEM((places, 2 * TILE), BF16),
            pltpu.VMEM((n_o, SUB, TILE), F32),
            pltpu.VMEM((n_o, SUB, TILE), F32),
            pltpu.SemaphoreType.DMA((LOAD,)),
            pltpu.SemaphoreType.DMA((3 + 5 * ITERS,)),
            pltpu.SemaphoreType.DMA((3 + 5 * ITERS,)),
            pltpu.SemaphoreType.DMA((n_f // 2,)),
            pltpu.SemaphoreType.DMA((n_f // 2,)),
            pltpu.SemaphoreType.DMA((ITERS, n_o)),
            pltpu.SemaphoreType.DMA((ITERS, n_o)),
        ],
        compiler_params=pltpu.CompilerParams(
            collective_id=0, has_side_effects=True, vmem_limit_bytes=60 << 20
        ),
    )(slices, tile_brick[:, :, 0], tile_base, fluence[None, :], counts)
    return new, brick.reshape(1, SUB * TILE)


def solution(mesh):
    n_o, n_f = mesh.shape["orient"], mesh.shape["frame"]
    in_specs = (
        P("orient", "frame"),
        P("frame", None),
        P("frame"),
        P("frame", "orient", None),
        P("frame", "orient"),
    )
    out_specs = (P("orient", "frame"), P(("orient", "frame"), None))
    return jax.shard_map(
        functools.partial(on_device, n_o, n_f),
        mesh=mesh,
        in_specs=in_specs,
        out_specs=out_specs,
        check_vma=False,
    )
```

```python
import functools

import jax
import jax.numpy as jnp
from jax import lax
from jax.experimental import pallas as pl
from jax.experimental.pallas import tpu as pltpu
from jax.sharding import PartitionSpec as P

VOX = 1024
TILE = 128
SUB = VOX // TILE
ITERS = 2
BACKGROUND = 0.1
SHARPNESS = 0.02
MESH = pl.DeviceIdType.MESH
F32 = jnp.float32
BF16 = jnp.bfloat16
LOAD = 4


def split2(x):
    high = x.astype(BF16)
    return high, (x - high.astype(F32)).astype(BF16)


def split3(x):
    high = x.astype(BF16)
    rest = x - high.astype(F32)
    mid = rest.astype(BF16)
    return high, mid, (rest - mid.astype(F32)).astype(BF16)


def iota(shape, axis):
    return lax.broadcasted_iota(jnp.int32, shape, axis)


def kernel(
    n_o,
    n_f,
    slices_ref,
    brick_ref,
    base_ref,
    fluence_ref,
    counts_ref,
    new_ref,
    out_ref,
    raw,
    count_high,
    count_low,
    count_high_t,
    count_low_t,
    held,
    stats,
    dens,
    gather_to,
    gather_from,
    shifts,
    moved,
    tiles,
    marks,
    logs,
    part_out,
    pair_in,
    paired,
    part_in,
    volume,
    spread,
    hits_out,
    hits_in,
    load_sem,
    send_sem,
    recv_sem,
    first_recv,
    first_pass,
    pair_recv,
    wide_recv,
    wide_pass,
):
    o = lax.axis_index("orient")
    f = lax.axis_index("frame")
    n = n_o * n_f
    me = o * n_f + f
    rows = slices_ref.shape[0]
    frames = counts_ref.shape[0]
    pair = 2 * rows
    block = n_f * SUB
    places = n_o * block
    chunks = frames // TILE
    half = n_f // 2
    ring = n_f // 4
    core = lax.rem(f, 2)
    chip = lax.div(f, 2)
    sibling = f + 1 - 2 * core
    mine = core * half + chip
    lane = iota((rows, TILE), 1)

    def near(d, size):
        return min(d, size - d)

    depth = n_o // 2
    turns_o = sorted(
        ((z, y) for z in range(depth) for y in range(2)), key=lambda d: -near(d[0], depth) - d[1]
    )
    turns_f = sorted(
        ((x, y, c) for x in range(ring) for y in range(2) for c in range(2)),
        key=lambda d: -(4 * near(d[0], ring) + 8 * d[1] + d[2]),
    )
    at_z, at_y = lax.div(o, 2), lax.rem(o, 2)
    peers_o = [lax.rem(at_z + z, depth) * 2 + lax.rem(at_y + y, 2) for z, y in turns_o]
    chip_x, chip_y = lax.div(chip, 2), lax.rem(chip, 2)
    chips = [
        lax.rem(chip_x + x, ring) * 2 + lax.rem(chip_y + y, 2) for x, y, c in turns_f
    ]
    sides = [lax.rem(core + c, 2) for x, y, c in turns_f]
    peers_f = [at * 2 + side for at, side in zip(chips, sides)]
    here_o, here_f = turns_o.index((0, 0)), turns_f.index((0, 0, 0))
    same_core = [k for k in range(n_f) if turns_f[k][2] == 0]

    def hops(i, k):
        (z, low), (x, high, c) = turns_o[i], turns_f[k]
        return near(z, depth) + near(x, ring) + ((0, 1), (2, 1))[high][low]

    pairs = sorted(
        ((i, k) for i in range(n_o) for k in same_core), key=lambda d: -hops(*d)
    )
    far = hops(*pairs[0]) - 1
    others = [d for d in pairs if d != (here_o, here_f)]

    def is_peer(i, k):
        if (i, k) == (here_o, here_f):
            return False
        return k in same_core or i == here_o or hops(i, k) >= far

    step = frames // LOAD
    for i in range(LOAD):
        pltpu.make_async_copy(
            counts_ref.at[pl.ds(i * step, step)], raw.at[pl.ds(i * step, step)], load_sem.at[i]
        ).start()
    barrier = pltpu.get_barrier_semaphore()
    peers = [(i, k) for i in range(n_o) for k in range(n_f) if is_peer(i, k)]
    for i, k in sorted(peers, key=lambda d: -hops(*d)):
        pl.semaphore_signal(
            barrier, inc=1, device_id=(peers_o[i], peers_f[k]), device_id_type=MESH
        )

    held[0, f, 0:rows] = slices_ref[...]
    named = brick_ref[...]
    inside = lax.rem(named, n_f)
    place = (
        lax.div(named, n_f) * block
        + (lax.rem(inside, 2) * half + lax.div(inside, 2)) * SUB
        + lax.div(base_ref[...], TILE)
    )
    shift = lax.rem(base_ref[...], TILE)
    held[0, f, rows : rows + 1] = jnp.concatenate([place, place + 1], axis=1).astype(F32)
    held[0, f, rows + 1 : rows + 2] = jnp.concatenate([shift, shift], axis=1).astype(F32)
    held[0, f, rows + 2 : rows + SUB] = jnp.zeros((SUB - 2, TILE), F32)

    def load(i):
        here = pl.ds(i * step, step)
        pltpu.make_async_copy(counts_ref.at[here], raw.at[here], load_sem.at[i]).wait()

        def convert(j, c):
            at = pl.ds(pl.multiple_of(j * TILE, TILE), TILE)
            high, low = split2(raw[here, at])
            count_high[here, at] = high
            count_low[here, at] = low
            count_high_t[at, here] = high.T
            count_low_t[at, here] = low.T
            return c

        lax.fori_loop(0, n_f, convert, 0)

    for i in range(LOAD):
        load(i)
    pl.semaphore_wait(barrier, len(peers))

    def copy(which, src, dst, to):
        return pltpu.make_async_remote_copy(
            src_ref=src,
            dst_ref=dst,
            send_sem=send_sem.at[which],
            recv_sem=recv_sem.at[which],
            device_id=to,
            device_id_type=MESH,
        )

    def send_frame(which, src, dst):
        def body(j, c):
            peer = lax.rem(f + j, n_f)
            copy(which, src(peer), dst, (o, peer)).start()
            return c

        lax.fori_loop(1, n_f, body, 0)

    def send_orient(which, src, dst):
        def body(j, c):
            peer = lax.rem(o + j, n_o)
            copy(which, src(peer), dst, (peer, f)).start()
            return c

        lax.fori_loop(1, n_o, body, 0)

    def received(which, whole):
        copy(which, whole, whole, (lax.rem(o + 1, n_o), f)).wait_recv()

    def sent(which, whole):
        copy(which, whole, whole, (lax.rem(o + 1, n_o), f)).wait_send()

    def deliver(src, dst, out, into, to):
        return pltpu.make_async_remote_copy(
            src_ref=src,
            dst_ref=dst,
            send_sem=out,
            recv_sem=into,
            device_id=to,
            device_id_type=MESH,
        )

    def pass_first(at):
        packet = held.at[0, at * 2 + core]
        deliver(packet, packet, send_sem.at[1], first_pass.at[at], (o, sibling)).start()

    away = [k for k in same_core if k != here_f]
    for k in away:
        packet = held.at[0, f]
        deliver(packet, packet, send_sem.at[0], first_recv.at[chip], (o, peers_f[k])).start()
    pass_first(chip)
    for k in reversed(away):
        packet = held.at[0, peers_f[k]]
        into = first_recv.at[chips[k]]
        deliver(packet, packet, send_sem.at[0], into, (o, sibling)).wait_recv()
        pass_first(chips[k])
    for k in reversed(same_core):
        packet = held.at[0, chips[k] * 2 + 1 - core]
        into = first_pass.at[chips[k]]
        deliver(packet, packet, send_sem.at[1], into, (o, sibling)).wait_recv()
    diagonal = iota((rows, TILE), 0) == lane
    eye = iota((pair, pair), 0) == iota((pair, pair), 1)

    def prepare_to(t):
        row = held[0, t, rows : rows + 1]
        at = pl.ds(pl.multiple_of(t * pair, pair), pair)
        for i in range(n_o):
            place = (iota((block, pair), 0) + peers_o[i] * block).astype(F32)
            gather_to[i * block : (i + 1) * block, at] = jnp.where(
                place == row, 1.0, 0.0
            ).astype(BF16)
        shift = jnp.sum(
            jnp.where(eye, held[0, t, rows + 1 : rows + 2], 0.0), axis=1, keepdims=True
        )
        shift = jnp.broadcast_to(shift[0:rows], (rows, TILE)).astype(jnp.int32)
        shifts[t] = shift
        mark = jnp.where(lane >= shift, 1.0, 0.0)
        marks[at, :] = jnp.concatenate([mark, 1.0 - mark], axis=0).astype(BF16)

    def prepare_from(t):
        row = held[0, t, rows : rows + 1]
        at = pl.ds(pl.multiple_of(t * pair, pair), pair)
        column = jnp.sum(jnp.where(eye, row, 0.0), axis=1, keepdims=True)
        place = iota((pair, places), 1).astype(F32)
        gather_from[at, :] = jnp.where(place == column, 1.0, 0.0).astype(BF16)

    def by_twos(work):
        def body(t, c):
            work(t * 2)
            work(t * 2 + 1)
            return c

        lax.fori_loop(0, n_f // 2, body, 0)

    def count_hits():
        index = iota((n_o * SUB, pair), 0)
        place = (lax.div(index, SUB) * block + mine * SUB + lax.rem(index, SUB)).astype(F32)
        chosen = jnp.concatenate(
            [jnp.where(place == held[0, t, rows : rows + 1], 1.0, 0.0).astype(BF16) for t in range(n_f)],
            axis=1,
        )
        hits = jnp.dot(chosen, marks[...], preferred_element_type=F32)
        for i in range(n_o):
            hits_out[i] = hits[i * SUB : (i + 1) * SUB]
        send_orient(2, lambda peer: hits_out.at[peer], hits_in.at[o])
        hits_in[o] = hits_out[o]

    def expand(t, many):
        at = pl.ds(t * pair if many > 1 else pl.multiple_of(t * pair, pair), many * pair)
        found = jnp.dot(gather_from[at, :], spread[...], preferred_element_type=F32)
        found = found[:, :TILE] + found[:, TILE:]
        values = []
        for i in range(many):
            shift = shifts[t + i]
            value = jnp.where(
                lane >= shift,
                found[i * pair : i * pair + rows],
                found[i * pair + rows : (i + 1) * pair],
            )
            for k in range(7):
                value = jnp.where(
                    (shift & (1 << k)) != 0, pltpu.roll(value, TILE - (1 << k), 1), value
                )
            values.append(value)
        return values

    def iteration(turn, c):
        def take_logs(t, total):
            value = held[turn, t, 0:rows]
            at = pl.ds(pl.multiple_of(t * TILE, TILE), TILE)
            high, mid, low = split3(jnp.log(value + BACKGROUND))
            logs[0:rows, at] = high
            logs[rows : 2 * rows, at] = mid
            logs[2 * rows : 3 * rows, at] = low
            return total + value

        total = lax.fori_loop(0, n_f, take_logs, jnp.zeros((rows, TILE), F32))
        total = jnp.sum(total, axis=1, keepdims=True)
        like = jnp.dot(logs[...], count_high_t[...], preferred_element_type=F32) + jnp.dot(
            logs[...], count_low_t[...], preferred_element_type=F32
        )
        like = like[:rows] + like[rows : 2 * rows] + like[2 * rows :]
        score = SHARPNESS * (like - total * fluence_ref[...])
        top = jnp.max(score, axis=0, keepdims=True)
        expo = jnp.exp(score - top)
        norm = jnp.sum(expo, axis=0, keepdims=True)
        own = stats.at[turn, o]
        for k in range(chunks):
            own[k : k + 1, :] = top[:, k * TILE : (k + 1) * TILE]
            own[chunks + k : chunks + k + 1, :] = norm[:, k * TILE : (k + 1) * TILE]
        send_orient(3 + turn, lambda peer: stats.at[turn, o], stats.at[turn, o])

        @pl.when(turn == 0)
        def _():
            by_twos(prepare_to)
            count_hits()

        received(3 + turn, stats.at[turn, pl.ds(0, n_o - 1)])
        peak = stats[turn, 0, 0:chunks, :]
        for i in range(1, n_o):
            peak = jnp.maximum(peak, stats[turn, i, 0:chunks, :])
        whole = jnp.zeros((chunks, TILE), F32)
        for i in range(n_o):
            whole = whole + stats[turn, i, chunks : 2 * chunks, :] * jnp.exp(
                stats[turn, i, 0:chunks, :] - peak
            )
        factor = jnp.exp(stats[turn, o, 0:chunks, :] - peak) / whole
        factor = jnp.concatenate([factor[k : k + 1, :] for k in range(chunks)], axis=1)
        prob = expo * factor
        den = jnp.sum(prob * fluence_ref[...], axis=1, keepdims=True)
        dens[turn, f] = jnp.sum(jnp.where(diagonal, den, 0.0), axis=0, keepdims=True)
        send_frame(5 + turn, lambda peer: dens.at[turn, f], dens.at[turn, f])

        probs = jnp.concatenate(split2(prob), axis=0)
        num = jnp.dot(probs, count_high[...], preferred_element_type=F32) + jnp.dot(
            probs, count_low[...], preferred_element_type=F32
        )
        num = num[:rows] + num[rows:]
        for t in range(n_f):
            value = num[:, t * TILE : (t + 1) * TILE] + jnp.where(f == t, held[turn, t, 0:rows], 0.0)
            shift = shifts[t]
            for k in range(7):
                value = jnp.where((shift & (1 << k)) != 0, pltpu.roll(value, 1 << k, 1), value)
            moved[t] = value

        @pl.when(turn == 0)
        def _():
            by_twos(prepare_from)

        received(5 + turn, dens.at[turn, pl.ds(0, n_f - 1)])
        weight = dens[turn, 0]
        for i in range(1, n_f):
            weight = weight + dens[turn, i]
        weight = jnp.sum(jnp.where(diagonal, weight, 0.0), axis=1, keepdims=True)
        inverse = 1.0 / (weight + 1.0)
        for t in range(n_f):
            high, low = split2(moved[t] * inverse)
            first = lane >= shifts[t]
            none = jnp.zeros((rows, TILE), BF16)
            at = t * pair
            tiles[at : at + rows, :TILE] = jnp.where(first, high, none)
            tiles[at : at + rows, TILE:] = jnp.where(first, low, none)
            tiles[at + rows : at + pair, :TILE] = jnp.where(first, none, high)
            tiles[at + rows : at + pair, TILE:] = jnp.where(first, none, low)

        groups = min(4, n_o)
        group = n_o // groups

        def product(g):
            here = slice(g * group * block, (g + 1) * group * block)
            part = jnp.dot(gather_to[here, :], tiles[...], preferred_element_type=F32)
            part = (part[:, :TILE] + part[:, TILE:]).reshape(group, 2, half, SUB, TILE)
            for j in range(group):
                i = g * group + j
                for side in range(2):
                    part_out[turn, side, i] = part[j, side]
                deliver(
                    part_out.at[turn, 1 - core, i],
                    pair_in.at[turn, i],
                    send_sem.at[13 + turn],
                    pair_recv.at[turn, i],
                    (o, sibling),
                ).start()

        def release(g):
            for i in range(g * group, (g + 1) * group):
                into = pair_recv.at[turn, i]
                got = pair_in.at[turn, i]
                deliver(got, got, send_sem.at[13 + turn], into, (o, sibling)).wait_recv()
                paired[turn, i] = part_out[turn, core, i] + pair_in[turn, i]
                for k in same_core:
                    if (i, k) != (here_o, here_f):
                        deliver(
                            paired.at[turn, i, chips[k]],
                            part_in.at[turn, o * half + chip],
                            send_sem.at[7 + turn],
                            recv_sem.at[7 + turn],
                            (peers_o[i], peers_f[k]),
                        ).start()

        for g in range(groups):
            product(g)
            if g >= 2:
                release(g - 2)
        for g in range(max(0, groups - 2), groups):
            release(g)
        part_in[turn, o * half + chip] = paired[turn, n_o - 1, chip]

        @pl.when(turn == 0)
        def _():
            received(2, hits_in.at[pl.ds(0, n_o - 1)])

        hits = jnp.sum(hits_in[...], axis=0)
        received(7 + turn, part_in.at[turn, pl.ds(0, n // 2 - 1)])
        brick = jnp.sum(part_in[turn], axis=0) / jnp.maximum(hits, 1.0)
        out_ref[...] = brick
        slot = o * n_f + mine
        volume[turn, slot] = brick

        for i, k in others:
            brick_at = volume.at[turn, slot]
            into = wide_recv.at[turn, o * half + chip]
            deliver(
                brick_at, brick_at, send_sem.at[9 + turn], into, (peers_o[i], peers_f[k])
            ).start()
            if hops(i, k) >= far:
                across = (peers_o[i], chips[k] * 2 + 1 - core)
                deliver(
                    brick_at, brick_at, send_sem.at[9 + turn], wide_pass.at[turn], across
                ).start()

        def pass_on(at):
            brick_at = volume.at[turn, at]
            deliver(
                brick_at, brick_at, send_sem.at[11 + turn], wide_pass.at[turn], (o, sibling)
            ).start()

        pass_on(slot)
        for i, k in reversed(others):
            at = peers_o[i] * n_f + core * half + chips[k]
            into = wide_recv.at[turn, peers_o[i] * half + chips[k]]
            brick_at = volume.at[turn, at]
            deliver(brick_at, brick_at, send_sem.at[9 + turn], into, (o, sibling)).wait_recv()
            if hops(i, k) < far:
                pass_on(at)
        bricks = volume.at[turn, pl.ds(0, n_o * half)]
        deliver(
            bricks, bricks, send_sem.at[11 + turn], wide_pass.at[turn], (o, sibling)
        ).wait_recv()
        high, low = split2(volume[turn].reshape(places, TILE))
        spread[:, :TILE] = high
        spread[:, TILE:] = low

        @pl.when(turn < ITERS - 1)
        def _():
            for t in range(0, n_f, 4):
                for k, value in enumerate(expand(t, 4)):
                    held[turn + 1, t + k, 0:rows] = value

        return c

    lax.fori_loop(0, ITERS, iteration, 0)
    new_ref[...] = expand(f, 1)[0]

    sent(0, held.at[0, pl.ds(0, half - 1)])
    sent(1, held.at[0, pl.ds(0, half)])
    sent(2, hits_out.at[pl.ds(0, n_o - 1)])
    for turn in range(ITERS):
        sent(3 + turn, stats.at[turn, pl.ds(0, n_o - 1)])
        sent(5 + turn, dens.at[turn, pl.ds(0, n_f - 1)])
        sent(7 + turn, part_in.at[turn, pl.ds(0, n // 2 - 1)])
        double = sum(hops(*d) >= far for d in others)
        sent(9 + turn, volume.at[turn, pl.ds(0, n_o * half - 1 + double)])
        sent(13 + turn, pair_in.at[turn])
        sent(11 + turn, volume.at[turn, pl.ds(0, n_o * half - double)])


def hand_over(new_ref, brick_ref, new_out, brick_out):
    new_out[...] = new_ref[...]
    brick_out[...] = brick_ref[...]


def on_device(n_o, n_f, slices, counts, fluence, tile_brick, tile_base):
    rows = slices.shape[0]
    frames, pixels = counts.shape
    pair = 2 * rows
    block = n_f * SUB
    places = n_o * block
    vmem = pl.BlockSpec(memory_space=pltpu.VMEM)
    shapes = (
        jax.ShapeDtypeStruct((rows, TILE), F32),
        jax.ShapeDtypeStruct((SUB, TILE), F32),
    )
    both = pl.pallas_call(
        functools.partial(kernel, n_o, n_f),
        out_shape=shapes,
        in_specs=[vmem, vmem, vmem, vmem, pl.BlockSpec(memory_space=pl.ANY)],
        out_specs=(vmem, vmem),
        scratch_shapes=[
            pltpu.VMEM((frames, pixels), F32),
            pltpu.VMEM((frames, pixels), BF16),
            pltpu.VMEM((frames, pixels), BF16),
            pltpu.VMEM((pixels, frames), BF16),
            pltpu.VMEM((pixels, frames), BF16),
            pltpu.VMEM((ITERS, n_f, rows + SUB, TILE), F32),
            pltpu.VMEM((ITERS, n_o, 2 * (frames // TILE), TILE), F32),
            pltpu.VMEM((ITERS, n_f, 1, TILE), F32),
            pltpu.VMEM((places, n_f * pair), BF16),
            pltpu.VMEM((n_f * pair, places), BF16),
            pltpu.VMEM((n_f, rows, TILE), jnp.int32),
            pltpu.VMEM((n_f, rows, TILE), F32),
            pltpu.VMEM((n_f * pair, 2 * TILE), BF16),
            pltpu.VMEM((n_f * pair, TILE), BF16),
            pltpu.VMEM((3 * rows, pixels), BF16),
            pltpu.VMEM((ITERS, 2, n_o, n_f // 2, SUB, TILE), F32),
            pltpu.VMEM((ITERS, n_o, n_f // 2, SUB, TILE), F32),
            pltpu.VMEM((ITERS, n_o, n_f // 2, SUB, TILE), F32),
            pltpu.VMEM((ITERS, n_o * n_f // 2, SUB, TILE), F32),
            pltpu.VMEM((ITERS, n_o * n_f, SUB, TILE), F32),
            pltpu.VMEM((places, 2 * TILE), BF16),
            pltpu.VMEM((n_o, SUB, TILE), F32),
            pltpu.VMEM((n_o, SUB, TILE), F32),
            pltpu.SemaphoreType.DMA((LOAD,)),
            pltpu.SemaphoreType.DMA((3 + 6 * ITERS,)),
            pltpu.SemaphoreType.DMA((3 + 6 * ITERS,)),
            pltpu.SemaphoreType.DMA((n_f // 2,)),
            pltpu.SemaphoreType.DMA((n_f // 2,)),
            pltpu.SemaphoreType.DMA((ITERS, n_o)),
            pltpu.SemaphoreType.DMA((ITERS, n_o * n_f // 2)),
            pltpu.SemaphoreType.DMA((ITERS,)),
        ],
        compiler_params=pltpu.CompilerParams(
            collective_id=0, has_side_effects=True, vmem_limit_bytes=60 << 20
        ),
    )(slices, tile_brick[:, :, 0], tile_base, fluence[None, :], counts)
    new, brick = pl.pallas_call(
        hand_over,
        out_shape=shapes,
        in_specs=[vmem, vmem],
        out_specs=(vmem, vmem),
    )(*both)
    return new, brick.reshape(1, SUB * TILE)


def solution(mesh):
    n_o, n_f = mesh.shape["orient"], mesh.shape["frame"]
    in_specs = (
        P("orient", "frame"),
        P("frame", None),
        P("frame"),
        P("frame", "orient", None),
        P("frame", "orient"),
    )
    out_specs = (P("orient", "frame"), P(("orient", "frame"), None))
    return jax.shard_map(
        functools.partial(on_device, n_o, n_f),
        mesh=mesh,
        in_specs=in_specs,
        out_specs=out_specs,
        check_vma=False,
    )
```

```python
import functools

import jax
import jax.numpy as jnp
from jax import lax
from jax.experimental import pallas as pl
from jax.experimental.pallas import tpu as pltpu
from jax.sharding import PartitionSpec as P

VOX = 1024
TILE = 128
SUB = VOX // TILE
ITERS = 2
BACKGROUND = 0.1
SHARPNESS = 0.02
MESH = pl.DeviceIdType.MESH
F32 = jnp.float32
BF16 = jnp.bfloat16
LOAD = 4


def split2(x):
    high = x.astype(BF16)
    return high, (x - high.astype(F32)).astype(BF16)


def split3(x):
    high = x.astype(BF16)
    rest = x - high.astype(F32)
    mid = rest.astype(BF16)
    return high, mid, (rest - mid.astype(F32)).astype(BF16)


def iota(shape, axis):
    return lax.broadcasted_iota(jnp.int32, shape, axis)


def kernel(
    n_o,
    n_f,
    slices_ref,
    brick_ref,
    base_ref,
    fluence_from,
    counts_ref,
    new_ref,
    out_ref,
    brick_here,
    base_here,
    fluence_ref,
    totals,
    raw,
    count_high,
    count_low,
    count_high_t,
    count_low_t,
    held,
    stats,
    dens,
    gather_to,
    gather_from,
    shifts,
    moved,
    tiles,
    marks,
    logs,
    part_out,
    pair_in,
    paired,
    part_in,
    volume,
    spread,
    hits_out,
    hits_in,
    load_sem,
    send_sem,
    recv_sem,
    first_recv,
    first_pass,
    pair_recv,
    wide_recv,
    wide_pass,
):
    o = lax.axis_index("orient")
    f = lax.axis_index("frame")
    n = n_o * n_f
    me = o * n_f + f
    rows = slices_ref.shape[0]
    frames = counts_ref.shape[0]
    pair = 2 * rows
    block = n_f * SUB
    places = n_o * block
    chunks = frames // TILE
    half = n_f // 2
    ring = n_f // 4
    core = lax.rem(f, 2)
    chip = lax.div(f, 2)
    sibling = f + 1 - 2 * core
    mine = core * half + chip
    lane = iota((rows, TILE), 1)

    def near(d, size):
        return min(d, size - d)

    depth = n_o // 2
    turns_o = sorted(
        ((z, y) for z in range(depth) for y in range(2)), key=lambda d: -near(d[0], depth) - d[1]
    )
    turns_f = sorted(
        ((x, y, c) for x in range(ring) for y in range(2) for c in range(2)),
        key=lambda d: -(4 * near(d[0], ring) + 8 * d[1] + d[2]),
    )
    at_z, at_y = lax.div(o, 2), lax.rem(o, 2)
    peers_o = [lax.rem(at_z + z, depth) * 2 + lax.rem(at_y + y, 2) for z, y in turns_o]
    chip_x, chip_y = lax.div(chip, 2), lax.rem(chip, 2)
    chips = [
        lax.rem(chip_x + x, ring) * 2 + lax.rem(chip_y + y, 2) for x, y, c in turns_f
    ]
    sides = [lax.rem(core + c, 2) for x, y, c in turns_f]
    peers_f = [at * 2 + side for at, side in zip(chips, sides)]
    here_o, here_f = turns_o.index((0, 0)), turns_f.index((0, 0, 0))
    same_core = [k for k in range(n_f) if turns_f[k][2] == 0]

    def hops(i, k):
        (z, low), (x, high, c) = turns_o[i], turns_f[k]
        return near(z, depth) + near(x, ring) + ((0, 1), (2, 1))[high][low]

    pairs = sorted(
        ((i, k) for i in range(n_o) for k in same_core), key=lambda d: -hops(*d)
    )
    far = hops(*pairs[0]) - 1
    others = [d for d in pairs if d != (here_o, here_f)]

    def is_peer(i, k):
        if (i, k) == (here_o, here_f):
            return False
        return k in same_core or i == here_o or hops(i, k) >= far

    step = frames // LOAD
    small = [
        pltpu.make_async_copy(src, dst, load_sem.at[LOAD + i])
        for i, (src, dst) in enumerate(
            [
                (brick_ref, brick_here),
                (base_ref, base_here),
                (fluence_from, fluence_ref),
                (slices_ref, held.at[0, f, pl.ds(0, rows)]),
            ]
        )
    ]
    for one in small:
        one.start()
    barrier = pltpu.get_barrier_semaphore()
    peers = [(i, k) for i in range(n_o) for k in range(n_f) if is_peer(i, k)]
    for i, k in sorted(peers, key=lambda d: -hops(*d)):
        pl.semaphore_signal(
            barrier, inc=1, device_id=(peers_o[i], peers_f[k]), device_id_type=MESH
        )

    for i in range(LOAD):
        pltpu.make_async_copy(
            counts_ref.at[pl.ds(i * step, step)], raw.at[pl.ds(i * step, step)], load_sem.at[i]
        ).start()
    for one in small:
        one.wait()

    named = brick_here[...]
    inside = lax.rem(named, n_f)
    place = (
        lax.div(named, n_f) * block
        + (lax.rem(inside, 2) * half + lax.div(inside, 2)) * SUB
        + lax.div(base_here[...], TILE)
    )
    shift = lax.rem(base_here[...], TILE)
    held[0, f, rows : rows + 1] = jnp.concatenate([place, place + 1], axis=1).astype(F32)
    held[0, f, rows + 1 : rows + 2] = jnp.concatenate([shift, shift], axis=1).astype(F32)
    held[0, f, rows + 2 : rows + SUB] = jnp.zeros((SUB - 2, TILE), F32)

    def load(i):
        here = pl.ds(i * step, step)
        pltpu.make_async_copy(counts_ref.at[here], raw.at[here], load_sem.at[i]).wait()

        def convert(j, c):
            at = pl.ds(pl.multiple_of(j * TILE, TILE), TILE)
            high, low = split2(raw[here, at])
            count_high[here, at] = high
            count_low[here, at] = low
            return c

        lax.fori_loop(0, n_f, convert, 0)

    for i in range(LOAD):
        load(i)
    pl.semaphore_wait(barrier, len(peers))

    def copy(which, turn, src, dst, to):
        return pltpu.make_async_remote_copy(
            src_ref=src,
            dst_ref=dst,
            send_sem=send_sem.at[which],
            recv_sem=recv_sem.at[which, turn],
            device_id=to,
            device_id_type=MESH,
        )

    def send_frame(which, turn, src, dst):
        def body(j, c):
            peer = lax.rem(f + j, n_f)
            copy(which, turn, src(peer), dst, (o, peer)).start()
            return c

        lax.fori_loop(1, n_f, body, 0)

    def send_orient(which, turn, src, dst):
        def body(j, c):
            peer = lax.rem(o + j, n_o)
            copy(which, turn, src(peer), dst, (peer, f)).start()
            return c

        lax.fori_loop(1, n_o, body, 0)

    def received(which, turn, whole):
        copy(which, turn, whole, whole, (lax.rem(o + 1, n_o), f)).wait_recv()

    def sent(which, whole):
        copy(which, 0, whole, whole, (lax.rem(o + 1, n_o), f)).wait_send()

    def deliver(src, dst, out, into, to):
        return pltpu.make_async_remote_copy(
            src_ref=src,
            dst_ref=dst,
            send_sem=out,
            recv_sem=into,
            device_id=to,
            device_id_type=MESH,
        )

    def pass_first(at, distance):
        packet = held.at[0, at * 2 + core]
        deliver(packet, packet, send_sem.at[1], first_pass.at[distance], (o, sibling)).start()

    def take(t, value):
        at = pl.ds(t * TILE if isinstance(t, int) else pl.multiple_of(t * TILE, TILE), TILE)
        high, mid, low = split3(jnp.log(value + BACKGROUND))
        logs[0:rows, at] = high
        logs[rows : 2 * rows, at] = mid
        logs[2 * rows : 3 * rows, at] = low
        return value

    away = sorted(
        (k for k in same_core if k != here_f), key=lambda k: -hops(here_o, k)
    )
    edge = hops(here_o, away[0])
    packet = held.at[0, f]
    for k in away:
        deliver(packet, packet, send_sem.at[0], first_recv.at[hops(here_o, k)], (o, peers_f[k])).start()
        if hops(here_o, k) == edge:
            across = (o, chips[k] * 2 + 1 - core)
            deliver(packet, packet, send_sem.at[0], first_pass.at[edge], across).start()
    pass_first(chip, 0)
    def turn_over(j, c):
        at = pl.ds(pl.multiple_of(j * TILE, TILE), TILE)
        count_high_t[at, :] = count_high[:, at].T
        count_low_t[at, :] = count_low[:, at].T
        return c

    lax.fori_loop(0, n_f, turn_over, 0)

    for distance in range(1, edge + 1):
        ring_of = [k for k in away if hops(here_o, k) == distance]
        if ring_of:
            some = held.at[0, pl.ds(0, len(ring_of))]
            into = first_recv.at[distance]
            deliver(some, some, send_sem.at[0], into, (o, sibling)).wait_recv()
        if distance < edge:
            for k in ring_of:
                pass_first(chips[k], distance)
    total = take(f, held[0, f, 0:rows])
    for k in reversed(away):
        total = total + take(peers_f[k], held[0, peers_f[k], 0:rows])
    for distance in range(edge + 1):
        ring_of = [k for k in same_core if hops(here_o, k) == distance]
        if ring_of:
            some = held.at[0, pl.ds(0, len(ring_of))]
            into = first_pass.at[distance]
            deliver(some, some, send_sem.at[1], into, (o, sibling)).wait_recv()
        for k in ring_of:
            at = chips[k] * 2 + 1 - core
            total = total + take(at, held[0, at, 0:rows])
    totals[...] = total
    diagonal = iota((rows, TILE), 0) == lane
    eye = iota((pair, pair), 0) == iota((pair, pair), 1)

    def prepare_to(t):
        row = held[0, t, rows : rows + 1]
        at = pl.ds(pl.multiple_of(t * pair, pair), pair)
        for i in range(n_o):
            place = (iota((block, pair), 0) + peers_o[i] * block).astype(F32)
            gather_to[i * block : (i + 1) * block, at] = jnp.where(
                place == row, 1.0, 0.0
            ).astype(BF16)
        shift = jnp.sum(
            jnp.where(eye, held[0, t, rows + 1 : rows + 2], 0.0), axis=1, keepdims=True
        )
        shift = jnp.broadcast_to(shift[0:rows], (rows, TILE)).astype(jnp.int32)
        shifts[t] = shift
        mark = jnp.where(lane >= shift, 1.0, 0.0)
        marks[at, :] = jnp.concatenate([mark, 1.0 - mark], axis=0).astype(BF16)

    def prepare_from(t):
        row = held[0, t, rows : rows + 1]
        at = pl.ds(pl.multiple_of(t * pair, pair), pair)
        column = jnp.sum(jnp.where(eye, row, 0.0), axis=1, keepdims=True)
        place = iota((pair, places), 1).astype(F32)
        gather_from[at, :] = jnp.where(place == column, 1.0, 0.0).astype(BF16)

    def by_twos(work):
        def body(t, c):
            work(t * 2)
            work(t * 2 + 1)
            return c

        lax.fori_loop(0, n_f // 2, body, 0)

    def count_hits():
        index = iota((n_o * SUB, pair), 0)
        place = (lax.div(index, SUB) * block + mine * SUB + lax.rem(index, SUB)).astype(F32)
        chosen = jnp.concatenate(
            [jnp.where(place == held[0, t, rows : rows + 1], 1.0, 0.0).astype(BF16) for t in range(n_f)],
            axis=1,
        )
        hits = jnp.dot(chosen, marks[...], preferred_element_type=F32)
        for i in range(n_o):
            hits_out[i] = hits[i * SUB : (i + 1) * SUB]
        send_orient(2, 0, lambda peer: hits_out.at[peer], hits_in.at[o])
        hits_in[o] = hits_out[o]

    def expand(t, many):
        at = pl.ds(t * pair if many > 1 else pl.multiple_of(t * pair, pair), many * pair)
        found = jnp.dot(gather_from[at, :], spread[...], preferred_element_type=F32)
        found = found[:, :TILE] + found[:, TILE:]
        values = []
        for i in range(many):
            shift = shifts[t + i]
            value = jnp.where(
                lane >= shift,
                found[i * pair : i * pair + rows],
                found[i * pair + rows : (i + 1) * pair],
            )
            for k in range(7):
                value = jnp.where(
                    (shift & (1 << k)) != 0, pltpu.roll(value, TILE - (1 << k), 1), value
                )
            values.append(value)
        return values

    def iteration(turn, c):
        total = jnp.sum(totals[...], axis=1, keepdims=True)
        like = jnp.dot(logs[...], count_high_t[...], preferred_element_type=F32) + jnp.dot(
            logs[...], count_low_t[...], preferred_element_type=F32
        )
        like = like[:rows] + like[rows : 2 * rows] + like[2 * rows :]
        score = SHARPNESS * (like - total * fluence_ref[...])
        top = jnp.max(score, axis=0, keepdims=True)
        expo = jnp.exp(score - top)
        norm = jnp.sum(expo, axis=0, keepdims=True)
        own = stats.at[turn, o]
        for k in range(chunks):
            own[k : k + 1, :] = top[:, k * TILE : (k + 1) * TILE]
            own[chunks + k : chunks + k + 1, :] = norm[:, k * TILE : (k + 1) * TILE]
        send_orient(3, turn, lambda peer: stats.at[turn, o], stats.at[turn, o])

        @pl.when(turn == 0)
        def _():
            by_twos(prepare_to)
            count_hits()

        received(3, turn, stats.at[turn, pl.ds(0, n_o - 1)])
        peak = stats[turn, 0, 0:chunks, :]
        for i in range(1, n_o):
            peak = jnp.maximum(peak, stats[turn, i, 0:chunks, :])
        whole = jnp.zeros((chunks, TILE), F32)
        for i in range(n_o):
            whole = whole + stats[turn, i, chunks : 2 * chunks, :] * jnp.exp(
                stats[turn, i, 0:chunks, :] - peak
            )
        factor = jnp.exp(stats[turn, o, 0:chunks, :] - peak) / whole
        factor = jnp.concatenate([factor[k : k + 1, :] for k in range(chunks)], axis=1)
        prob = expo * factor
        den = jnp.sum(prob * fluence_ref[...], axis=1, keepdims=True)
        dens[turn, f] = jnp.sum(jnp.where(diagonal, den, 0.0), axis=0, keepdims=True)
        send_frame(4, turn, lambda peer: dens.at[turn, f], dens.at[turn, f])

        probs = jnp.concatenate(split2(prob), axis=0)
        num = jnp.dot(probs, count_high[...], preferred_element_type=F32) + jnp.dot(
            probs, count_low[...], preferred_element_type=F32
        )
        num = num[:rows] + num[rows:]
        for t in range(n_f):
            value = num[:, t * TILE : (t + 1) * TILE] + jnp.where(f == t, held[turn, t, 0:rows], 0.0)
            shift = shifts[t]
            for k in range(7):
                value = jnp.where((shift & (1 << k)) != 0, pltpu.roll(value, 1 << k, 1), value)
            moved[t] = value

        @pl.when(turn == 0)
        def _():
            by_twos(prepare_from)

        received(4, turn, dens.at[turn, pl.ds(0, n_f - 1)])
        weight = dens[turn, 0]
        for i in range(1, n_f):
            weight = weight + dens[turn, i]
        weight = jnp.sum(jnp.where(diagonal, weight, 0.0), axis=1, keepdims=True)
        inverse = 1.0 / (weight + 1.0)
        for t in range(n_f):
            high, low = split2(moved[t] * inverse)
            first = lane >= shifts[t]
            none = jnp.zeros((rows, TILE), BF16)
            at = t * pair
            tiles[at : at + rows, :TILE] = jnp.where(first, high, none)
            tiles[at : at + rows, TILE:] = jnp.where(first, low, none)
            tiles[at + rows : at + pair, :TILE] = jnp.where(first, none, high)
            tiles[at + rows : at + pair, TILE:] = jnp.where(first, none, low)

        groups = min(4, n_o)
        group = n_o // groups

        def product(g):
            here = slice(g * group * block, (g + 1) * group * block)
            part = jnp.dot(gather_to[here, :], tiles[...], preferred_element_type=F32)
            part = (part[:, :TILE] + part[:, TILE:]).reshape(group, 2, half, SUB, TILE)
            for j in range(group):
                i = g * group + j
                for side in range(2):
                    part_out[turn, side, i] = part[j, side]
                deliver(
                    part_out.at[turn, 1 - core, i],
                    pair_in.at[turn, i],
                    send_sem.at[8],
                    pair_recv.at[turn, g],
                    (o, sibling),
                ).start()

        def release(g):
            got = pair_in.at[turn, pl.ds(g * group, group)]
            into = pair_recv.at[turn, g]
            deliver(got, got, send_sem.at[8], into, (o, sibling)).wait_recv()
            for i in range(g * group, (g + 1) * group):
                paired[turn, i] = part_out[turn, core, i] + pair_in[turn, i]
                for k in same_core:
                    if (i, k) != (here_o, here_f):
                        deliver(
                            paired.at[turn, i, chips[k]],
                            part_in.at[turn, o * half + chip],
                            send_sem.at[5],
                            recv_sem.at[5, turn],
                            (peers_o[i], peers_f[k]),
                        ).start()

        for g in range(groups):
            product(g)
            if g >= 2:
                release(g - 2)
        for g in range(max(0, groups - 2), groups):
            release(g)
        part_in[turn, o * half + chip] = paired[turn, n_o - 1, chip]

        @pl.when(turn == 0)
        def _():
            received(2, 0, hits_in.at[pl.ds(0, n_o - 1)])

        hits = jnp.sum(hits_in[...], axis=0)
        received(5, turn, part_in.at[turn, pl.ds(0, n // 2 - 1)])
        brick = jnp.sum(part_in[turn], axis=0) / jnp.maximum(hits, 1.0)
        out_ref[...] = brick
        slot = o * n_f + mine
        volume[turn, slot] = brick

        for i, k in others:
            brick_at = volume.at[turn, slot]
            into = wide_recv.at[turn, hops(i, k)]
            deliver(
                brick_at, brick_at, send_sem.at[6], into, (peers_o[i], peers_f[k])
            ).start()
            if hops(i, k) >= far:
                across = (peers_o[i], chips[k] * 2 + 1 - core)
                deliver(
                    brick_at, brick_at, send_sem.at[6], wide_pass.at[turn], across
                ).start()

        def pass_on(at):
            brick_at = volume.at[turn, at]
            deliver(
                brick_at, brick_at, send_sem.at[7], wide_pass.at[turn], (o, sibling)
            ).start()

        pass_on(slot)
        for distance in range(1, far + 2):
            ring_of = [d for d in others if hops(*d) == distance]
            if ring_of:
                some = volume.at[turn, pl.ds(0, len(ring_of))]
                into = wide_recv.at[turn, distance]
                deliver(some, some, send_sem.at[6], into, (o, sibling)).wait_recv()
            if distance < far:
                for i, k in ring_of:
                    pass_on(peers_o[i] * n_f + core * half + chips[k])
        bricks = volume.at[turn, pl.ds(0, n_o * half)]
        deliver(
            bricks, bricks, send_sem.at[7], wide_pass.at[turn], (o, sibling)
        ).wait_recv()
        high, low = split2(volume[turn].reshape(places, TILE))
        spread[:, :TILE] = high
        spread[:, TILE:] = low

        @pl.when(turn < ITERS - 1)
        def _():
            total = jnp.zeros((rows, TILE), F32)
            for t in range(0, n_f, 4):
                for k, value in enumerate(expand(t, 4)):
                    held[turn + 1, t + k, 0:rows] = value
                    total = total + take(t + k, value)
            totals[...] = total

        return c

    lax.fori_loop(0, ITERS, iteration, 0)
    new_ref[...] = expand(f, 1)[0]

    edges = sum(hops(here_o, k) == edge for k in away)
    sent(0, held.at[0, pl.ds(0, half - 1 + edges)])
    sent(1, held.at[0, pl.ds(0, half - edges)])
    sent(2, hits_out.at[pl.ds(0, n_o - 1)])
    double = sum(hops(*d) >= far for d in others)
    sent(3, stats.at[:, pl.ds(0, n_o - 1)])
    sent(4, dens.at[:, pl.ds(0, n_f - 1)])
    sent(5, part_in.at[:, pl.ds(0, n // 2 - 1)])
    sent(6, volume.at[:, pl.ds(0, n_o * half - 1 + double)])
    sent(7, volume.at[:, pl.ds(0, n_o * half - double)])
    sent(8, pair_in)


def on_device(n_o, n_f, slices, counts, fluence, tile_brick, tile_base):
    rows = slices.shape[0]
    frames, pixels = counts.shape
    pair = 2 * rows
    block = n_f * SUB
    places = n_o * block
    vmem = pl.BlockSpec(memory_space=pltpu.VMEM)
    new, brick = pl.pallas_call(
        functools.partial(kernel, n_o, n_f),
        out_shape=(pltpu.VMEM((rows, TILE), F32), pltpu.VMEM((SUB, TILE), F32)),
        in_specs=[pl.BlockSpec(memory_space=pl.ANY)] * 5,
        out_specs=(vmem, vmem),
        scratch_shapes=[
            pltpu.VMEM((1, rows), jnp.int32),
            pltpu.VMEM((1, rows), jnp.int32),
            pltpu.VMEM((1, frames), F32),
            pltpu.VMEM((rows, TILE), F32),
            pltpu.VMEM((frames, pixels), F32),
            pltpu.VMEM((frames, pixels), BF16),
            pltpu.VMEM((frames, pixels), BF16),
            pltpu.VMEM((pixels, frames), BF16),
            pltpu.VMEM((pixels, frames), BF16),
            pltpu.VMEM((ITERS, n_f, rows + SUB, TILE), F32),
            pltpu.VMEM((ITERS, n_o, 2 * (frames // TILE), TILE), F32),
            pltpu.VMEM((ITERS, n_f, 1, TILE), F32),
            pltpu.VMEM((places, n_f * pair), BF16),
            pltpu.VMEM((n_f * pair, places), BF16),
            pltpu.VMEM((n_f, rows, TILE), jnp.int32),
            pltpu.VMEM((n_f, rows, TILE), F32),
            pltpu.VMEM((n_f * pair, 2 * TILE), BF16),
            pltpu.VMEM((n_f * pair, TILE), BF16),
            pltpu.VMEM((3 * rows, pixels), BF16),
            pltpu.VMEM((ITERS, 2, n_o, n_f // 2, SUB, TILE), F32),
            pltpu.VMEM((ITERS, n_o, n_f // 2, SUB, TILE), F32),
            pltpu.VMEM((ITERS, n_o, n_f // 2, SUB, TILE), F32),
            pltpu.VMEM((ITERS, n_o * n_f // 2, SUB, TILE), F32),
            pltpu.VMEM((ITERS, n_o * n_f, SUB, TILE), F32),
            pltpu.VMEM((places, 2 * TILE), BF16),
            pltpu.VMEM((n_o, SUB, TILE), F32),
            pltpu.VMEM((n_o, SUB, TILE), F32),
            pltpu.SemaphoreType.DMA((LOAD + 4,)),
            pltpu.SemaphoreType.DMA((9,)),
            pltpu.SemaphoreType.DMA((6, ITERS)),
            pltpu.SemaphoreType.DMA((5,)),
            pltpu.SemaphoreType.DMA((5,)),
            pltpu.SemaphoreType.DMA((ITERS, 4)),
            pltpu.SemaphoreType.DMA((ITERS, 7)),
            pltpu.SemaphoreType.DMA((ITERS,)),
        ],
        compiler_params=pltpu.CompilerParams(
            collective_id=0, has_side_effects=True, vmem_limit_bytes=60 << 20
        ),
    )(slices, tile_brick[:, :, 0], tile_base, fluence[None, :], counts)
    return new, brick.reshape(1, SUB * TILE)


def solution(mesh):
    n_o, n_f = mesh.shape["orient"], mesh.shape["frame"]
    in_specs = (
        P("orient", "frame"),
        P("frame", None),
        P("frame"),
        P("frame", "orient", None),
        P("frame", "orient"),
    )
    out_specs = (P("orient", "frame"), P(("orient", "frame"), None))
    return jax.shard_map(
        functools.partial(on_device, n_o, n_f),
        mesh=mesh,
        in_specs=in_specs,
        out_specs=out_specs,
        check_vma=False,
    )
```

```python
import functools

import jax
import jax.numpy as jnp
from jax import lax
from jax.experimental import pallas as pl
from jax.experimental.pallas import tpu as pltpu
from jax.sharding import PartitionSpec as P

VOX = 1024
TILE = 128
SUB = VOX // TILE
ITERS = 2
BACKGROUND = 0.1
SHARPNESS = 0.02
MESH = pl.DeviceIdType.MESH
F32 = jnp.float32
BF16 = jnp.bfloat16
LOAD = 4
FAR = 7


def split2(x):
    high = x.astype(BF16)
    return high, (x - high.astype(F32)).astype(BF16)


def split3(x):
    high = x.astype(BF16)
    rest = x - high.astype(F32)
    mid = rest.astype(BF16)
    return high, mid, (rest - mid.astype(F32)).astype(BF16)


def iota(shape, axis):
    return lax.broadcasted_iota(jnp.int32, shape, axis)


def kernel(
    n_o,
    n_f,
    slices_ref,
    brick_ref,
    base_ref,
    fluence_from,
    counts_ref,
    new_ref,
    out_ref,
    brick_here,
    base_here,
    fluence_ref,
    totals,
    raw,
    count_high,
    count_low,
    count_high_t,
    count_low_t,
    held,
    stats,
    dens,
    where_to,
    gather_to,
    gather_from,
    shifts,
    moved,
    tiles,
    marks,
    logs,
    part_out,
    pair_in,
    paired,
    part_in,
    volume,
    spread,
    hits_out,
    hits_in,
    load_sem,
    send_sem,
    recv_sem,
    first_recv,
    first_pass,
    pair_recv,
    wide_recv,
    wide_pass,
):
    o = lax.axis_index("orient")
    f = lax.axis_index("frame")
    n = n_o * n_f
    me = o * n_f + f
    rows = slices_ref.shape[0]
    frames = counts_ref.shape[0]
    pair = 2 * rows
    block = n_f * SUB
    places = n_o * block
    chunks = frames // TILE
    half = n_f // 2
    ring = n_f // 4
    core = lax.rem(f, 2)
    chip = lax.div(f, 2)
    sibling = f + 1 - 2 * core
    mine = core * half + chip
    lane = iota((rows, TILE), 1)

    def near(d, size):
        return min(d, size - d)

    depth = n_o // 2
    turns_o = sorted(
        ((z, y) for z in range(depth) for y in range(2)), key=lambda d: -near(d[0], depth) - d[1]
    )
    turns_f = sorted(
        ((x, y, c) for x in range(ring) for y in range(2) for c in range(2)),
        key=lambda d: -(4 * near(d[0], ring) + 8 * d[1] + d[2]),
    )
    at_z, at_y = lax.div(o, 2), lax.rem(o, 2)
    peers_o = [lax.rem(at_z + z, depth) * 2 + lax.rem(at_y + y, 2) for z, y in turns_o]
    chip_x, chip_y = lax.div(chip, 2), lax.rem(chip, 2)
    chips = [
        lax.rem(chip_x + x, ring) * 2 + lax.rem(chip_y + y, 2) for x, y, c in turns_f
    ]
    sides = [lax.rem(core + c, 2) for x, y, c in turns_f]
    peers_f = [at * 2 + side for at, side in zip(chips, sides)]
    here_o, here_f = turns_o.index((0, 0)), turns_f.index((0, 0, 0))
    same_core = [k for k in range(n_f) if turns_f[k][2] == 0]

    def hops(i, k):
        (z, low), (x, high, c) = turns_o[i], turns_f[k]
        return near(z, depth) + near(x, ring) + ((0, 1), (2, 1))[high][low]

    pairs = sorted(
        ((i, k) for i in range(n_o) for k in same_core), key=lambda d: -hops(*d)
    )
    far = hops(*pairs[0]) - 1
    others = [d for d in pairs if d != (here_o, here_f)]

    far_pairs = [d for d in pairs if hops(*d) >= far]
    assert len(far_pairs) <= FAR
    groups = 4
    group = len(pairs) // groups

    def is_peer(i, k):
        if (i, k) == (here_o, here_f):
            return False
        return k in same_core or i == here_o or hops(i, k) >= far

    step = frames // LOAD
    small = [
        pltpu.make_async_copy(src, dst, load_sem.at[LOAD + i])
        for i, (src, dst) in enumerate(
            [
                (brick_ref, brick_here),
                (base_ref, base_here),
                (fluence_from, fluence_ref),
                (slices_ref, held.at[0, f, pl.ds(0, rows)]),
            ]
        )
    ]
    for one in small:
        one.start()
    barrier = pltpu.get_barrier_semaphore()
    peers = [(i, k) for i in range(n_o) for k in range(n_f) if is_peer(i, k)]
    for i, k in sorted(peers, key=lambda d: -hops(*d)):
        pl.semaphore_signal(
            barrier, inc=1, device_id=(peers_o[i], peers_f[k]), device_id_type=MESH
        )

    for i in range(LOAD):
        pltpu.make_async_copy(
            counts_ref.at[pl.ds(i * step, step)], raw.at[pl.ds(i * step, step)], load_sem.at[i]
        ).start()
    for one in small:
        one.wait()

    named = brick_here[...]
    inside = lax.rem(named, n_f)
    place = (
        lax.div(named, n_f) * block
        + (lax.rem(inside, 2) * half + lax.div(inside, 2)) * SUB
        + lax.div(base_here[...], TILE)
    )
    shift = lax.rem(base_here[...], TILE)
    held[0, f, rows : rows + 1] = jnp.concatenate([place, place + 1], axis=1).astype(F32)
    held[0, f, rows + 1 : rows + 2] = jnp.concatenate([shift, shift], axis=1).astype(F32)
    held[0, f, rows + 2 : rows + SUB] = jnp.zeros((SUB - 2, TILE), F32)

    for g in range(groups):
        for side in range(2):
            for j in range(group):
                i, k = pairs[g * group + j]
                own_side = core if side == 0 else 1 - core
                first = peers_o[i] * block + (own_side * half + chips[k]) * SUB
                at = ((g * 2 + side) * group + j) * SUB
                where_to[at : at + SUB, :] = (iota((SUB, pair), 0) + first).astype(F32)

    def load(i):
        here = pl.ds(i * step, step)
        pltpu.make_async_copy(counts_ref.at[here], raw.at[here], load_sem.at[i]).wait()

        def convert(j, c):
            at = pl.ds(pl.multiple_of(j * TILE, TILE), TILE)
            high, low = split2(raw[here, at])
            count_high[here, at] = high
            count_low[here, at] = low
            return c

        lax.fori_loop(0, n_f, convert, 0)

    for i in range(LOAD):
        load(i)
    pl.semaphore_wait(barrier, len(peers))

    def copy(which, turn, src, dst, to):
        return pltpu.make_async_remote_copy(
            src_ref=src,
            dst_ref=dst,
            send_sem=send_sem.at[which],
            recv_sem=recv_sem.at[which, turn],
            device_id=to,
            device_id_type=MESH,
        )

    def send_frame(which, turn, src, dst):
        def body(j, c):
            peer = lax.rem(f + j, n_f)
            copy(which, turn, src(peer), dst, (o, peer)).start()
            return c

        lax.fori_loop(1, n_f, body, 0)

    def send_orient(which, turn, src, dst):
        def body(j, c):
            peer = lax.rem(o + j, n_o)
            copy(which, turn, src(peer), dst, (peer, f)).start()
            return c

        lax.fori_loop(1, n_o, body, 0)

    def received(which, turn, whole):
        copy(which, turn, whole, whole, (lax.rem(o + 1, n_o), f)).wait_recv()

    def sent(which, whole):
        copy(which, 0, whole, whole, (lax.rem(o + 1, n_o), f)).wait_send()

    def deliver(src, dst, out, into, to):
        return pltpu.make_async_remote_copy(
            src_ref=src,
            dst_ref=dst,
            send_sem=out,
            recv_sem=into,
            device_id=to,
            device_id_type=MESH,
        )

    def pass_first(at, distance):
        packet = held.at[0, at * 2 + core]
        deliver(packet, packet, send_sem.at[1], first_pass.at[distance], (o, sibling)).start()

    def take(t, value):
        at = pl.ds(t * TILE if isinstance(t, int) else pl.multiple_of(t * TILE, TILE), TILE)
        high, mid, low = split3(jnp.log(value + BACKGROUND))
        logs[0:rows, at] = high
        logs[rows : 2 * rows, at] = mid
        logs[2 * rows : 3 * rows, at] = low
        return value

    away = sorted(
        (k for k in same_core if k != here_f), key=lambda k: -hops(here_o, k)
    )
    edge = hops(here_o, away[0])
    packet = held.at[0, f]
    for k in away:
        deliver(packet, packet, send_sem.at[0], first_recv.at[hops(here_o, k)], (o, peers_f[k])).start()
        if hops(here_o, k) == edge:
            across = (o, chips[k] * 2 + 1 - core)
            deliver(packet, packet, send_sem.at[0], first_pass.at[edge], across).start()
    pass_first(chip, 0)
    def turn_over(j, c):
        at = pl.ds(pl.multiple_of(j * TILE, TILE), TILE)
        count_high_t[at, :] = count_high[:, at].T
        count_low_t[at, :] = count_low[:, at].T
        return c

    lax.fori_loop(0, n_f, turn_over, 0)

    for distance in range(1, edge + 1):
        ring_of = [k for k in away if hops(here_o, k) == distance]
        if ring_of:
            some = held.at[0, pl.ds(0, len(ring_of))]
            into = first_recv.at[distance]
            deliver(some, some, send_sem.at[0], into, (o, sibling)).wait_recv()
        if distance < edge:
            for k in ring_of:
                pass_first(chips[k], distance)
    total = take(f, held[0, f, 0:rows])
    for k in reversed(away):
        total = total + take(peers_f[k], held[0, peers_f[k], 0:rows])
    for distance in range(edge + 1):
        ring_of = [k for k in same_core if hops(here_o, k) == distance]
        if ring_of:
            some = held.at[0, pl.ds(0, len(ring_of))]
            into = first_pass.at[distance]
            deliver(some, some, send_sem.at[1], into, (o, sibling)).wait_recv()
        for k in ring_of:
            at = chips[k] * 2 + 1 - core
            total = total + take(at, held[0, at, 0:rows])
    totals[...] = total
    diagonal = iota((rows, TILE), 0) == lane
    eye = iota((pair, pair), 0) == iota((pair, pair), 1)

    def prepare_to(t):
        row = held[0, t, rows : rows + 1]
        at = pl.ds(pl.multiple_of(t * pair, pair), pair)
        for i in range(n_o):
            place = where_to[i * block : (i + 1) * block, :]
            gather_to[i * block : (i + 1) * block, at] = jnp.where(
                place == row, 1.0, 0.0
            ).astype(BF16)
        shift = jnp.sum(
            jnp.where(eye, held[0, t, rows + 1 : rows + 2], 0.0), axis=1, keepdims=True
        )
        shift = jnp.broadcast_to(shift[0:rows], (rows, TILE)).astype(jnp.int32)
        shifts[t] = shift
        mark = jnp.where(lane >= shift, 1.0, 0.0)
        marks[at, :] = jnp.concatenate([mark, 1.0 - mark], axis=0).astype(BF16)

    def prepare_from(t):
        row = held[0, t, rows : rows + 1]
        at = pl.ds(pl.multiple_of(t * pair, pair), pair)
        column = jnp.sum(jnp.where(eye, row, 0.0), axis=1, keepdims=True)
        place = iota((pair, places), 1).astype(F32)
        gather_from[at, :] = jnp.where(place == column, 1.0, 0.0).astype(BF16)

    def by_twos(work):
        def body(t, c):
            work(t * 2)
            work(t * 2 + 1)
            return c

        lax.fori_loop(0, n_f // 2, body, 0)

    def count_hits():
        index = iota((n_o * SUB, pair), 0)
        place = (lax.div(index, SUB) * block + mine * SUB + lax.rem(index, SUB)).astype(F32)
        chosen = jnp.concatenate(
            [jnp.where(place == held[0, t, rows : rows + 1], 1.0, 0.0).astype(BF16) for t in range(n_f)],
            axis=1,
        )
        hits = jnp.dot(chosen, marks[...], preferred_element_type=F32)
        for i in range(n_o):
            hits_out[i] = hits[i * SUB : (i + 1) * SUB]
        send_orient(2, 0, lambda peer: hits_out.at[peer], hits_in.at[o])
        hits_in[o] = hits_out[o]

    def expand(t, many):
        at = pl.ds(t * pair if many > 1 else pl.multiple_of(t * pair, pair), many * pair)
        found = jnp.dot(gather_from[at, :], spread[...], preferred_element_type=F32)
        found = found[:, :TILE] + found[:, TILE:]
        values = []
        for i in range(many):
            shift = shifts[t + i]
            value = jnp.where(
                lane >= shift,
                found[i * pair : i * pair + rows],
                found[i * pair + rows : (i + 1) * pair],
            )
            for k in range(7):
                value = jnp.where(
                    (shift & (1 << k)) != 0, pltpu.roll(value, TILE - (1 << k), 1), value
                )
            values.append(value)
        return values

    def iteration(turn, c):
        total = jnp.sum(totals[...], axis=1, keepdims=True)
        like = jnp.dot(logs[...], count_high_t[...], preferred_element_type=F32) + jnp.dot(
            logs[...], count_low_t[...], preferred_element_type=F32
        )
        like = like[:rows] + like[rows : 2 * rows] + like[2 * rows :]
        score = SHARPNESS * (like - total * fluence_ref[...])
        top = jnp.max(score, axis=0, keepdims=True)
        expo = jnp.exp(score - top)
        norm = jnp.sum(expo, axis=0, keepdims=True)
        own = stats.at[turn, o]
        for k in range(chunks):
            own[k : k + 1, :] = top[:, k * TILE : (k + 1) * TILE]
            own[chunks + k : chunks + k + 1, :] = norm[:, k * TILE : (k + 1) * TILE]
        send_orient(3, turn, lambda peer: stats.at[turn, o], stats.at[turn, o])

        @pl.when(turn == 0)
        def _():
            by_twos(prepare_to)
            count_hits()

        received(3, turn, stats.at[turn, pl.ds(0, n_o - 1)])
        peak = stats[turn, 0, 0:chunks, :]
        for i in range(1, n_o):
            peak = jnp.maximum(peak, stats[turn, i, 0:chunks, :])
        whole = jnp.zeros((chunks, TILE), F32)
        for i in range(n_o):
            whole = whole + stats[turn, i, chunks : 2 * chunks, :] * jnp.exp(
                stats[turn, i, 0:chunks, :] - peak
            )
        factor = jnp.exp(stats[turn, o, 0:chunks, :] - peak) / whole
        factor = jnp.concatenate([factor[k : k + 1, :] for k in range(chunks)], axis=1)
        prob = expo * factor
        den = jnp.sum(prob * fluence_ref[...], axis=1, keepdims=True)
        dens[turn, f] = jnp.sum(jnp.where(diagonal, den, 0.0), axis=0, keepdims=True)
        send_frame(4, turn, lambda peer: dens.at[turn, f], dens.at[turn, f])

        probs = jnp.concatenate(split2(prob), axis=0)
        num = jnp.dot(probs, count_high[...], preferred_element_type=F32) + jnp.dot(
            probs, count_low[...], preferred_element_type=F32
        )
        num = num[:rows] + num[rows:]
        for t in range(n_f):
            value = num[:, t * TILE : (t + 1) * TILE] + jnp.where(f == t, held[turn, t, 0:rows], 0.0)
            shift = shifts[t]
            for k in range(7):
                value = jnp.where((shift & (1 << k)) != 0, pltpu.roll(value, 1 << k, 1), value)
            moved[t] = value

        @pl.when(turn == 0)
        def _():
            by_twos(prepare_from)

        received(4, turn, dens.at[turn, pl.ds(0, n_f - 1)])
        weight = dens[turn, 0]
        for i in range(1, n_f):
            weight = weight + dens[turn, i]
        weight = jnp.sum(jnp.where(diagonal, weight, 0.0), axis=1, keepdims=True)
        inverse = 1.0 / (weight + 1.0)
        for t in range(n_f):
            high, low = split2(moved[t] * inverse)
            first = lane >= shifts[t]
            none = jnp.zeros((rows, TILE), BF16)
            at = t * pair
            tiles[at : at + rows, :TILE] = jnp.where(first, high, none)
            tiles[at : at + rows, TILE:] = jnp.where(first, low, none)
            tiles[at + rows : at + pair, :TILE] = jnp.where(first, none, high)
            tiles[at + rows : at + pair, TILE:] = jnp.where(first, none, low)

        def to_owner(src, at, to):
            deliver(
                src, part_in.at[turn, at], send_sem.at[5], recv_sem.at[5, turn], to
            ).start()

        def product(g):
            here = slice(g * 2 * group * SUB, (g + 1) * 2 * group * SUB)
            part = jnp.dot(gather_to[here, :], tiles[...], preferred_element_type=F32)
            part = (part[:, :TILE] + part[:, TILE:]).reshape(2, group, SUB, TILE)
            part_out[turn, g, 0] = part[0]
            part_out[turn, g, 1] = part[1]
            for j in range(group):
                i, k = pairs[g * group + j]
                if hops(i, k) >= far:
                    to_owner(
                        part_out.at[turn, g, 0, j], o * half + chip, (peers_o[i], peers_f[k])
                    )
                    to_owner(
                        part_out.at[turn, g, 1, j],
                        n_o * half + far_pairs.index((i, k)),
                        (peers_o[i], chips[k] * 2 + 1 - core),
                    )
            deliver(
                part_out.at[turn, g, 1],
                pair_in.at[turn, g],
                send_sem.at[8],
                pair_recv.at[turn, g],
                (o, sibling),
            ).start()

        def release(g):
            got = pair_in.at[turn, g]
            into = pair_recv.at[turn, g]
            deliver(got, got, send_sem.at[8], into, (o, sibling)).wait_recv()
            paired[turn, g] = part_out[turn, g, 0] + pair_in[turn, g]
            for j in range(group):
                i, k = pairs[g * group + j]
                if hops(i, k) < far and (i, k) != (here_o, here_f):
                    to_owner(
                        paired.at[turn, g, j], o * half + chip, (peers_o[i], peers_f[k])
                    )

        for g in range(groups):
            product(g)
            if g >= 2:
                release(g - 2)
        release(groups - 2)
        release(groups - 1)
        part_in[turn, o * half + chip] = paired[turn, groups - 1, group - 1]

        @pl.when(turn == 0)
        def _():
            received(2, 0, hits_in.at[pl.ds(0, n_o - 1)])

        hits = jnp.sum(hits_in[...], axis=0)
        received(5, turn, part_in.at[turn, pl.ds(0, n // 2 - 1 + len(far_pairs))])
        brick = jnp.sum(part_in[turn, 0 : n // 2 + len(far_pairs)], axis=0) / jnp.maximum(hits, 1.0)
        out_ref[...] = brick
        slot = o * n_f + mine
        volume[turn, slot] = brick

        for i, k in others:
            brick_at = volume.at[turn, slot]
            into = wide_recv.at[turn, hops(i, k)]
            deliver(
                brick_at, brick_at, send_sem.at[6], into, (peers_o[i], peers_f[k])
            ).start()
            if hops(i, k) >= far:
                across = (peers_o[i], chips[k] * 2 + 1 - core)
                deliver(
                    brick_at, brick_at, send_sem.at[6], wide_pass.at[turn], across
                ).start()

        def pass_on(at):
            brick_at = volume.at[turn, at]
            deliver(
                brick_at, brick_at, send_sem.at[7], wide_pass.at[turn], (o, sibling)
            ).start()

        pass_on(slot)
        for distance in range(1, hops(*pairs[0]) + 1):
            ring_of = [d for d in others if hops(*d) == distance]
            if ring_of:
                some = volume.at[turn, pl.ds(0, len(ring_of))]
                into = wide_recv.at[turn, distance]
                deliver(some, some, send_sem.at[6], into, (o, sibling)).wait_recv()
            if distance < far:
                for i, k in ring_of:
                    pass_on(peers_o[i] * n_f + core * half + chips[k])
        bricks = volume.at[turn, pl.ds(0, n_o * half)]
        deliver(
            bricks, bricks, send_sem.at[7], wide_pass.at[turn], (o, sibling)
        ).wait_recv()
        high, low = split2(volume[turn].reshape(places, TILE))
        spread[:, :TILE] = high
        spread[:, TILE:] = low

        @pl.when(turn < ITERS - 1)
        def _():
            total = jnp.zeros((rows, TILE), F32)
            for t in range(0, n_f, 4):
                for k, value in enumerate(expand(t, 4)):
                    held[turn + 1, t + k, 0:rows] = value
                    total = total + take(t + k, value)
            totals[...] = total

        return c

    lax.fori_loop(0, ITERS, iteration, 0)
    new_ref[...] = expand(f, 1)[0]

    edges = sum(hops(here_o, k) == edge for k in away)
    sent(0, held.at[0, pl.ds(0, half - 1 + edges)])
    sent(1, held.at[0, pl.ds(0, half - edges)])
    sent(2, hits_out.at[pl.ds(0, n_o - 1)])
    double = len(far_pairs)
    sent(3, stats.at[:, pl.ds(0, n_o - 1)])
    sent(4, dens.at[:, pl.ds(0, n_f - 1)])
    sent(5, part_in.at[:, pl.ds(0, n // 2 - 1 + double)])
    sent(6, volume.at[:, pl.ds(0, n_o * half - 1 + double)])
    sent(7, volume.at[:, pl.ds(0, n_o * half - double)])
    sent(8, pair_in)


def on_device(n_o, n_f, slices, counts, fluence, tile_brick, tile_base):
    rows = slices.shape[0]
    frames, pixels = counts.shape
    pair = 2 * rows
    block = n_f * SUB
    places = n_o * block
    vmem = pl.BlockSpec(memory_space=pltpu.VMEM)
    new, brick = pl.pallas_call(
        functools.partial(kernel, n_o, n_f),
        out_shape=(pltpu.VMEM((rows, TILE), F32), pltpu.VMEM((SUB, TILE), F32)),
        in_specs=[pl.BlockSpec(memory_space=pl.ANY)] * 5,
        out_specs=(vmem, vmem),
        scratch_shapes=[
            pltpu.VMEM((1, rows), jnp.int32),
            pltpu.VMEM((1, rows), jnp.int32),
            pltpu.VMEM((1, frames), F32),
            pltpu.VMEM((rows, TILE), F32),
            pltpu.VMEM((frames, pixels), F32),
            pltpu.VMEM((frames, pixels), BF16),
            pltpu.VMEM((frames, pixels), BF16),
            pltpu.VMEM((pixels, frames), BF16),
            pltpu.VMEM((pixels, frames), BF16),
            pltpu.VMEM((ITERS, n_f, rows + SUB, TILE), F32),
            pltpu.VMEM((ITERS, n_o, 2 * (frames // TILE), TILE), F32),
            pltpu.VMEM((ITERS, n_f, 1, TILE), F32),
            pltpu.VMEM((places, pair), F32),
            pltpu.VMEM((places, n_f * pair), BF16),
            pltpu.VMEM((n_f * pair, places), BF16),
            pltpu.VMEM((n_f, rows, TILE), jnp.int32),
            pltpu.VMEM((n_f, rows, TILE), F32),
            pltpu.VMEM((n_f * pair, 2 * TILE), BF16),
            pltpu.VMEM((n_f * pair, TILE), BF16),
            pltpu.VMEM((3 * rows, pixels), BF16),
            pltpu.VMEM((ITERS, 4, 2, n_o * n_f // 8, SUB, TILE), F32),
            pltpu.VMEM((ITERS, 4, n_o * n_f // 8, SUB, TILE), F32),
            pltpu.VMEM((ITERS, 4, n_o * n_f // 8, SUB, TILE), F32),
            pltpu.VMEM((ITERS, n_o * n_f // 2 + FAR, SUB, TILE), F32),
            pltpu.VMEM((ITERS, n_o * n_f, SUB, TILE), F32),
            pltpu.VMEM((places, 2 * TILE), BF16),
            pltpu.VMEM((n_o, SUB, TILE), F32),
            pltpu.VMEM((n_o, SUB, TILE), F32),
            pltpu.SemaphoreType.DMA((LOAD + 4,)),
            pltpu.SemaphoreType.DMA((9,)),
            pltpu.SemaphoreType.DMA((6, ITERS)),
            pltpu.SemaphoreType.DMA((5,)),
            pltpu.SemaphoreType.DMA((5,)),
            pltpu.SemaphoreType.DMA((ITERS, 4)),
            pltpu.SemaphoreType.DMA((ITERS, 7)),
            pltpu.SemaphoreType.DMA((ITERS,)),
        ],
        compiler_params=pltpu.CompilerParams(
            collective_id=0, has_side_effects=True, vmem_limit_bytes=60 << 20
        ),
    )(slices, tile_brick[:, :, 0], tile_base, fluence[None, :], counts)
    return new, brick.reshape(1, SUB * TILE)


def solution(mesh):
    n_o, n_f = mesh.shape["orient"], mesh.shape["frame"]
    in_specs = (
        P("orient", "frame"),
        P("frame", None),
        P("frame"),
        P("frame", "orient", None),
        P("frame", "orient"),
    )
    out_specs = (P("orient", "frame"), P(("orient", "frame"), None))
    return jax.shard_map(
        functools.partial(on_device, n_o, n_f),
        mesh=mesh,
        in_specs=in_specs,
        out_specs=out_specs,
        check_vma=False,
    )
```

```python
import functools

import jax
import jax.numpy as jnp
from jax import lax
from jax.experimental import pallas as pl
from jax.experimental.pallas import tpu as pltpu
from jax.sharding import PartitionSpec as P

VOX = 1024
TILE = 128
SUB = VOX // TILE
ITERS = 2
BACKGROUND = 0.1
SHARPNESS = 0.02
MESH = pl.DeviceIdType.MESH
F32 = jnp.float32
BF16 = jnp.bfloat16
LOAD = 4
FAR = 7


def split2(x):
    high = x.astype(BF16)
    return high, (x - high.astype(F32)).astype(BF16)


def split3(x):
    high = x.astype(BF16)
    rest = x - high.astype(F32)
    mid = rest.astype(BF16)
    return high, mid, (rest - mid.astype(F32)).astype(BF16)


def iota(shape, axis):
    return lax.broadcasted_iota(jnp.int32, shape, axis)


def kernel(
    n_o,
    n_f,
    slices_ref,
    brick_ref,
    base_ref,
    fluence_from,
    counts_ref,
    new_ref,
    out_ref,
    brick_here,
    base_here,
    fluence_ref,
    totals,
    raw,
    count_high,
    count_low,
    count_high_t,
    count_low_t,
    held,
    stats,
    dens,
    where_to,
    gather_to,
    gather_from,
    shifts,
    moved,
    tiles,
    marks,
    logs,
    part_out,
    pair_in,
    paired,
    part_in,
    volume,
    spread,
    hits_out,
    hits_in,
    load_sem,
    send_sem,
    recv_sem,
    first_recv,
    first_pass,
    pair_recv,
    wide_recv,
    wide_pass,
):
    o = lax.axis_index("orient")
    f = lax.axis_index("frame")
    n = n_o * n_f
    me = o * n_f + f
    rows = slices_ref.shape[0]
    frames = counts_ref.shape[0]
    pair = 2 * rows
    block = n_f * SUB
    places = n_o * block
    chunks = frames // TILE
    half = n_f // 2
    ring = n_f // 4
    core = lax.rem(f, 2)
    chip = lax.div(f, 2)
    sibling = f + 1 - 2 * core
    mine = core * half + chip
    lane = iota((rows, TILE), 1)

    def near(d, size):
        return min(d, size - d)

    depth = n_o // 2
    turns_o = sorted(
        ((z, y) for z in range(depth) for y in range(2)), key=lambda d: -near(d[0], depth) - d[1]
    )
    turns_f = sorted(
        ((x, y, c) for x in range(ring) for y in range(2) for c in range(2)),
        key=lambda d: -(4 * near(d[0], ring) + 8 * d[1] + d[2]),
    )
    at_z, at_y = lax.div(o, 2), lax.rem(o, 2)
    peers_o = [lax.rem(at_z + z, depth) * 2 + lax.rem(at_y + y, 2) for z, y in turns_o]
    chip_x, chip_y = lax.div(chip, 2), lax.rem(chip, 2)
    chips = [
        lax.rem(chip_x + x, ring) * 2 + lax.rem(chip_y + y, 2) for x, y, c in turns_f
    ]
    sides = [lax.rem(core + c, 2) for x, y, c in turns_f]
    peers_f = [at * 2 + side for at, side in zip(chips, sides)]
    here_o, here_f = turns_o.index((0, 0)), turns_f.index((0, 0, 0))
    same_core = [k for k in range(n_f) if turns_f[k][2] == 0]

    def hops(i, k):
        (z, low), (x, high, c) = turns_o[i], turns_f[k]
        return near(z, depth) + near(x, ring) + ((0, 1), (2, 1))[high][low]

    pairs = sorted(
        ((i, k) for i in range(n_o) for k in same_core), key=lambda d: -hops(*d)
    )
    far = hops(*pairs[0]) + 1
    others = [d for d in pairs if d != (here_o, here_f)]

    far_pairs = [d for d in pairs if hops(*d) >= far]
    assert len(far_pairs) <= FAR
    groups = 4
    group = len(pairs) // groups

    def is_peer(i, k):
        if (i, k) == (here_o, here_f):
            return False
        return k in same_core or i == here_o or hops(i, k) >= far

    step = frames // LOAD
    small = [
        pltpu.make_async_copy(src, dst, load_sem.at[LOAD + i])
        for i, (src, dst) in enumerate(
            [
                (brick_ref, brick_here),
                (base_ref, base_here),
                (fluence_from, fluence_ref),
                (slices_ref, held.at[0, f, pl.ds(0, rows)]),
            ]
        )
    ]
    for one in small:
        one.start()
    barrier = pltpu.get_barrier_semaphore()
    peers = [(i, k) for i in range(n_o) for k in range(n_f) if is_peer(i, k)]
    for i, k in sorted(peers, key=lambda d: -hops(*d)):
        pl.semaphore_signal(
            barrier, inc=1, device_id=(peers_o[i], peers_f[k]), device_id_type=MESH
        )

    for i in range(LOAD):
        pltpu.make_async_copy(
            counts_ref.at[pl.ds(i * step, step)], raw.at[pl.ds(i * step, step)], load_sem.at[i]
        ).start()
    for one in small:
        one.wait()

    named = brick_here[...]
    inside = lax.rem(named, n_f)
    place = (
        lax.div(named, n_f) * block
        + (lax.rem(inside, 2) * half + lax.div(inside, 2)) * SUB
        + lax.div(base_here[...], TILE)
    )
    shift = lax.rem(base_here[...], TILE)
    held[0, f, rows : rows + 1] = jnp.concatenate([place, place + 1], axis=1).astype(F32)
    held[0, f, rows + 1 : rows + 2] = jnp.concatenate([shift, shift], axis=1).astype(F32)
    held[0, f, rows + 2 : rows + SUB] = jnp.zeros((SUB - 2, TILE), F32)

    for g in range(groups):
        for side in range(2):
            for j in range(group):
                i, k = pairs[g * group + j]
                own_side = core if side == 0 else 1 - core
                first = peers_o[i] * block + (own_side * half + chips[k]) * SUB
                at = ((g * 2 + side) * group + j) * SUB
                where_to[at : at + SUB, :] = (iota((SUB, pair), 0) + first).astype(F32)

    def load(i):
        here = pl.ds(i * step, step)
        pltpu.make_async_copy(counts_ref.at[here], raw.at[here], load_sem.at[i]).wait()

        def convert(j, c):
            at = pl.ds(pl.multiple_of(j * TILE, TILE), TILE)
            high, low = split2(raw[here, at])
            count_high[here, at] = high
            count_low[here, at] = low
            return c

        lax.fori_loop(0, n_f, convert, 0)

    for i in range(LOAD):
        load(i)
    pl.semaphore_wait(barrier, len(peers))

    def copy(which, turn, src, dst, to):
        return pltpu.make_async_remote_copy(
            src_ref=src,
            dst_ref=dst,
            send_sem=send_sem.at[which],
            recv_sem=recv_sem.at[which, turn],
            device_id=to,
            device_id_type=MESH,
        )

    def send_frame(which, turn, src, dst):
        def body(j, c):
            peer = lax.rem(f + j, n_f)
            copy(which, turn, src(peer), dst, (o, peer)).start()
            return c

        lax.fori_loop(1, n_f, body, 0)

    def send_orient(which, turn, src, dst):
        def body(j, c):
            peer = lax.rem(o + j, n_o)
            copy(which, turn, src(peer), dst, (peer, f)).start()
            return c

        lax.fori_loop(1, n_o, body, 0)

    def received(which, turn, whole):
        copy(which, turn, whole, whole, (lax.rem(o + 1, n_o), f)).wait_recv()

    def sent(which, whole):
        copy(which, 0, whole, whole, (lax.rem(o + 1, n_o), f)).wait_send()

    def deliver(src, dst, out, into, to):
        return pltpu.make_async_remote_copy(
            src_ref=src,
            dst_ref=dst,
            send_sem=out,
            recv_sem=into,
            device_id=to,
            device_id_type=MESH,
        )

    def pass_first(at, distance):
        packet = held.at[0, at * 2 + core]
        deliver(packet, packet, send_sem.at[1], first_pass.at[distance], (o, sibling)).start()

    def take(t, value):
        at = pl.ds(t * TILE if isinstance(t, int) else pl.multiple_of(t * TILE, TILE), TILE)
        high, mid, low = split3(jnp.log(value + BACKGROUND))
        logs[0:rows, at] = high
        logs[rows : 2 * rows, at] = mid
        logs[2 * rows : 3 * rows, at] = low
        return value

    away = sorted(
        (k for k in same_core if k != here_f), key=lambda k: -hops(here_o, k)
    )
    edge = hops(here_o, away[0]) + 1
    packet = held.at[0, f]
    for k in away:
        deliver(packet, packet, send_sem.at[0], first_recv.at[hops(here_o, k)], (o, peers_f[k])).start()
        if hops(here_o, k) == edge:
            across = (o, chips[k] * 2 + 1 - core)
            deliver(packet, packet, send_sem.at[0], first_pass.at[edge], across).start()
    pass_first(chip, 0)
    def turn_over(j, c):
        at = pl.ds(pl.multiple_of(j * TILE, TILE), TILE)
        count_high_t[at, :] = count_high[:, at].T
        count_low_t[at, :] = count_low[:, at].T
        return c

    lax.fori_loop(0, n_f, turn_over, 0)

    for distance in range(1, edge + 1):
        ring_of = [k for k in away if hops(here_o, k) == distance]
        if ring_of:
            some = held.at[0, pl.ds(0, len(ring_of))]
            into = first_recv.at[distance]
            deliver(some, some, send_sem.at[0], into, (o, sibling)).wait_recv()
        if distance < edge:
            for k in ring_of:
                pass_first(chips[k], distance)
    total = take(f, held[0, f, 0:rows])
    for k in reversed(away):
        total = total + take(peers_f[k], held[0, peers_f[k], 0:rows])
    for distance in range(edge + 1):
        ring_of = [k for k in same_core if hops(here_o, k) == distance]
        if ring_of:
            some = held.at[0, pl.ds(0, len(ring_of))]
            into = first_pass.at[distance]
            deliver(some, some, send_sem.at[1], into, (o, sibling)).wait_recv()
        for k in ring_of:
            at = chips[k] * 2 + 1 - core
            total = total + take(at, held[0, at, 0:rows])
    totals[...] = total
    diagonal = iota((rows, TILE), 0) == lane
    eye = iota((pair, pair), 0) == iota((pair, pair), 1)

    def prepare_to(t):
        row = held[0, t, rows : rows + 1]
        at = pl.ds(pl.multiple_of(t * pair, pair), pair)
        for i in range(n_o):
            place = where_to[i * block : (i + 1) * block, :]
            gather_to[i * block : (i + 1) * block, at] = jnp.where(
                place == row, 1.0, 0.0
            ).astype(BF16)
        shift = jnp.sum(
            jnp.where(eye, held[0, t, rows + 1 : rows + 2], 0.0), axis=1, keepdims=True
        )
        shift = jnp.broadcast_to(shift[0:rows], (rows, TILE)).astype(jnp.int32)
        shifts[t] = shift
        mark = jnp.where(lane >= shift, 1.0, 0.0)
        marks[at, :] = jnp.concatenate([mark, 1.0 - mark], axis=0).astype(BF16)

    def prepare_from(t):
        row = held[0, t, rows : rows + 1]
        at = pl.ds(pl.multiple_of(t * pair, pair), pair)
        column = jnp.sum(jnp.where(eye, row, 0.0), axis=1, keepdims=True)
        place = iota((pair, places), 1).astype(F32)
        gather_from[at, :] = jnp.where(place == column, 1.0, 0.0).astype(BF16)

    def by_twos(work):
        def body(t, c):
            work(t * 2)
            work(t * 2 + 1)
            return c

        lax.fori_loop(0, n_f // 2, body, 0)

    def count_hits():
        index = iota((n_o * SUB, pair), 0)
        place = (lax.div(index, SUB) * block + mine * SUB + lax.rem(index, SUB)).astype(F32)
        chosen = jnp.concatenate(
            [jnp.where(place == held[0, t, rows : rows + 1], 1.0, 0.0).astype(BF16) for t in range(n_f)],
            axis=1,
        )
        hits = jnp.dot(chosen, marks[...], preferred_element_type=F32)
        for i in range(n_o):
            hits_out[i] = hits[i * SUB : (i + 1) * SUB]
        send_orient(2, 0, lambda peer: hits_out.at[peer], hits_in.at[o])
        hits_in[o] = hits_out[o]

    def expand(t, many):
        at = pl.ds(t * pair if many > 1 else pl.multiple_of(t * pair, pair), many * pair)
        found = jnp.dot(gather_from[at, :], spread[...], preferred_element_type=F32)
        found = found[:, :TILE] + found[:, TILE:]
        values = []
        for i in range(many):
            shift = shifts[t + i]
            value = jnp.where(
                lane >= shift,
                found[i * pair : i * pair + rows],
                found[i * pair + rows : (i + 1) * pair],
            )
            for k in range(7):
                value = jnp.where(
                    (shift & (1 << k)) != 0, pltpu.roll(value, TILE - (1 << k), 1), value
                )
            values.append(value)
        return values

    def iteration(turn, c):
        total = jnp.sum(totals[...], axis=1, keepdims=True)
        like = jnp.dot(logs[...], count_high_t[...], preferred_element_type=F32) + jnp.dot(
            logs[...], count_low_t[...], preferred_element_type=F32
        )
        like = like[:rows] + like[rows : 2 * rows] + like[2 * rows :]
        score = SHARPNESS * (like - total * fluence_ref[...])
        top = jnp.max(score, axis=0, keepdims=True)
        expo = jnp.exp(score - top)
        norm = jnp.sum(expo, axis=0, keepdims=True)
        own = stats.at[turn, o]
        for k in range(chunks):
            own[k : k + 1, :] = top[:, k * TILE : (k + 1) * TILE]
            own[chunks + k : chunks + k + 1, :] = norm[:, k * TILE : (k + 1) * TILE]
        send_orient(3, turn, lambda peer: stats.at[turn, o], stats.at[turn, o])

        @pl.when(turn == 0)
        def _():
            by_twos(prepare_to)
            count_hits()

        received(3, turn, stats.at[turn, pl.ds(0, n_o - 1)])
        peak = stats[turn, 0, 0:chunks, :]
        for i in range(1, n_o):
            peak = jnp.maximum(peak, stats[turn, i, 0:chunks, :])
        whole = jnp.zeros((chunks, TILE), F32)
        for i in range(n_o):
            whole = whole + stats[turn, i, chunks : 2 * chunks, :] * jnp.exp(
                stats[turn, i, 0:chunks, :] - peak
            )
        factor = jnp.exp(stats[turn, o, 0:chunks, :] - peak) / whole
        factor = jnp.concatenate([factor[k : k + 1, :] for k in range(chunks)], axis=1)
        prob = expo * factor
        den = jnp.sum(prob * fluence_ref[...], axis=1, keepdims=True)
        dens[turn, f] = jnp.sum(jnp.where(diagonal, den, 0.0), axis=0, keepdims=True)
        send_frame(4, turn, lambda peer: dens.at[turn, f], dens.at[turn, f])

        probs = jnp.concatenate(split2(prob), axis=0)
        num = jnp.dot(probs, count_high[...], preferred_element_type=F32) + jnp.dot(
            probs, count_low[...], preferred_element_type=F32
        )
        num = num[:rows] + num[rows:]
        for t in range(n_f):
            value = num[:, t * TILE : (t + 1) * TILE] + jnp.where(f == t, held[turn, t, 0:rows], 0.0)
            shift = shifts[t]
            for k in range(7):
                value = jnp.where((shift & (1 << k)) != 0, pltpu.roll(value, 1 << k, 1), value)
            moved[t] = value

        @pl.when(turn == 0)
        def _():
            by_twos(prepare_from)

        received(4, turn, dens.at[turn, pl.ds(0, n_f - 1)])
        weight = dens[turn, 0]
        for i in range(1, n_f):
            weight = weight + dens[turn, i]
        weight = jnp.sum(jnp.where(diagonal, weight, 0.0), axis=1, keepdims=True)
        inverse = 1.0 / (weight + 1.0)
        for t in range(n_f):
            high, low = split2(moved[t] * inverse)
            first = lane >= shifts[t]
            none = jnp.zeros((rows, TILE), BF16)
            at = t * pair
            tiles[at : at + rows, :TILE] = jnp.where(first, high, none)
            tiles[at : at + rows, TILE:] = jnp.where(first, low, none)
            tiles[at + rows : at + pair, :TILE] = jnp.where(first, none, high)
            tiles[at + rows : at + pair, TILE:] = jnp.where(first, none, low)

        def to_owner(src, at, to):
            deliver(
                src, part_in.at[turn, at], send_sem.at[5], recv_sem.at[5, turn], to
            ).start()

        def product(g):
            here = slice(g * 2 * group * SUB, (g + 1) * 2 * group * SUB)
            part = jnp.dot(gather_to[here, :], tiles[...], preferred_element_type=F32)
            part = (part[:, :TILE] + part[:, TILE:]).reshape(2, group, SUB, TILE)
            part_out[turn, g, 0] = part[0]
            part_out[turn, g, 1] = part[1]
            for j in range(group):
                i, k = pairs[g * group + j]
                if hops(i, k) >= far:
                    to_owner(
                        part_out.at[turn, g, 0, j], o * half + chip, (peers_o[i], peers_f[k])
                    )
                    to_owner(
                        part_out.at[turn, g, 1, j],
                        n_o * half + far_pairs.index((i, k)),
                        (peers_o[i], chips[k] * 2 + 1 - core),
                    )
            deliver(
                part_out.at[turn, g, 1],
                pair_in.at[turn, g],
                send_sem.at[8],
                pair_recv.at[turn, g],
                (o, sibling),
            ).start()

        def release(g):
            got = pair_in.at[turn, g]
            into = pair_recv.at[turn, g]
            deliver(got, got, send_sem.at[8], into, (o, sibling)).wait_recv()
            paired[turn, g] = part_out[turn, g, 0] + pair_in[turn, g]
            for j in range(group):
                i, k = pairs[g * group + j]
                if hops(i, k) < far and (i, k) != (here_o, here_f):
                    to_owner(
                        paired.at[turn, g, j], o * half + chip, (peers_o[i], peers_f[k])
                    )

        for g in range(groups):
            product(g)
            if g >= 2:
                release(g - 2)
        release(groups - 2)
        release(groups - 1)
        part_in[turn, o * half + chip] = paired[turn, groups - 1, group - 1]

        @pl.when(turn == 0)
        def _():
            received(2, 0, hits_in.at[pl.ds(0, n_o - 1)])

        hits = jnp.sum(hits_in[...], axis=0)
        received(5, turn, part_in.at[turn, pl.ds(0, n // 2 - 1 + len(far_pairs))])
        brick = jnp.sum(part_in[turn, 0 : n // 2 + len(far_pairs)], axis=0) / jnp.maximum(hits, 1.0)
        out_ref[...] = brick
        slot = o * n_f + mine
        volume[turn, slot] = brick

        for i, k in others:
            brick_at = volume.at[turn, slot]
            into = wide_recv.at[turn, hops(i, k)]
            deliver(
                brick_at, brick_at, send_sem.at[6], into, (peers_o[i], peers_f[k])
            ).start()
            if hops(i, k) >= far:
                across = (peers_o[i], chips[k] * 2 + 1 - core)
                deliver(
                    brick_at, brick_at, send_sem.at[6], wide_pass.at[turn], across
                ).start()

        def pass_on(at):
            brick_at = volume.at[turn, at]
            deliver(
                brick_at, brick_at, send_sem.at[7], wide_pass.at[turn], (o, sibling)
            ).start()

        pass_on(slot)
        for distance in range(1, hops(*pairs[0]) + 1):
            ring_of = [d for d in others if hops(*d) == distance]
            if ring_of:
                some = volume.at[turn, pl.ds(0, len(ring_of))]
                into = wide_recv.at[turn, distance]
                deliver(some, some, send_sem.at[6], into, (o, sibling)).wait_recv()
            if distance < far:
                for i, k in ring_of:
                    pass_on(peers_o[i] * n_f + core * half + chips[k])
        bricks = volume.at[turn, pl.ds(0, n_o * half)]
        deliver(
            bricks, bricks, send_sem.at[7], wide_pass.at[turn], (o, sibling)
        ).wait_recv()
        high, low = split2(volume[turn].reshape(places, TILE))
        spread[:, :TILE] = high
        spread[:, TILE:] = low

        @pl.when(turn < ITERS - 1)
        def _():
            total = jnp.zeros((rows, TILE), F32)
            for t in range(0, n_f, 4):
                for k, value in enumerate(expand(t, 4)):
                    held[turn + 1, t + k, 0:rows] = value
                    total = total + take(t + k, value)
            totals[...] = total

        return c

    lax.fori_loop(0, ITERS, iteration, 0)
    new_ref[...] = expand(f, 1)[0]

    edges = sum(hops(here_o, k) == edge for k in away)
    sent(0, held.at[0, pl.ds(0, half - 1 + edges)])
    sent(1, held.at[0, pl.ds(0, half - edges)])
    sent(2, hits_out.at[pl.ds(0, n_o - 1)])
    double = len(far_pairs)
    sent(3, stats.at[:, pl.ds(0, n_o - 1)])
    sent(4, dens.at[:, pl.ds(0, n_f - 1)])
    sent(5, part_in.at[:, pl.ds(0, n // 2 - 1 + double)])
    sent(6, volume.at[:, pl.ds(0, n_o * half - 1 + double)])
    sent(7, volume.at[:, pl.ds(0, n_o * half - double)])
    sent(8, pair_in)


def on_device(n_o, n_f, slices, counts, fluence, tile_brick, tile_base):
    rows = slices.shape[0]
    frames, pixels = counts.shape
    pair = 2 * rows
    block = n_f * SUB
    places = n_o * block
    vmem = pl.BlockSpec(memory_space=pltpu.VMEM)
    new, brick = pl.pallas_call(
        functools.partial(kernel, n_o, n_f),
        out_shape=(pltpu.VMEM((rows, TILE), F32), pltpu.VMEM((SUB, TILE), F32)),
        in_specs=[pl.BlockSpec(memory_space=pl.ANY)] * 5,
        out_specs=(vmem, vmem),
        scratch_shapes=[
            pltpu.VMEM((1, rows), jnp.int32),
            pltpu.VMEM((1, rows), jnp.int32),
            pltpu.VMEM((1, frames), F32),
            pltpu.VMEM((rows, TILE), F32),
            pltpu.VMEM((frames, pixels), F32),
            pltpu.VMEM((frames, pixels), BF16),
            pltpu.VMEM((frames, pixels), BF16),
            pltpu.VMEM((pixels, frames), BF16),
            pltpu.VMEM((pixels, frames), BF16),
            pltpu.VMEM((ITERS, n_f, rows + SUB, TILE), F32),
            pltpu.VMEM((ITERS, n_o, 2 * (frames // TILE), TILE), F32),
            pltpu.VMEM((ITERS, n_f, 1, TILE), F32),
            pltpu.VMEM((places, pair), F32),
            pltpu.VMEM((places, n_f * pair), BF16),
            pltpu.VMEM((n_f * pair, places), BF16),
            pltpu.VMEM((n_f, rows, TILE), jnp.int32),
            pltpu.VMEM((n_f, rows, TILE), F32),
            pltpu.VMEM((n_f * pair, 2 * TILE), BF16),
            pltpu.VMEM((n_f * pair, TILE), BF16),
            pltpu.VMEM((3 * rows, pixels), BF16),
            pltpu.VMEM((ITERS, 4, 2, n_o * n_f // 8, SUB, TILE), F32),
            pltpu.VMEM((ITERS, 4, n_o * n_f // 8, SUB, TILE), F32),
            pltpu.VMEM((ITERS, 4, n_o * n_f // 8, SUB, TILE), F32),
            pltpu.VMEM((ITERS, n_o * n_f // 2 + FAR, SUB, TILE), F32),
            pltpu.VMEM((ITERS, n_o * n_f, SUB, TILE), F32),
            pltpu.VMEM((places, 2 * TILE), BF16),
            pltpu.VMEM((n_o, SUB, TILE), F32),
            pltpu.VMEM((n_o, SUB, TILE), F32),
            pltpu.SemaphoreType.DMA((LOAD + 4,)),
            pltpu.SemaphoreType.DMA((9,)),
            pltpu.SemaphoreType.DMA((6, ITERS)),
            pltpu.SemaphoreType.DMA((5,)),
            pltpu.SemaphoreType.DMA((5,)),
            pltpu.SemaphoreType.DMA((ITERS, 4)),
            pltpu.SemaphoreType.DMA((ITERS, 7)),
            pltpu.SemaphoreType.DMA((ITERS,)),
        ],
        compiler_params=pltpu.CompilerParams(
            collective_id=0, has_side_effects=True, vmem_limit_bytes=60 << 20
        ),
    )(slices, tile_brick[:, :, 0], tile_base, fluence[None, :], counts)
    return new, brick.reshape(1, SUB * TILE)


def solution(mesh):
    n_o, n_f = mesh.shape["orient"], mesh.shape["frame"]
    in_specs = (
        P("orient", "frame"),
        P("frame", None),
        P("frame"),
        P("frame", "orient", None),
        P("frame", "orient"),
    )
    out_specs = (P("orient", "frame"), P(("orient", "frame"), None))
    return jax.shard_map(
        functools.partial(on_device, n_o, n_f),
        mesh=mesh,
        in_specs=in_specs,
        out_specs=out_specs,
        check_vma=False,
    )
```

```python
import functools

import jax
import jax.numpy as jnp
from jax import lax
from jax.experimental import pallas as pl
from jax.experimental.pallas import tpu as pltpu
from jax.sharding import PartitionSpec as P

VOX = 1024
TILE = 128
SUB = VOX // TILE
ITERS = 2
BACKGROUND = 0.1
SHARPNESS = 0.02
MESH = pl.DeviceIdType.MESH
F32 = jnp.float32
BF16 = jnp.bfloat16
LOAD = 4
FAR = 7


def split2(x):
    high = x.astype(BF16)
    return high, (x - high.astype(F32)).astype(BF16)


def split3(x):
    high = x.astype(BF16)
    rest = x - high.astype(F32)
    mid = rest.astype(BF16)
    return high, mid, (rest - mid.astype(F32)).astype(BF16)


def iota(shape, axis):
    return lax.broadcasted_iota(jnp.int32, shape, axis)


def kernel(
    n_o,
    n_f,
    slices_ref,
    brick_ref,
    base_ref,
    fluence_from,
    counts_ref,
    new_ref,
    out_ref,
    brick_here,
    base_here,
    fluence_ref,
    totals,
    raw,
    count_high,
    count_low,
    count_high_t,
    count_low_t,
    held,
    stats,
    dens,
    where_to,
    gather_to,
    gather_from,
    shifts,
    moved,
    tiles,
    marks,
    logs,
    part_out,
    pair_in,
    paired,
    part_in,
    volume,
    spread,
    hits_out,
    hits_in,
    load_sem,
    send_sem,
    recv_sem,
    first_recv,
    first_pass,
    pair_recv,
    wide_recv,
    wide_pass,
):
    o = lax.axis_index("orient")
    f = lax.axis_index("frame")
    n = n_o * n_f
    me = o * n_f + f
    rows = slices_ref.shape[0]
    frames = counts_ref.shape[0]
    pair = 2 * rows
    block = n_f * SUB
    places = n_o * block
    chunks = frames // TILE
    half = n_f // 2
    ring = n_f // 4
    core = lax.rem(f, 2)
    chip = lax.div(f, 2)
    sibling = f + 1 - 2 * core
    mine = core * half + chip
    lane = iota((rows, TILE), 1)

    def near(d, size):
        return min(d, size - d)

    depth = n_o // 2
    turns_o = sorted(
        ((z, y) for z in range(depth) for y in range(2)), key=lambda d: -near(d[0], depth) - d[1]
    )
    turns_f = sorted(
        ((x, y, c) for x in range(ring) for y in range(2) for c in range(2)),
        key=lambda d: -(4 * near(d[0], ring) + 8 * d[1] + d[2]),
    )
    at_z, at_y = lax.div(o, 2), lax.rem(o, 2)
    peers_o = [lax.rem(at_z + z, depth) * 2 + lax.rem(at_y + y, 2) for z, y in turns_o]
    chip_x, chip_y = lax.div(chip, 2), lax.rem(chip, 2)
    chips = [
        lax.rem(chip_x + x, ring) * 2 + lax.rem(chip_y + y, 2) for x, y, c in turns_f
    ]
    sides = [lax.rem(core + c, 2) for x, y, c in turns_f]
    peers_f = [at * 2 + side for at, side in zip(chips, sides)]
    here_o, here_f = turns_o.index((0, 0)), turns_f.index((0, 0, 0))
    same_core = [k for k in range(n_f) if turns_f[k][2] == 0]

    def hops(i, k):
        (z, low), (x, high, c) = turns_o[i], turns_f[k]
        return near(z, depth) + near(x, ring) + ((0, 1), (2, 1))[high][low]

    pairs = sorted(
        ((i, k) for i in range(n_o) for k in same_core), key=lambda d: -hops(*d)
    )
    far = hops(*pairs[0]) + 1
    others = [d for d in pairs if d != (here_o, here_f)]

    far_pairs = [d for d in pairs if hops(*d) >= far]
    assert len(far_pairs) <= FAR
    groups = 4
    group = len(pairs) // groups

    def is_peer(i, k):
        if (i, k) == (here_o, here_f):
            return False
        return k in same_core or i == here_o or hops(i, k) >= far

    step = frames // LOAD
    small = [
        pltpu.make_async_copy(src, dst, load_sem.at[LOAD + i])
        for i, (src, dst) in enumerate(
            [
                (brick_ref, brick_here),
                (base_ref, base_here),
                (fluence_from, fluence_ref),
                (slices_ref, held.at[0, f, pl.ds(0, rows)]),
            ]
        )
    ]
    for one in small:
        one.start()
    barrier = pltpu.get_barrier_semaphore()
    peers = [(i, k) for i in range(n_o) for k in range(n_f) if is_peer(i, k)]
    for i, k in sorted(peers, key=lambda d: -hops(*d)):
        pl.semaphore_signal(
            barrier, inc=1, device_id=(peers_o[i], peers_f[k]), device_id_type=MESH
        )

    for i in range(LOAD):
        pltpu.make_async_copy(
            counts_ref.at[pl.ds(i * step, step)], raw.at[pl.ds(i * step, step)], load_sem.at[i]
        ).start()
    for one in small:
        one.wait()

    named = brick_here[...]
    inside = lax.rem(named, n_f)
    place = (
        lax.div(named, n_f) * block
        + (lax.rem(inside, 2) * half + lax.div(inside, 2)) * SUB
        + lax.div(base_here[...], TILE)
    )
    shift = lax.rem(base_here[...], TILE)
    held[0, f, rows : rows + 1] = jnp.concatenate([place, place + 1], axis=1).astype(F32)
    held[0, f, rows + 1 : rows + 2] = jnp.concatenate([shift, shift], axis=1).astype(F32)
    held[0, f, rows + 2 : rows + SUB] = jnp.zeros((SUB - 2, TILE), F32)

    for g in range(groups):
        for side in range(2):
            for j in range(group):
                i, k = pairs[g * group + j]
                own_side = core if side == 0 else 1 - core
                first = peers_o[i] * block + (own_side * half + chips[k]) * SUB
                at = ((g * 2 + side) * group + j) * SUB
                where_to[at : at + SUB, :] = (iota((SUB, pair), 0) + first).astype(F32)

    def load(i):
        here = pl.ds(i * step, step)
        pltpu.make_async_copy(counts_ref.at[here], raw.at[here], load_sem.at[i]).wait()

        def convert(j, c):
            at = pl.ds(pl.multiple_of(j * TILE, TILE), TILE)
            high, low = split2(raw[here, at])
            count_high[here, at] = high
            count_low[here, at] = low
            return c

        lax.fori_loop(0, n_f, convert, 0)

    for i in range(LOAD):
        load(i)
    pl.semaphore_wait(barrier, len(peers))

    def copy(which, turn, src, dst, to):
        return pltpu.make_async_remote_copy(
            src_ref=src,
            dst_ref=dst,
            send_sem=send_sem.at[which],
            recv_sem=recv_sem.at[which, turn],
            device_id=to,
            device_id_type=MESH,
        )

    def send_frame(which, turn, src, dst):
        def body(j, c):
            peer = lax.rem(f + j, n_f)
            copy(which, turn, src(peer), dst, (o, peer)).start()
            return c

        lax.fori_loop(1, n_f, body, 0)

    def send_orient(which, turn, src, dst):
        def body(j, c):
            peer = lax.rem(o + j, n_o)
            copy(which, turn, src(peer), dst, (peer, f)).start()
            return c

        lax.fori_loop(1, n_o, body, 0)

    def received(which, turn, whole):
        copy(which, turn, whole, whole, (lax.rem(o + 1, n_o), f)).wait_recv()

    def sent(which, whole):
        copy(which, 0, whole, whole, (lax.rem(o + 1, n_o), f)).wait_send()

    def deliver(src, dst, out, into, to):
        return pltpu.make_async_remote_copy(
            src_ref=src,
            dst_ref=dst,
            send_sem=out,
            recv_sem=into,
            device_id=to,
            device_id_type=MESH,
        )

    def pass_first(at, distance):
        packet = held.at[0, at * 2 + core]
        deliver(packet, packet, send_sem.at[1], first_pass.at[distance], (o, sibling)).start()

    def take(t, value):
        at = pl.ds(t * TILE if isinstance(t, int) else pl.multiple_of(t * TILE, TILE), TILE)
        high, mid, low = split3(jnp.log(value + BACKGROUND))
        logs[0:rows, at] = high
        logs[rows : 2 * rows, at] = mid
        logs[2 * rows : 3 * rows, at] = low
        return value

    away = sorted(
        (k for k in same_core if k != here_f), key=lambda k: -hops(here_o, k)
    )
    edge = hops(here_o, away[0]) + 1
    packet = held.at[0, f]
    for k in away:
        deliver(packet, packet, send_sem.at[0], first_recv.at[hops(here_o, k)], (o, peers_f[k])).start()
        if hops(here_o, k) == edge:
            across = (o, chips[k] * 2 + 1 - core)
            deliver(packet, packet, send_sem.at[0], first_pass.at[edge], across).start()
    pass_first(chip, 0)
    def turn_over(j, c):
        at = pl.ds(pl.multiple_of(j * TILE, TILE), TILE)
        count_high_t[at, :] = count_high[:, at].T
        count_low_t[at, :] = count_low[:, at].T
        return c

    lax.fori_loop(0, n_f, turn_over, 0)

    for distance in range(1, edge + 1):
        ring_of = [k for k in away if hops(here_o, k) == distance]
        if ring_of:
            some = held.at[0, pl.ds(0, len(ring_of))]
            into = first_recv.at[distance]
            deliver(some, some, send_sem.at[0], into, (o, sibling)).wait_recv()
        if distance < edge:
            for k in ring_of:
                pass_first(chips[k], distance)
    total = take(f, held[0, f, 0:rows])
    for k in reversed(away):
        total = total + take(peers_f[k], held[0, peers_f[k], 0:rows])
    for distance in range(edge + 1):
        ring_of = [k for k in same_core if hops(here_o, k) == distance]
        if ring_of:
            some = held.at[0, pl.ds(0, len(ring_of))]
            into = first_pass.at[distance]
            deliver(some, some, send_sem.at[1], into, (o, sibling)).wait_recv()
        for k in ring_of:
            at = chips[k] * 2 + 1 - core
            total = total + take(at, held[0, at, 0:rows])
    totals[...] = total
    diagonal = iota((rows, TILE), 0) == lane
    eye = iota((pair, pair), 0) == iota((pair, pair), 1)

    def prepare_to(t):
        row = held[0, t, rows : rows + 1]
        at = pl.ds(pl.multiple_of(t * pair, pair), pair)
        for i in range(n_o):
            place = where_to[i * block : (i + 1) * block, :]
            gather_to[i * block : (i + 1) * block, at] = jnp.where(
                place == row, 1.0, 0.0
            ).astype(BF16)
        shift = jnp.sum(
            jnp.where(eye, held[0, t, rows + 1 : rows + 2], 0.0), axis=1, keepdims=True
        )
        shift = jnp.broadcast_to(shift[0:rows], (rows, TILE)).astype(jnp.int32)
        shifts[t] = shift
        mark = jnp.where(lane >= shift, 1.0, 0.0)
        marks[at, :] = jnp.concatenate([mark, 1.0 - mark], axis=0).astype(BF16)

    def prepare_from(t):
        row = held[0, t, rows : rows + 1]
        at = pl.ds(pl.multiple_of(t * pair, pair), pair)
        column = jnp.sum(jnp.where(eye, row, 0.0), axis=1, keepdims=True)
        place = iota((pair, places), 1).astype(F32)
        gather_from[at, :] = jnp.where(place == column, 1.0, 0.0).astype(BF16)

    def by_twos(work):
        def body(t, c):
            work(t * 2)
            work(t * 2 + 1)
            return c

        lax.fori_loop(0, n_f // 2, body, 0)

    def count_hits():
        index = iota((n_o * SUB, pair), 0)
        place = (lax.div(index, SUB) * block + mine * SUB + lax.rem(index, SUB)).astype(F32)
        chosen = jnp.concatenate(
            [jnp.where(place == held[0, t, rows : rows + 1], 1.0, 0.0).astype(BF16) for t in range(n_f)],
            axis=1,
        )
        hits = jnp.dot(chosen, marks[...], preferred_element_type=F32)
        for i in range(n_o):
            hits_out[i] = hits[i * SUB : (i + 1) * SUB]
        send_orient(2, 0, lambda peer: hits_out.at[peer], hits_in.at[o])
        hits_in[o] = hits_out[o]

    def expand(t, many):
        at = pl.ds(t * pair if many > 1 else pl.multiple_of(t * pair, pair), many * pair)
        found = jnp.dot(gather_from[at, :], spread[...], preferred_element_type=F32)
        found = found[:, :TILE] + found[:, TILE:]
        values = []
        for i in range(many):
            shift = shifts[t + i]
            value = jnp.where(
                lane >= shift,
                found[i * pair : i * pair + rows],
                found[i * pair + rows : (i + 1) * pair],
            )
            for k in range(7):
                value = jnp.where(
                    (shift & (1 << k)) != 0, pltpu.roll(value, TILE - (1 << k), 1), value
                )
            values.append(value)
        return values

    def iteration(turn, c):
        total = jnp.sum(totals[...], axis=1, keepdims=True)
        like = jnp.dot(logs[...], count_high_t[...], preferred_element_type=F32)
        rest = jnp.dot(
            logs[0 : 2 * rows, :], count_low_t[...], preferred_element_type=F32
        )
        like = like[:rows] + like[rows : 2 * rows] + like[2 * rows :]
        like = like + (rest[:rows] + rest[rows:])
        score = SHARPNESS * (like - total * fluence_ref[...])
        top = jnp.max(score, axis=0, keepdims=True)
        expo = jnp.exp(score - top)
        norm = jnp.sum(expo, axis=0, keepdims=True)
        own = stats.at[turn, o]
        for k in range(chunks):
            own[k : k + 1, :] = top[:, k * TILE : (k + 1) * TILE]
            own[chunks + k : chunks + k + 1, :] = norm[:, k * TILE : (k + 1) * TILE]
        send_orient(3, turn, lambda peer: stats.at[turn, o], stats.at[turn, o])

        @pl.when(turn == 0)
        def _():
            by_twos(prepare_to)
            count_hits()

        received(3, turn, stats.at[turn, pl.ds(0, n_o - 1)])
        peak = stats[turn, 0, 0:chunks, :]
        for i in range(1, n_o):
            peak = jnp.maximum(peak, stats[turn, i, 0:chunks, :])
        whole = jnp.zeros((chunks, TILE), F32)
        for i in range(n_o):
            whole = whole + stats[turn, i, chunks : 2 * chunks, :] * jnp.exp(
                stats[turn, i, 0:chunks, :] - peak
            )
        factor = jnp.exp(stats[turn, o, 0:chunks, :] - peak) / whole
        factor = jnp.concatenate([factor[k : k + 1, :] for k in range(chunks)], axis=1)
        prob = expo * factor
        den = jnp.sum(prob * fluence_ref[...], axis=1, keepdims=True)
        dens[turn, f] = jnp.sum(jnp.where(diagonal, den, 0.0), axis=0, keepdims=True)
        send_frame(4, turn, lambda peer: dens.at[turn, f], dens.at[turn, f])

        probs = jnp.concatenate(split2(prob), axis=0)
        num = jnp.dot(probs, count_high[...], preferred_element_type=F32)
        num = (num[:rows] + num[rows:]) + jnp.dot(
            probs[:rows], count_low[...], preferred_element_type=F32
        )
        for t in range(n_f):
            value = num[:, t * TILE : (t + 1) * TILE] + jnp.where(f == t, held[turn, t, 0:rows], 0.0)
            shift = shifts[t]
            for k in range(7):
                value = jnp.where((shift & (1 << k)) != 0, pltpu.roll(value, 1 << k, 1), value)
            moved[t] = value

        @pl.when(turn == 0)
        def _():
            by_twos(prepare_from)

        received(4, turn, dens.at[turn, pl.ds(0, n_f - 1)])
        weight = dens[turn, 0]
        for i in range(1, n_f):
            weight = weight + dens[turn, i]
        weight = jnp.sum(jnp.where(diagonal, weight, 0.0), axis=1, keepdims=True)
        inverse = 1.0 / (weight + 1.0)
        for t in range(n_f):
            high, low = split2(moved[t] * inverse)
            first = lane >= shifts[t]
            none = jnp.zeros((rows, TILE), BF16)
            at = t * pair
            tiles[at : at + rows, :TILE] = jnp.where(first, high, none)
            tiles[at : at + rows, TILE:] = jnp.where(first, low, none)
            tiles[at + rows : at + pair, :TILE] = jnp.where(first, none, high)
            tiles[at + rows : at + pair, TILE:] = jnp.where(first, none, low)

        def to_owner(src, at, to):
            deliver(
                src, part_in.at[turn, at], send_sem.at[5], recv_sem.at[5, turn], to
            ).start()

        def product(g):
            here = slice(g * 2 * group * SUB, (g + 1) * 2 * group * SUB)
            part = jnp.dot(gather_to[here, :], tiles[...], preferred_element_type=F32)
            part = (part[:, :TILE] + part[:, TILE:]).reshape(2, group, SUB, TILE)
            part_out[turn, g, 0] = part[0]
            part_out[turn, g, 1] = part[1]
            for j in range(group):
                i, k = pairs[g * group + j]
                if hops(i, k) >= far:
                    to_owner(
                        part_out.at[turn, g, 0, j], o * half + chip, (peers_o[i], peers_f[k])
                    )
                    to_owner(
                        part_out.at[turn, g, 1, j],
                        n_o * half + far_pairs.index((i, k)),
                        (peers_o[i], chips[k] * 2 + 1 - core),
                    )
            deliver(
                part_out.at[turn, g, 1],
                pair_in.at[turn, g],
                send_sem.at[8],
                pair_recv.at[turn, g],
                (o, sibling),
            ).start()

        def release(g):
            got = pair_in.at[turn, g]
            into = pair_recv.at[turn, g]
            deliver(got, got, send_sem.at[8], into, (o, sibling)).wait_recv()
            paired[turn, g] = part_out[turn, g, 0] + pair_in[turn, g]
            for j in range(group):
                i, k = pairs[g * group + j]
                if hops(i, k) < far and (i, k) != (here_o, here_f):
                    to_owner(
                        paired.at[turn, g, j], o * half + chip, (peers_o[i], peers_f[k])
                    )

        for g in range(groups):
            product(g)
            if g >= 2:
                release(g - 2)
        release(groups - 2)
        release(groups - 1)
        part_in[turn, o * half + chip] = paired[turn, groups - 1, group - 1]

        @pl.when(turn == 0)
        def _():
            received(2, 0, hits_in.at[pl.ds(0, n_o - 1)])

        hits = jnp.sum(hits_in[...], axis=0)
        received(5, turn, part_in.at[turn, pl.ds(0, n // 2 - 1 + len(far_pairs))])
        brick = jnp.sum(part_in[turn, 0 : n // 2 + len(far_pairs)], axis=0) / jnp.maximum(hits, 1.0)
        out_ref[...] = brick
        slot = o * n_f + mine
        volume[turn, slot] = brick

        for i, k in others:
            brick_at = volume.at[turn, slot]
            into = wide_recv.at[turn, hops(i, k)]
            deliver(
                brick_at, brick_at, send_sem.at[6], into, (peers_o[i], peers_f[k])
            ).start()
            if hops(i, k) >= far:
                across = (peers_o[i], chips[k] * 2 + 1 - core)
                deliver(
                    brick_at, brick_at, send_sem.at[6], wide_pass.at[turn], across
                ).start()

        def pass_on(at):
            brick_at = volume.at[turn, at]
            deliver(
                brick_at, brick_at, send_sem.at[7], wide_pass.at[turn], (o, sibling)
            ).start()

        pass_on(slot)
        for distance in range(1, hops(*pairs[0]) + 1):
            ring_of = [d for d in others if hops(*d) == distance]
            if ring_of:
                some = volume.at[turn, pl.ds(0, len(ring_of))]
                into = wide_recv.at[turn, distance]
                deliver(some, some, send_sem.at[6], into, (o, sibling)).wait_recv()
            if distance < far:
                for i, k in ring_of:
                    pass_on(peers_o[i] * n_f + core * half + chips[k])
        bricks = volume.at[turn, pl.ds(0, n_o * half)]
        deliver(
            bricks, bricks, send_sem.at[7], wide_pass.at[turn], (o, sibling)
        ).wait_recv()
        high, low = split2(volume[turn].reshape(places, TILE))
        spread[:, :TILE] = high
        spread[:, TILE:] = low

        @pl.when(turn < ITERS - 1)
        def _():
            total = jnp.zeros((rows, TILE), F32)
            for t in range(0, n_f, 4):
                for k, value in enumerate(expand(t, 4)):
                    held[turn + 1, t + k, 0:rows] = value
                    total = total + take(t + k, value)
            totals[...] = total

        return c

    lax.fori_loop(0, ITERS, iteration, 0)
    new_ref[...] = expand(f, 1)[0]

    edges = sum(hops(here_o, k) == edge for k in away)
    sent(0, held.at[0, pl.ds(0, half - 1 + edges)])
    sent(1, held.at[0, pl.ds(0, half - edges)])
    sent(2, hits_out.at[pl.ds(0, n_o - 1)])
    double = len(far_pairs)
    sent(3, stats.at[:, pl.ds(0, n_o - 1)])
    sent(4, dens.at[:, pl.ds(0, n_f - 1)])
    sent(5, part_in.at[:, pl.ds(0, n // 2 - 1 + double)])
    sent(6, volume.at[:, pl.ds(0, n_o * half - 1 + double)])
    sent(7, volume.at[:, pl.ds(0, n_o * half - double)])
    sent(8, pair_in)


def on_device(n_o, n_f, slices, counts, fluence, tile_brick, tile_base):
    rows = slices.shape[0]
    frames, pixels = counts.shape
    pair = 2 * rows
    block = n_f * SUB
    places = n_o * block
    vmem = pl.BlockSpec(memory_space=pltpu.VMEM)
    new, brick = pl.pallas_call(
        functools.partial(kernel, n_o, n_f),
        out_shape=(pltpu.VMEM((rows, TILE), F32), pltpu.VMEM((SUB, TILE), F32)),
        in_specs=[pl.BlockSpec(memory_space=pl.ANY)] * 5,
        out_specs=(vmem, vmem),
        scratch_shapes=[
            pltpu.VMEM((1, rows), jnp.int32),
            pltpu.VMEM((1, rows), jnp.int32),
            pltpu.VMEM((1, frames), F32),
            pltpu.VMEM((rows, TILE), F32),
            pltpu.VMEM((frames, pixels), F32),
            pltpu.VMEM((frames, pixels), BF16),
            pltpu.VMEM((frames, pixels), BF16),
            pltpu.VMEM((pixels, frames), BF16),
            pltpu.VMEM((pixels, frames), BF16),
            pltpu.VMEM((ITERS, n_f, rows + SUB, TILE), F32),
            pltpu.VMEM((ITERS, n_o, 2 * (frames // TILE), TILE), F32),
            pltpu.VMEM((ITERS, n_f, 1, TILE), F32),
            pltpu.VMEM((places, pair), F32),
            pltpu.VMEM((places, n_f * pair), BF16),
            pltpu.VMEM((n_f * pair, places), BF16),
            pltpu.VMEM((n_f, rows, TILE), jnp.int32),
            pltpu.VMEM((n_f, rows, TILE), F32),
            pltpu.VMEM((n_f * pair, 2 * TILE), BF16),
            pltpu.VMEM((n_f * pair, TILE), BF16),
            pltpu.VMEM((3 * rows, pixels), BF16),
            pltpu.VMEM((ITERS, 4, 2, n_o * n_f // 8, SUB, TILE), F32),
            pltpu.VMEM((ITERS, 4, n_o * n_f // 8, SUB, TILE), F32),
            pltpu.VMEM((ITERS, 4, n_o * n_f // 8, SUB, TILE), F32),
            pltpu.VMEM((ITERS, n_o * n_f // 2 + FAR, SUB, TILE), F32),
            pltpu.VMEM((ITERS, n_o * n_f, SUB, TILE), F32),
            pltpu.VMEM((places, 2 * TILE), BF16),
            pltpu.VMEM((n_o, SUB, TILE), F32),
            pltpu.VMEM((n_o, SUB, TILE), F32),
            pltpu.SemaphoreType.DMA((LOAD + 4,)),
            pltpu.SemaphoreType.DMA((9,)),
            pltpu.SemaphoreType.DMA((6, ITERS)),
            pltpu.SemaphoreType.DMA((5,)),
            pltpu.SemaphoreType.DMA((5,)),
            pltpu.SemaphoreType.DMA((ITERS, 4)),
            pltpu.SemaphoreType.DMA((ITERS, 7)),
            pltpu.SemaphoreType.DMA((ITERS,)),
        ],
        compiler_params=pltpu.CompilerParams(
            collective_id=0, has_side_effects=True, vmem_limit_bytes=60 << 20
        ),
    )(slices, tile_brick[:, :, 0], tile_base, fluence[None, :], counts)
    return new, brick.reshape(1, SUB * TILE)


def solution(mesh):
    n_o, n_f = mesh.shape["orient"], mesh.shape["frame"]
    in_specs = (
        P("orient", "frame"),
        P("frame", None),
        P("frame"),
        P("frame", "orient", None),
        P("frame", "orient"),
    )
    out_specs = (P("orient", "frame"), P(("orient", "frame"), None))
    return jax.shard_map(
        functools.partial(on_device, n_o, n_f),
        mesh=mesh,
        in_specs=in_specs,
        out_specs=out_specs,
        check_vma=False,
    )
```
